32 devices in a mesh: cfg: 1, node: 32 (over z, y, x, core), pair: 1.
Axes of the slice: x: 2, y: 2, z: 4, core: 2. Of those that a mesh axis runs over, the one named last changes fastest.
Arguments:
- node_blocks: float32 [256, 2, 256, 256], P(('cfg', 'node'), None, None, 'pair'), may hold values from -1.5 to 1.5
- node_slot: int32 [256], replicated, may hold values from 0 to 255, as said below
- pair_list: int32 [128, 2], replicated, may hold values from 0 to 255, as said below
- second_list: int32 [128, 2], replicated, may hold values from 0 to 127, as said below
- targets: int32 [128], replicated, may hold values from 0 to 63, as said below
- spin_signs: int32 [128], replicated, may hold values from -1 to 1, as said below
Outputs:
- results: float32 [64, 2, 256, 256], P(('cfg', 'node'), None, None, 'pair')
The draws below stay inside these ranges and needn't reach their ends.
Inputs may be any that keep to these rules, and one draw needn't show every extreme that they name: `node_slot`: A permutation of the slots. `pair_list`: rows b * 4 to (b + 1) * 4 - 1 form block b. The first node of a pair in block b sits at a slot of b * 8 to (b + 1) * 8 - 1. For every block b and every owner o, at most 1 pair of block b has its second node at slots o * 8 to (o + 1) * 8 - 1; one owner supplies exactly 1 such node to every block. `second_list`: rows b * 4 to (b + 1) * 4 - 1 form block b. The first pair of a product in block b lies in block b of the pairs. For every block b and owner o, at most 1 product of block b has its second pair in block o of the pairs; one owner supplies exactly 1 such pair product to every block. `targets`: products of block b target results b * 2 to (b + 1) * 2 - 1. `spin_signs`: each entry is -1 or 1.
All inputs are finite; a program needn't handle non-finite values.
Results may differ from the reference program's by a relative error of at most 0.000098.
Values sent between devices are 32-bit elements; how exact they have to be, the bound alone decides.
No kernel may reach another device: no remote copies, remote signals or barrier semaphores. Data moves between devices by JAX's collectives and lax.ppermute only.
A program may use at most 128 MiB of HBM per device.

```python
import jax
import jax.numpy as jnp
from jax import lax

ORDER = 256
NODE_COL = 8
PAIR_COL = 4
RES_COL = 2
CAP = 1
NODES = 256
PAIRS = 128
SECONDS = 128
RESULTS = 64


def owner_table(seed_key, columns):
    common_owner = jax.random.randint(jax.random.fold_in(seed_key, 0), (), 0, columns)

    def one_column(column):
        return jax.random.permutation(jax.random.fold_in(seed_key, column + 1), columns)
    orders = jax.vmap(one_column)(jnp.arange(columns))
    position = jnp.argmax((orders == common_owner).astype(jnp.int32), axis=1)
    leading = orders[:, 0]
    row_ids = jnp.arange(columns)
    orders = orders.at[row_ids, position].set(leading)
    orders = orders.at[:, 0].set(common_owner)
    return orders.astype(jnp.int32)


def contraction_graph(key):
    columns = NODES // NODE_COL
    node_slot = jax.random.permutation(jax.random.fold_in(key, 101), NODES).astype(jnp.int32)
    slot_node = jnp.argsort(node_slot).astype(jnp.int32)
    groups = jnp.arange(PAIR_COL) // CAP
    column_ids = jnp.arange(columns)[:, None]
    first_slot = column_ids * NODE_COL + jax.random.randint(jax.random.fold_in(key, 102), (columns, PAIR_COL), 0, NODE_COL)
    second_owner = owner_table(jax.random.fold_in(key, 103), columns)[:, groups]
    second_slot = second_owner * NODE_COL + jax.random.randint(jax.random.fold_in(key, 104), (columns, PAIR_COL), 0, NODE_COL)
    pair_list = jnp.stack([slot_node[first_slot], slot_node[second_slot]], axis=-1).reshape(PAIRS, 2)
    left_pair = column_ids * PAIR_COL + jax.random.randint(jax.random.fold_in(key, 105), (columns, PAIR_COL), 0, PAIR_COL)
    right_owner = owner_table(jax.random.fold_in(key, 106), columns)[:, groups]
    right_pair = right_owner * PAIR_COL + jax.random.randint(jax.random.fold_in(key, 107), (columns, PAIR_COL), 0, PAIR_COL)
    second_list = jnp.stack([left_pair, right_pair], axis=-1).reshape(SECONDS, 2)
    targets = (column_ids * RES_COL + jax.random.randint(jax.random.fold_in(key, 108), (columns, PAIR_COL), 0, RES_COL)).reshape(SECONDS)
    return (node_slot, pair_list.astype(jnp.int32), second_list.astype(jnp.int32), targets.astype(jnp.int32))


def draw_node_slot(key, part):
    return contraction_graph(key)[0]


def draw_pair_list(key, part):
    return contraction_graph(key)[1]


def draw_second_list(key, part):
    return contraction_graph(key)[2]


def draw_targets(key, part):
    return contraction_graph(key)[3]


def draw_spin_signs(key, part):
    return (2 * jax.random.randint(jax.random.fold_in(key, 201), (SECONDS,), 0, 2) - 1).astype(jnp.int32)


def level_of(key, extent, shards, low, top_value):
    def one(dim, shards_of):
        steps = jax.random.uniform(jax.random.fold_in(jax.random.fold_in(key, 6), dim), (shards_of,), jnp.float32, low / len(shards), top_value / len(shards))
        return jnp.repeat(jnp.exp(steps), extent[dim] // shards_of).reshape((-1,) + (1,) * (len(extent) - dim - 1))

    factor_of = one(*shards[0])
    for cut in shards[1:]:
        factor_of = factor_of * one(*cut)
    return factor_of


def gaussian(rng, dims, scale, bound, shards=(), kind=jnp.bfloat16):
    factor_of = level_of(rng, dims, shards, -0.22, 0.18) if shards else 1.0
    drawn = jax.random.normal(rng, dims, jnp.float32) * scale * factor_of
    return jnp.minimum(jnp.maximum(drawn, -bound), bound).astype(kind)


def setup_inputs(seed: int = 0, part: int = 0) -> dict:
    keys = jax.random.split(jax.random.key(seed), 7)
    part_keys = jax.random.split(jax.random.fold_in(keys[6], part), 7)
    node_blocks = gaussian(part_keys[0], (NODES, 2, ORDER, ORDER), ((2 * ORDER) ** -0.375), 1.5, ((0, 32),), jnp.float32)
    node_slot = draw_node_slot(jax.random.fold_in(keys[6], 71), part)
    pair_list = draw_pair_list(jax.random.fold_in(keys[6], 71), part)
    second_list = draw_second_list(jax.random.fold_in(keys[6], 71), part)
    targets = draw_targets(jax.random.fold_in(keys[6], 71), part)
    spin_signs = draw_spin_signs(jax.random.fold_in(keys[6], 71), part)
    return dict(node_blocks=node_blocks, node_slot=node_slot, pair_list=pair_list, second_list=second_list, targets=targets, spin_signs=spin_signs)


def matmul_high(left_side, right_side):
    return jnp.matmul(left_side, right_side, precision=lax.Precision.HIGHEST)


def complex_product(left_side, right_side):
    real_part = matmul_high(left_side[:, 0], right_side[:, 0]) - matmul_high(left_side[:, 1], right_side[:, 1])
    imag_part = matmul_high(left_side[:, 0], right_side[:, 1]) + matmul_high(left_side[:, 1], right_side[:, 0])
    return jnp.stack([real_part, imag_part], axis=1)


def reference(node_blocks, node_slot, pair_list, second_list, targets, spin_signs):
    first_nodes = jnp.take(node_blocks, node_slot[pair_list[:, 0]], axis=0)
    second_nodes = jnp.take(node_blocks, node_slot[pair_list[:, 1]], axis=0)
    products = complex_product(first_nodes, second_nodes)
    left_side = jnp.take(products, second_list[:, 0], axis=0)
    right_side = jnp.take(products, second_list[:, 1], axis=0)
    weights = spin_signs.astype(jnp.float32)[:, None, None, None]
    seconds = complex_product(left_side, right_side) * weights
    return jax.ops.segment_sum(seconds, targets, num_segments=RESULTS)
```

```python
import jax
import jax.numpy as jnp
from jax import lax
from jax.sharding import PartitionSpec as P

RES_COL = 2


def complex_product(left_side, right_side):
    half_width = right_side.shape[3]
    stacked_left = jnp.concatenate([left_side[:, 0], left_side[:, 1]], axis=2)
    real_right = jnp.concatenate([right_side[:, 0], -right_side[:, 1]], axis=1)
    imag_right = jnp.concatenate([right_side[:, 1], right_side[:, 0]], axis=1)
    stacked_right = jnp.concatenate([real_right, imag_right], axis=2)
    joined = jnp.einsum(
        "jmk,jkn->jmn",
        stacked_left,
        stacked_right,
        precision=lax.Precision.HIGHEST,
        preferred_element_type=jnp.float32,
    )
    return jnp.stack([joined[:, :, :half_width], joined[:, :, half_width:]], axis=1)


def fetch_items(local_items, wanted):
    spread = lax.all_to_all(local_items, "node", split_axis=2, concat_axis=0, tiled=True)
    picked = jnp.take(spread, wanted, axis=0)
    return lax.all_to_all(picked, "node", split_axis=0, concat_axis=2, tiled=True)


def per_device(node_blocks, node_slot, pair_list, second_list, targets, spin_signs):
    columns = lax.axis_size("node")
    column = lax.axis_index("node")
    node_col = node_blocks.shape[0]
    pair_col = pair_list.shape[0] // columns
    block_start = column * pair_col
    second_nodes = fetch_items(node_blocks, node_slot[pair_list[:, 1]])
    own_pairs = lax.dynamic_slice_in_dim(pair_list, block_start, pair_col, 0)
    first_slot = node_slot[own_pairs[:, 0]] - column * node_col
    whole_nodes = lax.all_gather(node_blocks, "pair", axis=3, tiled=True)
    first_nodes = jnp.take(whole_nodes, first_slot, axis=0)
    products = complex_product(first_nodes, second_nodes)
    right_side = fetch_items(products, second_list[:, 1])
    whole_products = lax.all_gather(products, "pair", axis=3, tiled=True)
    own_seconds = lax.dynamic_slice_in_dim(second_list, block_start, pair_col, 0)
    left_side = jnp.take(whole_products, own_seconds[:, 0] - block_start, axis=0)
    own_signs = lax.dynamic_slice_in_dim(spin_signs, block_start, pair_col, 0).astype(jnp.float32)
    seconds = complex_product(left_side, right_side) * own_signs[:, None, None, None]
    own_targets = lax.dynamic_slice_in_dim(targets, block_start, pair_col, 0) - column * RES_COL
    selector = (own_targets[None, :] == jnp.arange(RES_COL)[:, None]).astype(jnp.float32)
    return jnp.einsum(
        "rj,jxmn->rxmn",
        selector,
        seconds,
        precision=lax.Precision.HIGHEST,
        preferred_element_type=jnp.float32,
    )


def solution(mesh):
    placed = (P(("cfg", "node"), None, None, "pair"), P(), P(), P(), P(), P())
    return jax.shard_map(
        per_device,
        mesh=mesh,
        in_specs=placed,
        out_specs=P(("cfg", "node"), None, None, "pair"),
        check_vma=False,
    )
```

```python
import functools

import jax
import jax.numpy as jnp
from jax import lax
from jax.experimental import pallas as pl
from jax.experimental.pallas import tpu as pltpu
from jax.sharding import PartitionSpec as P

RES_COL = 2
LANES = 128
NODE_SHARE = 9 / 32
PAIR_SHARE = 0.5
ANY = pl.BlockSpec(memory_space=pl.ANY)
SMEM = pl.BlockSpec(memory_space=pltpu.SMEM)
VMEM = pl.BlockSpec(memory_space=pltpu.VMEM)


def cut_kernel(in_ref, out_ref):
    rows = out_ref.shape[3]
    for j in range(out_ref.shape[0]):
        out_ref[j] = in_ref[:, :, j * rows : (j + 1) * rows, :]


def cut_rows(nodes, group, part, width):
    count, _, order, _ = nodes.shape
    rows = order // group
    steps = 4 if group % 4 == 0 else 1
    return pl.pallas_call(
        cut_kernel,
        grid=(steps,),
        in_specs=[pl.BlockSpec((count, 2, order // steps, width), lambda i: (0, 0, i, part))],
        out_specs=pl.BlockSpec((group // steps, count, 2, rows, width), lambda i: (i, 0, 0, 0, 0)),
        out_shape=jax.ShapeDtypeStruct((group, count, 2, rows, width), jnp.float32),
        name="cut_rows",
    )(nodes)


def cross_kernel(skip, half_ref, ids_ref, spread_ref, out_ref, seen_ref, sem):
    half = half_ref[0]
    count, room = spread_ref.shape[0], out_ref.shape[0]
    asked = ids_ref.shape[0] // 2

    def clear(i, carry):
        seen_ref[i] = 0
        return carry

    lax.fori_loop(0, count, clear, 0, unroll=8)

    def visit(q, found):
        item = ids_ref[(1 - half) * asked + q] - half * count
        inside = (item >= 0) & (item < count)
        safe = jnp.where(inside, item, 0)
        fresh = inside & (seen_ref[safe] == 0)
        place = found - skip

        @pl.when(fresh)
        def _():
            seen_ref[safe] = 1

        @pl.when(fresh & (place >= 0) & (place < room))
        def _():
            pltpu.make_async_copy(spread_ref.at[safe], out_ref.at[place], sem).start()

        return found + fresh.astype(jnp.int32)

    found = lax.fori_loop(0, asked, visit, jnp.int32(0))

    def fill(i, carry):
        pltpu.make_async_copy(spread_ref.at[0], out_ref.at[i], sem).start()
        return carry

    lax.fori_loop(jnp.clip(found - skip, 0, room), room, fill, 0)
    pltpu.make_async_copy(spread_ref.at[pl.ds(0, room)], out_ref, sem).wait()


def pick_cross(half, ids, spread, skip, room):
    return pl.pallas_call(
        functools.partial(cross_kernel, skip),
        in_specs=[SMEM, SMEM, ANY],
        out_specs=VMEM,
        out_shape=jax.ShapeDtypeStruct((room,) + spread.shape[1:], jnp.float32),
        scratch_shapes=[pltpu.SMEM((spread.shape[0],), jnp.int32), pltpu.SemaphoreType.DMA],
        name="pick_cross",
    )(half, ids, spread)


def own_kernel(half_ref, ids_ref, spread_ref, recv_ref, extra_ref, out_ref, place_ref, sem):
    half = half_ref[0]
    count, room = spread_ref.shape[0], recv_ref.shape[0]
    asked = out_ref.shape[0]

    def clear(i, carry):
        place_ref[i] = -1
        return carry

    lax.fori_loop(0, count, clear, 0, unroll=8)

    def visit(q, found):
        item = ids_ref[half * asked + q]
        here = item - half * count
        there = item - (1 - half) * count
        inside = (here >= 0) & (here < count)

        @pl.when(inside)
        def _():
            pltpu.make_async_copy(spread_ref.at[here], out_ref.at[q], sem).start()

        safe = jnp.where(inside, 0, there)
        known = place_ref[safe]
        fresh = (known < 0) & jnp.logical_not(inside)
        place = jnp.where(known < 0, found, known)

        @pl.when(fresh)
        def _():
            place_ref[safe] = found

        @pl.when(jnp.logical_not(inside) & (place < room))
        def _():
            pltpu.make_async_copy(recv_ref.at[place], out_ref.at[q], sem).start()

        @pl.when(jnp.logical_not(inside) & (place >= room))
        def _():
            pltpu.make_async_copy(extra_ref.at[place - room], out_ref.at[q], sem).start()

        return found + fresh.astype(jnp.int32)

    lax.fori_loop(0, asked, visit, jnp.int32(0))
    pltpu.make_async_copy(spread_ref.at[pl.ds(0, asked)], out_ref, sem).wait()


def pick_own(half, ids, spread, recv, extra):
    asked = ids.shape[0] // 2
    return pl.pallas_call(
        own_kernel,
        in_specs=[SMEM, SMEM, ANY, ANY, ANY],
        out_specs=VMEM,
        out_shape=jax.ShapeDtypeStruct((asked,) + spread.shape[1:], jnp.float32),
        scratch_shapes=[pltpu.SMEM((spread.shape[0],), jnp.int32), pltpu.SemaphoreType.DMA],
        name="pick_own",
    )(half, ids, spread, recv, extra)


def most_crossing(ids, count):
    asked = ids.shape[0] // 2
    items = jnp.arange(2 * count, dtype=jnp.int32)
    hits = (ids.reshape(2, asked, 1) == items).any(axis=1)
    crossing = hits & (items // count != jnp.arange(2, dtype=jnp.int32)[:, None])
    return jnp.max(jnp.sum(crossing.astype(jnp.int32), axis=1))


def fetch_items(parts, ids, share):
    devices = lax.axis_size("node")
    group = devices // 2
    half = (lax.axis_index("node") // group).astype(jnp.int32).reshape(1)
    halves = [[h * group + i for i in range(group)] for h in range(2)]
    swap = [(i, (i + group) % devices) for i in range(devices)]
    count = group * parts[0].shape[1]
    room = min(count, max(8, int(count * share)))
    crowded = most_crossing(ids, count) > room
    fetched = []
    for part in parts:
        spread = lax.all_to_all(part, "node", 0, 0, axis_index_groups=halves, tiled=True)
        spread = spread.reshape((count,) + spread.shape[2:])
        recv = lax.ppermute(pick_cross(half, ids, spread, 0, room), "node", swap)
        rest = count - room
        if rest:
            extra = lax.cond(
                crowded,
                lambda x: lax.ppermute(pick_cross(half, ids, x, room, rest), "node", swap),
                lambda x: jnp.zeros((rest,) + x.shape[1:], x.dtype),
                spread,
            )
        else:
            extra = recv
        picked = pick_own(half, ids, spread, recv, extra)
        picked = picked.reshape((group, picked.shape[0] // group) + picked.shape[1:])
        fetched.append(
            lax.all_to_all(picked, "node", 0, 0, axis_index_groups=halves, tiled=True)
        )
    return fetched


def joined(left_real, left_imag, right):
    order = left_real.shape[1]
    width = right.shape[-1]
    right_real = right[:, 0, 0].reshape(order, width)
    right_imag = right[:, 0, 1].reshape(order, width)
    stacked_left = jnp.concatenate([left_real, left_imag], axis=1)
    stacked_right = jnp.concatenate(
        [
            jnp.concatenate([right_real, right_imag], axis=1),
            jnp.concatenate([-right_imag, right_real], axis=1),
        ],
        axis=0,
    )
    return jnp.dot(
        stacked_left,
        stacked_right,
        precision=lax.Precision.HIGHEST,
        preferred_element_type=jnp.float32,
    )


def pair_kernel(first_ref, left_ref, right_ref, out_ref):
    group, _, _, rows, width = out_ref.shape
    both = joined(left_ref[0, 0], left_ref[0, 1], right_ref[...])
    out_ref[:, 0, 0] = both[:, :width].reshape(group, rows, width)
    out_ref[:, 0, 1] = both[:, width:].reshape(group, rows, width)


def pair_products(first_slot, nodes, right):
    group, pairs, _, rows, width = right.shape
    block = (group, 1, 2, rows, width)
    order = nodes.shape[2]
    return pl.pallas_call(
        pair_kernel,
        grid_spec=pltpu.PrefetchScalarGridSpec(
            num_scalar_prefetch=1,
            grid=(pairs,),
            in_specs=[
                pl.BlockSpec((1, 2, order, order), lambda k, first: (first[k], 0, 0, 0)),
                pl.BlockSpec(block, lambda k, first: (0, k, 0, 0, 0)),
            ],
            out_specs=pl.BlockSpec(block, lambda k, first: (0, k, 0, 0, 0)),
        ),
        out_shape=jax.ShapeDtypeStruct(right.shape, jnp.float32),
        name="pair_products",
    )(first_slot, nodes, right)


def second_kernel(side_count, left_index, target, sign, *refs):
    left_refs, right_ref, out_ref = refs[:side_count], refs[side_count], refs[-1]
    step = pl.program_id(0)
    order = out_ref.shape[2]
    width = right_ref.shape[-1]

    @pl.when(step == 0)
    def _():
        out_ref[...] = jnp.zeros_like(out_ref)

    sides = [
        jnp.concatenate([ref[:, 0, c].reshape(order, ref.shape[-1]) for ref in left_refs], axis=1)
        for c in range(2)
    ]
    both = joined(sides[0], sides[1], right_ref[...]) * sign[step].astype(jnp.float32)
    row = target[step]
    out_ref[row, 0] += both[:, :width]
    out_ref[row, 1] += both[:, width:]


def second_products(left_index, target, sign, lefts, right, part, parts, before):
    group, seconds, _, rows, width = right.shape
    order = group * rows
    block = (group, 1, 2, rows, width)
    left_spec = pl.BlockSpec(block, lambda k, left, t, s: (0, left[k], 0, 0, 0))
    in_specs = [left_spec] * len(lefts)
    in_specs.append(pl.BlockSpec(block, lambda k, left, t, s: (0, k, 0, 0, 0)))
    operands = [left_index, target, sign, *lefts, right]
    aliases = {}
    if before is not None:
        aliases = {len(operands): 0}
        operands.append(before)
        in_specs.append(ANY)
    return pl.pallas_call(
        functools.partial(second_kernel, len(lefts)),
        grid_spec=pltpu.PrefetchScalarGridSpec(
            num_scalar_prefetch=3,
            grid=(seconds,),
            in_specs=in_specs,
            out_specs=pl.BlockSpec(
                (RES_COL, 2, order, width), lambda k, left, t, s: (0, 0, 0, part)
            ),
        ),
        out_shape=jax.ShapeDtypeStruct((RES_COL, 2, order, width * parts), jnp.float32),
        input_output_aliases=aliases,
        name="second_products",
    )(*operands)


def per_device(node_blocks, node_slot, pair_list, second_list, targets, spin_signs):
    devices = lax.axis_size("node")
    column = lax.axis_index("node")
    group = devices // 2
    node_col, _, _, local_width = node_blocks.shape
    pair_col = pair_list.shape[0] // devices
    second_col = second_list.shape[0] // devices
    width = min(LANES, local_width)
    parts = local_width // width
    cuts = [cut_rows(node_blocks, group, c, width) for c in range(parts)]
    rights = fetch_items(cuts, node_slot[pair_list[:, 1]], NODE_SHARE)
    own_pairs = lax.dynamic_slice_in_dim(pair_list, column * pair_col, pair_col, 0)
    first_slot = node_slot[own_pairs[:, 0]] - column * node_col
    whole_nodes = node_blocks
    if lax.axis_size("pair") > 1:
        whole_nodes = lax.all_gather(node_blocks, "pair", axis=3, tiled=True)
    products = [pair_products(first_slot, whole_nodes, right) for right in rights]
    second_rights = fetch_items(products, second_list[:, 1], PAIR_SHARE)
    lefts = products
    if lax.axis_size("pair") > 1:
        gathered = [lax.all_gather(product, "pair", axis=0) for product in products]
        lefts = [g[c] for c in range(lax.axis_size("pair")) for g in gathered]
    own_seconds = lax.dynamic_slice_in_dim(second_list, column * second_col, second_col, 0)
    left_index = own_seconds[:, 0] - column * pair_col
    own_signs = lax.dynamic_slice_in_dim(spin_signs, column * second_col, second_col, 0)
    own_targets = lax.dynamic_slice_in_dim(targets, column * second_col, second_col, 0)
    own_targets = own_targets - column * RES_COL
    results = None
    for part, right in enumerate(second_rights):
        results = second_products(
            left_index, own_targets, own_signs, lefts, right, part, parts, results
        )
    return results


def solution(mesh):
    placed = (P(("cfg", "node"), None, None, "pair"), P(), P(), P(), P(), P())
    return jax.shard_map(
        per_device,
        mesh=mesh,
        in_specs=placed,
        out_specs=P(("cfg", "node"), None, None, "pair"),
        check_vma=False,
    )
```

```python
import functools

import jax
import jax.numpy as jnp
from jax import lax
from jax.experimental import pallas as pl
from jax.experimental.pallas import tpu as pltpu
from jax.sharding import PartitionSpec as P


RES_COL = 2
LANES = 128
NODE_SHARE = 9 / 32
PAIR_SHARE = 0.5
ANY = pl.BlockSpec(memory_space=pl.ANY)
SMEM = pl.BlockSpec(memory_space=pltpu.SMEM)
VMEM = pl.BlockSpec(memory_space=pltpu.VMEM)
PARAMS = pltpu.CompilerParams(vmem_limit_bytes=16 * 1024 * 1024)


def cut_kernel(in_ref, out_ref):
    rows = out_ref.shape[3]
    for j in range(out_ref.shape[0]):
        out_ref[j] = in_ref[:, :, j * rows : (j + 1) * rows, :]


def cut_rows(nodes, group, part, width):
    count, _, order, _ = nodes.shape
    rows = order // group
    steps = 4 if group % 4 == 0 else 1
    return pl.pallas_call(
        cut_kernel,
        grid=(steps,),
        in_specs=[pl.BlockSpec((count, 2, order // steps, width), lambda i: (0, 0, i, part))],
        out_specs=pl.BlockSpec((group // steps, count, 2, rows, width), lambda i: (i, 0, 0, 0, 0)),
        out_shape=jax.ShapeDtypeStruct((group, count, 2, rows, width), jnp.float32),
        name="cut_rows",
    )(nodes)


def plan_kernel(room, half_ref, ids_ref, send_ref, source_ref, crowded_ref, place_ref):
    half = half_ref[0]
    count = send_ref.shape[0]
    asked = source_ref.shape[0]

    def clear(i, carry):
        place_ref[i] = -1
        send_ref[i % count] = 0
        return carry

    lax.fori_loop(0, 2 * count, clear, 0, unroll=8)

    def visit_other(q, found):
        item = ids_ref[(1 - half) * asked + q]
        here = item - half * count
        inside = (here >= 0) & (here < count)
        fresh = inside & (place_ref[item] < 0)

        @pl.when(fresh)
        def _():
            place_ref[item] = found
            send_ref[found] = here

        return found + fresh.astype(jnp.int32)

    def visit_own(q, found):
        item = ids_ref[half * asked + q]
        here = item - half * count
        inside = (here >= 0) & (here < count)
        known = place_ref[item]
        fresh = jnp.logical_not(inside) & (known < 0)

        @pl.when(fresh)
        def _():
            place_ref[item] = found

        place = jnp.where(known < 0, found, known)
        source_ref[q] = jnp.where(inside, here, count + place)
        return found + fresh.astype(jnp.int32)

    sent = lax.fori_loop(0, asked, visit_other, jnp.int32(0))
    received = lax.fori_loop(0, asked, visit_own, jnp.int32(0))
    crowded_ref[0] = (jnp.maximum(sent, received) > room).astype(jnp.int32)


def make_plan(half, ids, count, room):
    asked = ids.shape[0] // 2
    return pl.pallas_call(
        functools.partial(plan_kernel, room),
        in_specs=[SMEM, SMEM],
        out_specs=[SMEM, SMEM, SMEM],
        out_shape=[
            jax.ShapeDtypeStruct((count,), jnp.int32),
            jax.ShapeDtypeStruct((asked,), jnp.int32),
            jax.ShapeDtypeStruct((1,), jnp.int32),
        ],
        scratch_shapes=[pltpu.SMEM((2 * count,), jnp.int32)],
        compiler_params=PARAMS,
        name="make_plan",
    )(half, ids)


def cross_kernel(skip, send_ref, spread_ref, out_ref):
    def copy(i, carry):
        out_ref[i] = spread_ref[send_ref[skip + i]]
        return carry

    lax.fori_loop(0, out_ref.shape[0], copy, 0, unroll=4)


def pick_cross(send, spread, skip, room):
    return pl.pallas_call(
        functools.partial(cross_kernel, skip),
        in_specs=[SMEM, VMEM],
        out_specs=VMEM,
        out_shape=jax.ShapeDtypeStruct((room,) + spread.shape[1:], jnp.float32),
        compiler_params=PARAMS,
        name="pick_cross",
    )(send, spread)


def own_kernel(source_ref, spread_ref, recv_ref, extra_ref, out_ref, sem):
    count, room = spread_ref.shape[0], recv_ref.shape[0]

    def copy(q, carry):
        source = source_ref[q]

        @pl.when(source < count)
        def _():
            out_ref[q] = spread_ref[source]

        @pl.when((source >= count) & (source < count + room))
        def _():
            out_ref[q] = recv_ref[source - count]

        @pl.when(source >= count + room)
        def _():
            late = pltpu.make_async_copy(extra_ref.at[source - count - room], out_ref.at[q], sem)
            late.start()
            late.wait()

        return carry

    lax.fori_loop(0, out_ref.shape[0], copy, 0)


def pick_own(source, spread, recv, extra):
    return pl.pallas_call(
        own_kernel,
        in_specs=[SMEM, VMEM, VMEM, ANY],
        out_specs=VMEM,
        out_shape=jax.ShapeDtypeStruct((source.shape[0],) + spread.shape[1:], jnp.float32),
        scratch_shapes=[pltpu.SemaphoreType.DMA],
        compiler_params=PARAMS,
        name="pick_own",
    )(source, spread, recv, extra)


def fetch_items(parts, ids, share):
    devices = lax.axis_size("node")
    group = devices // 2
    half = (lax.axis_index("node") // group).astype(jnp.int32).reshape(1)
    halves = [[h * group + i for i in range(group)] for h in range(2)]
    swap = [(i, (i + group) % devices) for i in range(devices)]
    count = group * parts[0].shape[1]
    room = min(count - 1, max(8, int(count * share)))
    rest = count - room
    send, source, crowded = make_plan(half, ids, count, room)
    fetched = []
    for part in parts:
        spread = lax.all_to_all(part, "node", 0, 0, axis_index_groups=halves, tiled=True)
        spread = spread.reshape((count,) + spread.shape[2:])
        leaving = pick_cross(send, spread, 0, room)
        recv = lax.ppermute(leaving, "node", swap)
        extra = lax.cond(
            crowded[0] > 0,
            lambda x, s: lax.ppermute(pick_cross(s, x, room, rest), "node", swap),
            lambda x, s: jnp.zeros((rest,) + x.shape[1:], x.dtype),
            spread,
            send,
        )
        picked = pick_own(source, spread, recv, extra)
        picked = picked.reshape((group, picked.shape[0] // group) + picked.shape[1:])
        fetched.append(lax.all_to_all(picked, "node", 0, 0, axis_index_groups=halves, tiled=True))
    return fetched


def joined(left_real, left_imag, right):
    order = left_real.shape[1]
    width = right.shape[-1]
    right_real = right[:, 0, 0].reshape(order, width)
    right_imag = right[:, 0, 1].reshape(order, width)
    stacked_left = jnp.concatenate([left_real, left_imag], axis=1)
    stacked_right = jnp.concatenate(
        [
            jnp.concatenate([right_real, right_imag], axis=1),
            jnp.concatenate([-right_imag, right_real], axis=1),
        ],
        axis=0,
    )
    return jnp.dot(
        stacked_left,
        stacked_right,
        precision=lax.Precision.HIGHEST,
        preferred_element_type=jnp.float32,
    )


def pair_kernel(first_ref, nodes_ref, right_ref, out_ref, left_ref, sems):
    group, _, _, rows, width = out_ref.shape
    step = pl.program_id(0)

    def fetch(k):
        return pltpu.make_async_copy(nodes_ref.at[first_ref[k]], left_ref.at[k], sems.at[k])

    @pl.when(step == 0)
    def _():
        for k in range(left_ref.shape[0]):
            fetch(k).start()

    fetch(step).wait()
    left = left_ref[step]
    both = joined(left[0], left[1], right_ref[...])
    out_ref[:, 0, 0] = both[:, :width].reshape(group, rows, width)
    out_ref[:, 0, 1] = both[:, width:].reshape(group, rows, width)


def pair_products(first_slot, nodes, right):
    group, pairs, _, rows, width = right.shape
    block = (group, 1, 2, rows, width)
    order = nodes.shape[2]
    return pl.pallas_call(
        pair_kernel,
        grid_spec=pltpu.PrefetchScalarGridSpec(
            num_scalar_prefetch=1,
            grid=(pairs,),
            in_specs=[
                pl.BlockSpec(memory_space=pltpu.HBM),
                pl.BlockSpec(block, lambda k, first: (0, k, 0, 0, 0)),
            ],
            out_specs=pl.BlockSpec(block, lambda k, first: (0, k, 0, 0, 0)),
            scratch_shapes=[
                pltpu.VMEM((pairs, 2, order, order), jnp.float32),
                pltpu.SemaphoreType.DMA((pairs,)),
            ],
        ),
        out_shape=jax.ShapeDtypeStruct(right.shape, jnp.float32),
        compiler_params=PARAMS,
        name="pair_products",
    )(first_slot, nodes, right)


def second_kernel(side_count, left_index, target, sign, *refs):
    left_refs, right_ref, out_ref = refs[:side_count], refs[side_count], refs[-1]
    step = pl.program_id(0)
    order = out_ref.shape[2]
    width = right_ref.shape[-1]

    @pl.when(step == 0)
    def _():
        out_ref[...] = jnp.zeros_like(out_ref)

    sides = [
        jnp.concatenate([ref[:, 0, c].reshape(order, ref.shape[-1]) for ref in left_refs], axis=1)
        for c in range(2)
    ]
    both = joined(sides[0], sides[1], right_ref[...]) * sign[step].astype(jnp.float32)
    row = target[step]
    out_ref[row, 0] += both[:, :width]
    out_ref[row, 1] += both[:, width:]


def second_products(left_index, target, sign, lefts, right, part, parts, before):
    group, seconds, _, rows, width = right.shape
    order = group * rows
    block = (group, 1, 2, rows, width)
    left_spec = pl.BlockSpec(block, lambda k, left, t, s: (0, left[k], 0, 0, 0))
    in_specs = [left_spec] * len(lefts)
    in_specs.append(pl.BlockSpec(block, lambda k, left, t, s: (0, k, 0, 0, 0)))
    operands = [left_index, target, sign, *lefts, right]
    aliases = {}
    if before is not None:
        aliases = {len(operands): 0}
        operands.append(before)
        in_specs.append(ANY)
    return pl.pallas_call(
        functools.partial(second_kernel, len(lefts)),
        grid_spec=pltpu.PrefetchScalarGridSpec(
            num_scalar_prefetch=3,
            grid=(seconds,),
            in_specs=in_specs,
            out_specs=pl.BlockSpec(
                (RES_COL, 2, order, width), lambda k, left, t, s: (0, 0, 0, part)
            ),
        ),
        out_shape=jax.ShapeDtypeStruct((RES_COL, 2, order, width * parts), jnp.float32),
        input_output_aliases=aliases,
        compiler_params=PARAMS,
        name="second_products",
    )(*operands)


def per_device(node_blocks, node_slot, pair_list, second_list, targets, spin_signs):
    devices = lax.axis_size("node")
    column = lax.axis_index("node")
    group = devices // 2
    node_col, _, _, local_width = node_blocks.shape
    pair_col = pair_list.shape[0] // devices
    second_col = second_list.shape[0] // devices
    width = min(LANES, local_width)
    parts = local_width // width
    cuts = [cut_rows(node_blocks, group, c, width) for c in range(parts)]
    rights = fetch_items(cuts, node_slot[pair_list[:, 1]], NODE_SHARE)
    own_pairs = lax.dynamic_slice_in_dim(pair_list, column * pair_col, pair_col, 0)
    first_slot = node_slot[own_pairs[:, 0]] - column * node_col
    whole_nodes = node_blocks
    if lax.axis_size("pair") > 1:
        whole_nodes = lax.all_gather(node_blocks, "pair", axis=3, tiled=True)
    products = [pair_products(first_slot, whole_nodes, right) for right in rights]
    second_rights = fetch_items(products, second_list[:, 1], PAIR_SHARE)
    lefts = products
    if lax.axis_size("pair") > 1:
        gathered = [lax.all_gather(product, "pair", axis=0) for product in products]
        lefts = [g[c] for c in range(lax.axis_size("pair")) for g in gathered]
    own_seconds = lax.dynamic_slice_in_dim(second_list, column * second_col, second_col, 0)
    left_index = own_seconds[:, 0] - column * pair_col
    own_signs = lax.dynamic_slice_in_dim(spin_signs, column * second_col, second_col, 0)
    own_targets = lax.dynamic_slice_in_dim(targets, column * second_col, second_col, 0)
    own_targets = own_targets - column * RES_COL
    results = None
    for part, right in enumerate(second_rights):
        results = second_products(
            left_index, own_targets, own_signs, lefts, right, part, parts, results
        )
    return results


def solution(mesh):
    placed = (P(("cfg", "node"), None, None, "pair"), P(), P(), P(), P(), P())

    return jax.shard_map(
        per_device,
        mesh=mesh,
        in_specs=placed,
        out_specs=P(("cfg", "node"), None, None, "pair"),
        check_vma=False,
    )
```

```python
import functools

import jax
import jax.numpy as jnp
from jax import lax
from jax.experimental import pallas as pl
from jax.experimental.pallas import tpu as pltpu
from jax.sharding import PartitionSpec as P


RES_COL = 2
LANES = 128
EARLY_SHARE = 27 / 64
LATE_SHARE = 3 / 32
ANY = pl.BlockSpec(memory_space=pl.ANY)
HBM = pl.BlockSpec(memory_space=pltpu.HBM)
SMEM = pl.BlockSpec(memory_space=pltpu.SMEM)
VMEM = pl.BlockSpec(memory_space=pltpu.VMEM)
PARAMS = pltpu.CompilerParams(vmem_limit_bytes=24 * 1024 * 1024)


def cut_kernel(in_ref, out_ref):
    rows = out_ref.shape[3]
    for j in range(out_ref.shape[0]):
        out_ref[j] = in_ref[:, :, j * rows : (j + 1) * rows, :]


def cut_rows(nodes, group, part, width):
    count, _, order, _ = nodes.shape
    rows = order // group
    steps = 4 if group % 4 == 0 else 1
    return pl.pallas_call(
        cut_kernel,
        grid=(steps,),
        in_specs=[pl.BlockSpec((count, 2, order // steps, width), lambda i: (0, 0, i, part))],
        out_specs=pl.BlockSpec((group // steps, count, 2, rows, width), lambda i: (i, 0, 0, 0, 0)),
        out_shape=jax.ShapeDtypeStruct((group, count, 2, rows, width), jnp.float32),
        name="cut_rows",
    )(nodes)


def plan_kernel(rooms, half_ref, *refs):
    ids_refs, send_refs, source_refs = refs[:2], refs[2:4], refs[4:6]
    crowded_ref, place_ref = refs[6:]
    half = half_ref[0]
    count = send_refs[0].shape[0]
    bases = (count, count + rooms[0])
    everything = count + rooms[0] + rooms[1]

    def clear(i, carry):
        place_ref[i] = -1
        return carry

    def empty(i, carry):
        for send_ref in send_refs:
            send_ref[i] = 0
        return carry

    lax.fori_loop(0, 2 * count, clear, 0, unroll=8)
    lax.fori_loop(0, count, empty, 0, unroll=8)
    most = jnp.int32(0)
    for ids_ref, send_ref, source_ref, base, room in zip(
        ids_refs, send_refs, source_refs, bases, rooms
    ):
        asked = source_ref.shape[0]

        def visit_other(q, found):
            item = ids_ref[(1 - half) * asked + q]
            here = item - half * count
            fresh = (here >= 0) & (here < count) & (place_ref[item] < 0)

            @pl.when(fresh)
            def _():
                place_ref[item] = 0
                send_ref[found] = here

            return found + fresh.astype(jnp.int32)

        def visit_own(q, found):
            item = ids_ref[half * asked + q]
            here = item - half * count
            inside = (here >= 0) & (here < count)
            known = place_ref[item]
            fresh = jnp.logical_not(inside) & (known < 0)
            there = everything + item - (1 - half) * count
            place = jnp.where(known < 0, jnp.where(found < room, base + found, there), known)

            @pl.when(fresh)
            def _():
                place_ref[item] = place

            source_ref[q] = jnp.where(inside, here, place)
            return found + fresh.astype(jnp.int32)

        sent = lax.fori_loop(0, asked, visit_other, jnp.int32(0))
        received = lax.fori_loop(0, asked, visit_own, jnp.int32(0))
        most = jnp.maximum(most, jnp.maximum(sent, received) - room)
    crowded_ref[0] = (most > 0).astype(jnp.int32)


def make_plan(half, early, late, count, rooms):
    whole = jax.ShapeDtypeStruct((count,), jnp.int32)
    return pl.pallas_call(
        functools.partial(plan_kernel, rooms),
        in_specs=[SMEM] * 3,
        out_specs=[SMEM] * 5,
        out_shape=[
            whole,
            whole,
            jax.ShapeDtypeStruct((early.shape[0] // 2,), jnp.int32),
            jax.ShapeDtypeStruct((late.shape[0] // 2,), jnp.int32),
            jax.ShapeDtypeStruct((1,), jnp.int32),
        ],
        scratch_shapes=[pltpu.SMEM((2 * count,), jnp.int32)],
        compiler_params=PARAMS,
        name="make_plan",
    )(half, early, late)


def leave_kernel(send_ref, *refs):
    spread_refs, out_ref = refs[:-1], refs[-1]
    for c, spread_ref in enumerate(spread_refs):

        def copy(i, carry):
            out_ref[i, c] = spread_ref[send_ref[i]]
            return carry

        lax.fori_loop(0, out_ref.shape[0], copy, 0, unroll=4)


def pick_leaving(send, spreads, room):
    return pl.pallas_call(
        leave_kernel,
        in_specs=[SMEM] + [VMEM] * len(spreads),
        out_specs=VMEM,
        out_shape=jax.ShapeDtypeStruct((room, len(spreads)) + spreads[0].shape[1:], jnp.float32),
        compiler_params=PARAMS,
        name="pick_leaving",
    )(send, *spreads)


def collect_kernel(parts, bounds, source_ref, *refs):
    spread_refs, early_refs, extra_refs = (refs[i * parts : (i + 1) * parts] for i in range(3))
    late_ref = refs[3 * parts] if bounds[2] > bounds[1] else None
    out_ref, sem = refs[-2:]
    here, early, late = bounds

    def copy(q, carry):
        source = source_ref[q]

        @pl.when(source < here)
        def _():
            for c in range(parts):
                out_ref[q, c] = spread_refs[c][source]

        @pl.when((source >= here) & (source < early))
        def _():
            for c in range(parts):
                out_ref[q, c] = early_refs[c][source - here, 0]

        if late_ref is not None:

            @pl.when((source >= early) & (source < late))
            def _():
                for c in range(parts):
                    out_ref[q, c] = late_ref[source - early, c]

        return carry

    lax.fori_loop(0, out_ref.shape[0], copy, 0)

    def fetch(q, carry):
        source = source_ref[q] - late

        @pl.when(source >= 0)
        def _():
            for c in range(parts):
                slow = pltpu.make_async_copy(extra_refs[c].at[source], out_ref.at[q, c], sem)
                slow.start()
                slow.wait()

        return carry

    lax.fori_loop(0, out_ref.shape[0], fetch, 0)


def collect(source, spreads, earlies, extras, late, bounds):
    parts = len(spreads)
    arrays = [*spreads, *earlies, *extras]
    specs = [VMEM] * (2 * parts) + [ANY] * parts
    if late is not None:
        arrays.append(late)
        specs.append(VMEM)
    return pl.pallas_call(
        functools.partial(collect_kernel, parts, bounds),
        in_specs=[SMEM] + specs,
        out_specs=VMEM,
        out_shape=jax.ShapeDtypeStruct(
            (source.shape[0], parts) + spreads[0].shape[1:], jnp.float32
        ),
        scratch_shapes=[pltpu.SemaphoreType.DMA],
        compiler_params=PARAMS,
        name="collect",
    )(source, *arrays)


def fetch_items(cuts, early_ids, late_ids):
    devices = lax.axis_size("node")
    group = devices // 2
    half = (lax.axis_index("node") // group).astype(jnp.int32).reshape(1)
    halves = [[h * group + i for i in range(group)] for h in range(2)]
    swap = [(i, (i + group) % devices) for i in range(devices)]
    count = group * cuts[0].shape[1]
    rooms = tuple(min(count, max(8, int(count * share))) for share in (EARLY_SHARE, LATE_SHARE))
    send_early, send_late, early_source, late_source, crowded = make_plan(
        half, early_ids.reshape(-1), late_ids.reshape(-1), count, rooms
    )

    def exchange(x):
        x = x.reshape((group, x.shape[0] // group) + x.shape[1:])
        return lax.all_to_all(x, "node", 0, 0, axis_index_groups=halves, tiled=True)

    spreads, earlies, extras = [], [], []
    for cut in cuts:
        spread = lax.all_to_all(cut, "node", 0, 0, axis_index_groups=halves, tiled=True)
        spread = spread.reshape((count,) + spread.shape[2:])
        leaving = pick_leaving(send_early, [spread], rooms[0])
        earlies.append(lax.ppermute(leaving, "node", swap))
        extras.append(
            lax.cond(
                crowded[0] > 0,
                lambda x: lax.ppermute(x, "node", swap),
                jnp.zeros_like,
                spread,
            )
        )
        spreads.append(spread)
    leaving = pick_leaving(send_late, spreads, rooms[1])
    late = lax.ppermute(leaving, "node", swap)
    bounds = (count, count + rooms[0], count + rooms[0] + rooms[1])
    delivered = []
    for c in range(len(cuts)):
        picked = collect(
            early_source,
            spreads[c : c + 1],
            earlies[c : c + 1],
            extras[c : c + 1],
            None,
            (count, count + rooms[0], count + rooms[0]),
        )
        delivered.append(exchange(picked))
    picked = collect(late_source, spreads, earlies, extras, late, bounds)
    last = exchange(picked)
    return delivered, last


def product(left_real, left_imag, blocks):
    order = left_real.shape[1]
    right_real, right_imag = (
        jnp.concatenate([b[:, c].reshape(order, b.shape[-1]) for b in blocks], axis=1)
        for c in range(2)
    )
    stacked_left = jnp.concatenate([left_real, left_imag], axis=1)
    stacked_right = jnp.concatenate(
        [
            jnp.concatenate([right_real, right_imag], axis=1),
            jnp.concatenate([-right_imag, right_real], axis=1),
        ],
        axis=0,
    )
    return jnp.dot(
        stacked_left,
        stacked_right,
        precision=lax.Precision.HIGHEST,
        preferred_element_type=jnp.float32,
    )


def multiply_kernel(first_ref, left_ref, *refs):
    right_refs, out_ref, hold_ref, sems = refs[:-3], refs[-3], refs[-2], refs[-1]
    step = pl.program_id(0)
    width = out_ref.shape[-1]

    def fetch(k):
        return pltpu.make_async_copy(left_ref.at[first_ref[k]], hold_ref.at[k], sems.at[k])

    @pl.when(step == 0)
    def _():
        for k in range(hold_ref.shape[0]):
            fetch(k).start()

    fetch(step).wait()
    left = hold_ref[step]
    both = product(left[0], left[1], [ref[:, 0, 0] for ref in right_refs])
    out_ref[0, 0] = both[:, :width]
    out_ref[0, 1] = both[:, width:]


def multiply(left_index, lefts, rights, offset, number):
    group, _, _, _, rows, width = rights[0].shape
    order = lefts.shape[2]
    cols = width * len(rights)
    right_spec = pl.BlockSpec(
        (group, 1, 1, 2, rows, width), lambda k, index: (0, offset + k, 0, 0, 0, 0)
    )
    return pl.pallas_call(
        multiply_kernel,
        grid_spec=pltpu.PrefetchScalarGridSpec(
            num_scalar_prefetch=1,
            grid=(number,),
            in_specs=[HBM] + [right_spec] * len(rights),
            out_specs=pl.BlockSpec((1, 2, order, cols), lambda k, index: (k, 0, 0, 0)),
            scratch_shapes=[
                pltpu.VMEM((number, 2, order, order), jnp.float32),
                pltpu.SemaphoreType.DMA((number,)),
            ],
        ),
        out_shape=jax.ShapeDtypeStruct((number, 2, order, cols), jnp.float32),
        compiler_params=PARAMS,
        name="multiply",
    )(left_index, lefts, *rights)


def finish_kernel(target, sign, left_ref, right_ref, out_ref):
    step = pl.program_id(0)
    width = out_ref.shape[-1]

    @pl.when(step == 0)
    def _():
        out_ref[...] = jnp.zeros_like(out_ref)

    blocks = [right_ref[:, 0, c] for c in range(right_ref.shape[2])]
    both = product(left_ref[0, 0], left_ref[0, 1], blocks) * sign[step].astype(jnp.float32)
    row = target[step]
    out_ref[row, 0] += both[:, :width]
    out_ref[row, 1] += both[:, width:]


def finish(target, sign, lefts, right):
    group, seconds, parts, _, rows, width = right.shape
    order = lefts.shape[2]
    whole = (RES_COL, 2, order, width * parts)
    return pl.pallas_call(
        finish_kernel,
        grid_spec=pltpu.PrefetchScalarGridSpec(
            num_scalar_prefetch=2,
            grid=(seconds,),
            in_specs=[
                pl.BlockSpec((1, 2, order, order), lambda k, t, s: (k, 0, 0, 0)),
                pl.BlockSpec((group, 1, parts, 2, rows, width), lambda k, t, s: (0, k, 0, 0, 0, 0)),
            ],
            out_specs=pl.BlockSpec(whole, lambda k, t, s: (0, 0, 0, 0)),
        ),
        out_shape=jax.ShapeDtypeStruct(whole, jnp.float32),
        compiler_params=PARAMS,
        name="finish",
    )(target, sign, lefts, right)


def all_columns(x):
    if lax.axis_size("pair") == 1:
        return x
    return lax.all_gather(x, "pair", axis=3, tiled=True)


def per_device(node_blocks, node_slot, pair_list, second_list, targets, spin_signs):
    devices = lax.axis_size("node")
    column = lax.axis_index("node")
    group = devices // 2
    node_col, _, _, local_width = node_blocks.shape
    pair_col = pair_list.shape[0] // devices
    second_col = second_list.shape[0] // devices
    width = min(LANES, local_width)
    cuts = [cut_rows(node_blocks, group, c, width) for c in range(local_width // width)]

    slots = node_slot[pair_list]
    second_slots = slots[second_list[:, 1]]
    early_ids = jnp.concatenate(
        [slots[:, 1].reshape(devices, pair_col), second_slots[:, 0].reshape(devices, second_col)],
        axis=1,
    )
    late_ids = second_slots[:, 1].reshape(devices, second_col)
    rights, lasts = fetch_items(cuts, early_ids, late_ids)

    own_slots = lax.dynamic_slice_in_dim(slots, column * pair_col, pair_col, 0)
    first_slot = own_slots[:, 0] - column * node_col
    own_seconds = lax.dynamic_slice_in_dim(second_list, column * second_col, second_col, 0)
    left_index = own_seconds[:, 0] - column * pair_col
    own_signs = lax.dynamic_slice_in_dim(spin_signs, column * second_col, second_col, 0)
    own_targets = lax.dynamic_slice_in_dim(targets, column * second_col, second_col, 0)
    own_targets = own_targets - column * RES_COL

    products = multiply(first_slot, all_columns(node_blocks), rights, 0, pair_col)
    longer = multiply(left_index, all_columns(products), rights, pair_col, second_col)
    return finish(own_targets, own_signs, all_columns(longer), lasts)


def solution(mesh):
    placed = (P(("cfg", "node"), None, None, "pair"), P(), P(), P(), P(), P())

    return jax.shard_map(
        per_device,
        mesh=mesh,
        in_specs=placed,
        out_specs=P(("cfg", "node"), None, None, "pair"),
        check_vma=False,
    )
```

```python
import functools

import jax
import jax.numpy as jnp
from jax import lax
from jax.experimental import pallas as pl
from jax.experimental.pallas import tpu as pltpu
from jax.sharding import PartitionSpec as P


RES_COL = 2
LANES = 128
EARLY_SHARE = 27 / 64
LATE_SHARE = 3 / 32
ANY = pl.BlockSpec(memory_space=pl.ANY)
HBM = pl.BlockSpec(memory_space=pltpu.HBM)
SMEM = pl.BlockSpec(memory_space=pltpu.SMEM)
VMEM = pl.BlockSpec(memory_space=pltpu.VMEM)
PARAMS = pltpu.CompilerParams(vmem_limit_bytes=24 * 1024 * 1024)
LARGE = pltpu.CompilerParams(vmem_limit_bytes=56 * 1024 * 1024)


def cut_kernel(in_ref, out_ref):
    rows = out_ref.shape[3]
    for j in range(out_ref.shape[0]):
        out_ref[j] = in_ref[:, :, j * rows : (j + 1) * rows, :]


def cut_rows(nodes, group, part, width):
    count, _, order, _ = nodes.shape
    rows = order // group
    steps = 4 if group % 4 == 0 else 1
    return pl.pallas_call(
        cut_kernel,
        grid=(steps,),
        in_specs=[pl.BlockSpec((count, 2, order // steps, width), lambda i: (0, 0, i, part))],
        out_specs=pl.BlockSpec((group // steps, count, 2, rows, width), lambda i: (i, 0, 0, 0, 0)),
        out_shape=jax.ShapeDtypeStruct((group, count, 2, rows, width), jnp.float32),
        name="cut_rows",
    )(nodes)


def plan_kernel(rooms, half_ref, *refs):
    ids_refs, send_refs, source_refs = refs[:2], refs[2:4], refs[4:6]
    crowded_ref, place_ref = refs[6:]
    half = half_ref[0]
    count = send_refs[0].shape[0]
    bases = (count, count + rooms[0])
    everything = count + rooms[0] + rooms[1]

    def clear(i, carry):
        place_ref[i] = -1
        return carry

    def empty(i, carry):
        for send_ref in send_refs:
            send_ref[i] = 0
        return carry

    lax.fori_loop(0, 2 * count, clear, 0, unroll=8)
    lax.fori_loop(0, count, empty, 0, unroll=8)
    most = jnp.int32(0)
    for ids_ref, send_ref, source_ref, base, room in zip(
        ids_refs, send_refs, source_refs, bases, rooms
    ):
        asked = source_ref.shape[0]

        def visit_other(q, found):
            item = ids_ref[(1 - half) * asked + q]
            here = item - half * count
            fresh = (here >= 0) & (here < count) & (place_ref[item] < 0)

            @pl.when(fresh)
            def _():
                place_ref[item] = 0
                send_ref[found] = here

            return found + fresh.astype(jnp.int32)

        def visit_own(q, found):
            item = ids_ref[half * asked + q]
            here = item - half * count
            inside = (here >= 0) & (here < count)
            known = place_ref[item]
            fresh = jnp.logical_not(inside) & (known < 0)
            there = everything + item - (1 - half) * count
            place = jnp.where(known < 0, jnp.where(found < room, base + found, there), known)

            @pl.when(fresh)
            def _():
                place_ref[item] = place

            source_ref[q] = jnp.where(inside, here, place)
            return found + fresh.astype(jnp.int32)

        sent = lax.fori_loop(0, asked, visit_other, jnp.int32(0))
        received = lax.fori_loop(0, asked, visit_own, jnp.int32(0))
        most = jnp.maximum(most, jnp.maximum(sent, received) - room)
    crowded_ref[0] = (most > 0).astype(jnp.int32)


def make_plan(half, early, late, count, rooms):
    whole = jax.ShapeDtypeStruct((count,), jnp.int32)
    return pl.pallas_call(
        functools.partial(plan_kernel, rooms),
        in_specs=[SMEM] * 3,
        out_specs=[SMEM] * 5,
        out_shape=[
            whole,
            whole,
            jax.ShapeDtypeStruct((early.shape[0] // 2,), jnp.int32),
            jax.ShapeDtypeStruct((late.shape[0] // 2,), jnp.int32),
            jax.ShapeDtypeStruct((1,), jnp.int32),
        ],
        scratch_shapes=[pltpu.SMEM((2 * count,), jnp.int32)],
        compiler_params=PARAMS,
        name="make_plan",
    )(half, early, late)


def leave_kernel(send_ref, *refs):
    spread_refs, out_ref = refs[:-1], refs[-1]
    for c, spread_ref in enumerate(spread_refs):

        def copy(i, carry):
            out_ref[i, c] = spread_ref[send_ref[i]]
            return carry

        lax.fori_loop(0, out_ref.shape[0], copy, 0, unroll=4)


def pick_leaving(send, spreads, room):
    return pl.pallas_call(
        leave_kernel,
        in_specs=[SMEM] + [VMEM] * len(spreads),
        out_specs=VMEM,
        out_shape=jax.ShapeDtypeStruct((room, len(spreads)) + spreads[0].shape[1:], jnp.float32),
        compiler_params=PARAMS,
        name="pick_leaving",
    )(send, *spreads)


def collect_kernel(parts, bounds, source_ref, crowded_ref, *refs):
    spread_refs, early_refs, extra_refs = (refs[i * parts : (i + 1) * parts] for i in range(3))
    here, early, late = bounds
    late_ref = refs[3 * parts] if late > early else None
    out_ref, sem = refs[-2:]

    def copy(q, carry):
        source = source_ref[q]
        near = jnp.minimum(source, here - 1)
        far = jnp.clip(source - here, 0, early - here - 1)
        for c in range(parts):
            value = jnp.where(source < here, spread_refs[c][near], early_refs[c][far, 0])
            if late_ref is not None:
                last = jnp.clip(source - early, 0, late - early - 1)
                value = jnp.where(source < early, value, late_ref[last, c])
            out_ref[q, c] = value
        return carry

    lax.fori_loop(0, out_ref.shape[0], copy, 0, unroll=4)

    @pl.when(crowded_ref[0] > 0)
    def _():
        def fetch(q, carry):
            source = source_ref[q] - late

            @pl.when(source >= 0)
            def _():
                for c in range(parts):
                    slow = pltpu.make_async_copy(
                        extra_refs[c].at[source], out_ref.at[q, c], sem
                    )
                    slow.start()
                    slow.wait()

            return carry

        lax.fori_loop(0, out_ref.shape[0], fetch, 0)


def collect(source, crowded, spreads, earlies, extras, late, bounds):
    parts = len(spreads)
    arrays = [*spreads, *earlies, *extras]
    specs = [VMEM] * (2 * parts) + [ANY] * parts
    if late is not None:
        arrays.append(late)
        specs.append(VMEM)
    return pl.pallas_call(
        functools.partial(collect_kernel, parts, bounds),
        in_specs=[SMEM, SMEM] + specs,
        out_specs=VMEM,
        out_shape=jax.ShapeDtypeStruct(
            (source.shape[0], parts) + spreads[0].shape[1:], jnp.float32
        ),
        scratch_shapes=[pltpu.SemaphoreType.DMA],
        compiler_params=PARAMS,
        name="collect",
    )(source, crowded, *arrays)


def fetch_items(cuts, early_ids, late_ids):
    devices = lax.axis_size("node")
    group = devices // 2
    half = (lax.axis_index("node") // group).astype(jnp.int32).reshape(1)
    halves = [[h * group + i for i in range(group)] for h in range(2)]
    swap = [(i, (i + group) % devices) for i in range(devices)]
    count = group * cuts[0].shape[1]
    rooms = tuple(min(count, max(8, int(count * share))) for share in (EARLY_SHARE, LATE_SHARE))
    send_early, send_late, early_source, late_source, crowded = make_plan(
        half, early_ids.reshape(-1), late_ids.reshape(-1), count, rooms
    )

    def exchange(x):
        x = x.reshape((group, x.shape[0] // group) + x.shape[1:])
        return lax.all_to_all(x, "node", 0, 0, axis_index_groups=halves, tiled=True)

    spreads, earlies, extras = [], [], []
    for cut in cuts:
        spread = lax.all_to_all(cut, "node", 0, 0, axis_index_groups=halves, tiled=True)
        spread = spread.reshape((count,) + spread.shape[2:])
        leaving = pick_leaving(send_early, [spread], rooms[0])
        earlies.append(lax.ppermute(leaving, "node", swap))
        extras.append(
            lax.cond(
                crowded[0] > 0,
                lambda x: lax.ppermute(x, "node", swap),
                jnp.zeros_like,
                spread,
            )
        )
        spreads.append(spread)
    leaving = pick_leaving(send_late, spreads, rooms[1])
    late = lax.ppermute(leaving, "node", swap)
    bounds = (count, count + rooms[0], count + rooms[0] + rooms[1])
    delivered = []
    for c in range(len(cuts)):
        picked = collect(
            early_source,
            crowded,
            spreads[c : c + 1],
            earlies[c : c + 1],
            extras[c : c + 1],
            None,
            (count, count + rooms[0], count + rooms[0]),
        )
        delivered.append(exchange(picked))
    picked = collect(late_source, crowded, spreads, earlies, extras, late, bounds)
    last = exchange(picked)
    return delivered, last


def product(left_real, left_imag, blocks):
    order = left_real.shape[1]
    right_real, right_imag = (
        jnp.concatenate([b[:, c].reshape(order, b.shape[-1]) for b in blocks], axis=1)
        for c in range(2)
    )
    stacked_left = jnp.concatenate([left_real, left_imag], axis=1)
    stacked_right = jnp.concatenate(
        [
            jnp.concatenate([right_real, right_imag], axis=1),
            jnp.concatenate([-right_imag, right_real], axis=1),
        ],
        axis=0,
    )
    return jnp.dot(
        stacked_left,
        stacked_right,
        precision=lax.Precision.HIGHEST,
        preferred_element_type=jnp.float32,
    )


def multiply_kernel(first_ref, left_ref, *refs):
    right_refs, out_ref, hold_ref, sems = refs[:-3], refs[-3], refs[-2], refs[-1]
    step = pl.program_id(0)
    width = out_ref.shape[-1]

    def fetch(k):
        return pltpu.make_async_copy(left_ref.at[first_ref[k]], hold_ref.at[k], sems.at[k])

    @pl.when(step == 0)
    def _():
        for k in range(hold_ref.shape[0]):
            fetch(k).start()

    fetch(step).wait()
    left = hold_ref[step]
    both = product(left[0], left[1], [ref[:, 0, 0] for ref in right_refs])
    out_ref[0, 0] = both[:, :width]
    out_ref[0, 1] = both[:, width:]


def multiply(left_index, lefts, rights, offset, number):
    group, _, _, _, rows, width = rights[0].shape
    order = lefts.shape[2]
    cols = width * len(rights)
    right_spec = pl.BlockSpec(
        (group, 1, 1, 2, rows, width), lambda k, index: (0, offset + k, 0, 0, 0, 0)
    )
    return pl.pallas_call(
        multiply_kernel,
        grid_spec=pltpu.PrefetchScalarGridSpec(
            num_scalar_prefetch=1,
            grid=(number,),
            in_specs=[HBM] + [right_spec] * len(rights),
            out_specs=pl.BlockSpec((1, 2, order, cols), lambda k, index: (k, 0, 0, 0)),
            scratch_shapes=[
                pltpu.VMEM((number, 2, order, order), jnp.float32),
                pltpu.SemaphoreType.DMA((number,)),
            ],
        ),
        out_shape=jax.ShapeDtypeStruct((number, 2, order, cols), jnp.float32),
        compiler_params=PARAMS,
        name="multiply",
    )(left_index, lefts, *rights)


def finish_kernel(target, sign, left_ref, right_ref, out_ref):
    step = pl.program_id(0)
    width = out_ref.shape[-1]

    @pl.when(step == 0)
    def _():
        out_ref[...] = jnp.zeros_like(out_ref)

    blocks = [right_ref[:, 0, c] for c in range(right_ref.shape[2])]
    both = product(left_ref[0, 0], left_ref[0, 1], blocks) * sign[step].astype(jnp.float32)
    row = target[step]
    out_ref[row, 0] += both[:, :width]
    out_ref[row, 1] += both[:, width:]


def finish(target, sign, lefts, right):
    group, seconds, parts, _, rows, width = right.shape
    order = lefts.shape[2]
    whole = (RES_COL, 2, order, width * parts)
    return pl.pallas_call(
        finish_kernel,
        grid_spec=pltpu.PrefetchScalarGridSpec(
            num_scalar_prefetch=2,
            grid=(seconds,),
            in_specs=[
                pl.BlockSpec((1, 2, order, order), lambda k, t, s: (k, 0, 0, 0)),
                pl.BlockSpec((group, 1, parts, 2, rows, width), lambda k, t, s: (0, k, 0, 0, 0, 0)),
            ],
            out_specs=pl.BlockSpec(whole, lambda k, t, s: (0, 0, 0, 0)),
        ),
        out_shape=jax.ShapeDtypeStruct(whole, jnp.float32),
        compiler_params=LARGE,
        name="finish",
    )(target, sign, lefts, right)


def all_columns(x):
    if lax.axis_size("pair") == 1:
        return x
    return lax.all_gather(x, "pair", axis=3, tiled=True)


def per_device(node_blocks, node_slot, pair_list, second_list, targets, spin_signs):
    devices = lax.axis_size("node")
    column = lax.axis_index("node")
    group = devices // 2
    node_col, _, _, local_width = node_blocks.shape
    pair_col = pair_list.shape[0] // devices
    second_col = second_list.shape[0] // devices
    width = min(LANES, local_width)
    cuts = [cut_rows(node_blocks, group, c, width) for c in range(local_width // width)]

    slots = node_slot[pair_list]
    second_slots = slots[second_list[:, 1]]
    early_ids = jnp.concatenate(
        [slots[:, 1].reshape(devices, pair_col), second_slots[:, 0].reshape(devices, second_col)],
        axis=1,
    )
    late_ids = second_slots[:, 1].reshape(devices, second_col)
    rights, lasts = fetch_items(cuts, early_ids, late_ids)

    own_slots = lax.dynamic_slice_in_dim(slots, column * pair_col, pair_col, 0)
    first_slot = own_slots[:, 0] - column * node_col
    own_seconds = lax.dynamic_slice_in_dim(second_list, column * second_col, second_col, 0)
    left_index = own_seconds[:, 0] - column * pair_col
    own_signs = lax.dynamic_slice_in_dim(spin_signs, column * second_col, second_col, 0)
    own_targets = lax.dynamic_slice_in_dim(targets, column * second_col, second_col, 0)
    own_targets = own_targets - column * RES_COL

    products = multiply(first_slot, all_columns(node_blocks), rights, 0, pair_col)
    longer = multiply(left_index, all_columns(products), rights, pair_col, second_col)
    return finish(own_targets, own_signs, all_columns(longer), lasts)


def solution(mesh):
    placed = (P(("cfg", "node"), None, None, "pair"), P(), P(), P(), P(), P())

    return jax.shard_map(
        per_device,
        mesh=mesh,
        in_specs=placed,
        out_specs=P(("cfg", "node"), None, None, "pair"),
        check_vma=False,
    )
```

```python
import functools

import jax
import jax.numpy as jnp
from jax import lax
from jax.experimental import pallas as pl
from jax.experimental.pallas import tpu as pltpu
from jax.sharding import PartitionSpec as P


RES_COL = 2
LANES = 128
CROSS_SHARE = 29 / 64
ANY = pl.BlockSpec(memory_space=pl.ANY)
HBM = pl.BlockSpec(memory_space=pltpu.HBM)
SMEM = pl.BlockSpec(memory_space=pltpu.SMEM)
VMEM = pl.BlockSpec(memory_space=pltpu.VMEM)
PARAMS = pltpu.CompilerParams(vmem_limit_bytes=24 * 1024 * 1024)
LARGE = pltpu.CompilerParams(vmem_limit_bytes=56 * 1024 * 1024)
CHAIN = pltpu.CompilerParams(vmem_limit_bytes=44 * 1024 * 1024)


def cut_kernel(in_ref, out_ref):
    rows = out_ref.shape[3]
    for j in range(out_ref.shape[0]):
        out_ref[j] = in_ref[:, :, j * rows : (j + 1) * rows, :]


def cut_rows(nodes, group, part, width):
    count, _, order, _ = nodes.shape
    rows = order // group
    steps = 4 if group % 4 == 0 else 1
    return pl.pallas_call(
        cut_kernel,
        grid=(steps,),
        in_specs=[pl.BlockSpec((count, 2, order // steps, width), lambda i: (0, 0, i, part))],
        out_specs=pl.BlockSpec((group // steps, count, 2, rows, width), lambda i: (i, 0, 0, 0, 0)),
        out_shape=jax.ShapeDtypeStruct((group, count, 2, rows, width), jnp.float32),
        name="cut_rows",
    )(nodes)


def plan_kernel(room, half_ref, ids_ref, send_ref, source_ref, crowded_ref, place_ref):
    half = half_ref[0]
    count = send_ref.shape[0]
    asked = source_ref.shape[0]

    def clear(i, carry):
        place_ref[i] = -1
        return carry

    def empty(i, carry):
        send_ref[i] = 0
        return carry

    lax.fori_loop(0, 2 * count, clear, 0, unroll=8)
    lax.fori_loop(0, count, empty, 0, unroll=8)

    def visit_other(q, found):
        item = ids_ref[(1 - half) * asked + q]
        here = item - half * count
        fresh = (here >= 0) & (here < count) & (place_ref[item] < 0)

        @pl.when(fresh)
        def _():
            place_ref[item] = 0
            send_ref[found] = here

        return found + fresh.astype(jnp.int32)

    def visit_own(q, found):
        item = ids_ref[half * asked + q]
        here = item - half * count
        inside = (here >= 0) & (here < count)
        known = place_ref[item]
        fresh = jnp.logical_not(inside) & (known < 0)
        there = count + room + item - (1 - half) * count
        place = jnp.where(known < 0, jnp.where(found < room, count + found, there), known)

        @pl.when(fresh)
        def _():
            place_ref[item] = place

        source_ref[q] = jnp.where(inside, here, place)
        return found + fresh.astype(jnp.int32)

    sent = lax.fori_loop(0, asked, visit_other, jnp.int32(0))
    received = lax.fori_loop(0, asked, visit_own, jnp.int32(0))
    crowded_ref[0] = (jnp.maximum(sent, received) > room).astype(jnp.int32)


def make_plan(half, ids, count, room):
    asked = ids.shape[0] // 2
    return pl.pallas_call(
        functools.partial(plan_kernel, room),
        in_specs=[SMEM] * 2,
        out_specs=[SMEM] * 3,
        out_shape=[
            jax.ShapeDtypeStruct((count,), jnp.int32),
            jax.ShapeDtypeStruct((asked,), jnp.int32),
            jax.ShapeDtypeStruct((1,), jnp.int32),
        ],
        scratch_shapes=[pltpu.SMEM((2 * count,), jnp.int32)],
        compiler_params=PARAMS,
        name="make_plan",
    )(half, ids)


def leave_kernel(send_ref, spread_ref, out_ref):
    def copy(i, carry):
        out_ref[i] = spread_ref[send_ref[i]]
        return carry

    lax.fori_loop(0, out_ref.shape[0], copy, 0, unroll=8)


def pick_leaving(send, spread, room):
    return pl.pallas_call(
        leave_kernel,
        in_specs=[SMEM, VMEM],
        out_specs=VMEM,
        out_shape=jax.ShapeDtypeStruct((room,) + spread.shape[1:], jnp.float32),
        compiler_params=PARAMS,
        name="pick_leaving",
    )(send, spread)


def collect_kernel(source_ref, crowded_ref, spread_ref, arrived_ref, extra_ref, out_ref, sem):
    count, room = spread_ref.shape[0], arrived_ref.shape[0]

    def copy(q, carry):
        source = source_ref[q]
        near = jnp.minimum(source, count - 1)
        far = jnp.clip(source - count, 0, room - 1)
        out_ref[q] = jnp.where(source < count, spread_ref[near], arrived_ref[far])
        return carry

    lax.fori_loop(0, out_ref.shape[0], copy, 0, unroll=8)

    @pl.when(crowded_ref[0] > 0)
    def _():
        def fetch(q, carry):
            source = source_ref[q] - (count + room)

            @pl.when(source >= 0)
            def _():
                slow = pltpu.make_async_copy(extra_ref.at[source], out_ref.at[q], sem)
                slow.start()
                slow.wait()

            return carry

        lax.fori_loop(0, out_ref.shape[0], fetch, 0)


def collect(source, crowded, spread, arrived, extra):
    return pl.pallas_call(
        collect_kernel,
        in_specs=[SMEM, SMEM, VMEM, VMEM, ANY],
        out_specs=VMEM,
        out_shape=jax.ShapeDtypeStruct((source.shape[0],) + spread.shape[1:], jnp.float32),
        scratch_shapes=[pltpu.SemaphoreType.DMA],
        compiler_params=PARAMS,
        name="collect",
    )(source, crowded, spread, arrived, extra)


def fetch_items(cuts, ids):
    devices = lax.axis_size("node")
    group = devices // 2
    half = (lax.axis_index("node") // group).astype(jnp.int32).reshape(1)
    halves = [[h * group + i for i in range(group)] for h in range(2)]
    swap = [(i, (i + group) % devices) for i in range(devices)]
    count = group * cuts[0].shape[1]
    room = min(count, max(8, int(count * CROSS_SHARE)))
    send, source, crowded = make_plan(half, ids.reshape(-1), count, room)

    def exchange(x):
        return lax.all_to_all(x, "node", 0, 0, axis_index_groups=halves, tiled=True)

    delivered = []
    for cut in cuts:
        spread = exchange(cut)
        spread = spread.reshape((count,) + spread.shape[2:])
        leaving = pick_leaving(send, spread, room)
        arrived = lax.ppermute(leaving, "node", swap)
        extra = lax.cond(
            crowded[0] > 0,
            lambda x: lax.ppermute(x, "node", swap),
            jnp.zeros_like,
            spread,
        )
        picked = collect(source, crowded, spread, arrived, extra)
        picked = picked.reshape((group, ids.shape[1]) + picked.shape[1:])
        delivered.append(exchange(picked))
    return delivered


def halves_of(x):
    high = x.astype(jnp.bfloat16)
    return high, (x - high.astype(jnp.float32)).astype(jnp.bfloat16)


def stacked(blocks):
    order = blocks[0].shape[0] * blocks[0].shape[2]
    real, imag = (
        jnp.concatenate([b[:, c].reshape(order, b.shape[-1]) for b in blocks], axis=1)
        for c in range(2)
    )
    pairs = zip(halves_of(real), halves_of(imag))
    return [
        jnp.concatenate([jnp.concatenate([r, i], axis=1), jnp.concatenate([-i, r], axis=1)], axis=0)
        for r, i in pairs
    ]


def product(left, blocks):
    left_high, left_low = halves_of(left)
    right_high, right_low = stacked(blocks)
    dot = functools.partial(jnp.dot, preferred_element_type=jnp.float32)
    small = dot(left_high, right_low) + dot(left_low, right_high)
    return dot(left_high, right_high) + small


def wide(ref):
    return jnp.concatenate([ref[0, 0], ref[0, 1]], axis=1)


def triple_spec(array):
    group, _, _, rows, width = array.shape
    return pl.BlockSpec((group, 3, 2, rows, width), lambda k, *scalars: (0, k, 0, 0, 0))


def multiply_kernel(which, index_ref, left_ref, *refs):
    right_refs, out_ref = refs[:-1], refs[-1]
    both = product(wide(left_ref), [ref[:, which] for ref in right_refs])
    width = out_ref.shape[-1]
    out_ref[0, 0] = both[:, :width]
    out_ref[0, 1] = both[:, width:]


def multiply(left_index, lefts, rights, which):
    order = lefts.shape[2]
    number = left_index.shape[0]
    cols = sum(right.shape[-1] for right in rights)
    return pl.pallas_call(
        functools.partial(multiply_kernel, which),
        grid_spec=pltpu.PrefetchScalarGridSpec(
            num_scalar_prefetch=1,
            grid=(number,),
            in_specs=[
                pl.BlockSpec((1, 2, order, order), lambda k, index: (index[k], 0, 0, 0)),
                *[triple_spec(right) for right in rights],
            ],
            out_specs=pl.BlockSpec((1, 2, order, cols), lambda k, index: (k, 0, 0, 0)),
        ),
        out_shape=jax.ShapeDtypeStruct((number, 2, order, cols), jnp.float32),
        compiler_params=CHAIN,
        name="multiply",
    )(left_index, lefts, *rights)


def add_result(step, target, sign, both, out_ref):
    width = out_ref.shape[-1]

    @pl.when(step == 0)
    def _():
        out_ref[...] = jnp.zeros_like(out_ref)

    both = both * sign[step].astype(jnp.float32)
    row = target[step]
    out_ref[row, 0] += both[:, :width]
    out_ref[row, 1] += both[:, width:]


def finish_kernel(target, sign, left_ref, *refs):
    right_refs, out_ref = refs[:-1], refs[-1]
    both = product(wide(left_ref), [ref[:, 2] for ref in right_refs])
    add_result(pl.program_id(0), target, sign, both, out_ref)


def finish(target, sign, lefts, rights):
    order = lefts.shape[2]
    whole = (RES_COL, 2, order, sum(right.shape[-1] for right in rights))
    return pl.pallas_call(
        finish_kernel,
        grid_spec=pltpu.PrefetchScalarGridSpec(
            num_scalar_prefetch=2,
            grid=(lefts.shape[0],),
            in_specs=[
                pl.BlockSpec((1, 2, order, order), lambda k, t, s: (k, 0, 0, 0)),
                *[triple_spec(right) for right in rights],
            ],
            out_specs=pl.BlockSpec(whole, lambda k, t, s: (0, 0, 0, 0)),
        ),
        out_shape=jax.ShapeDtypeStruct(whole, jnp.float32),
        compiler_params=LARGE,
        name="finish",
    )(target, sign, lefts, *rights)


def chain_kernel(slot, target, sign, node_ref, start_ref, *refs):
    right_refs, out_ref = refs[:-1], refs[-1]
    last = product(wide(node_ref), [right_refs[-1][:, 0]])
    width = last.shape[1] // 2
    first = jnp.concatenate(
        [start_ref[0, 0], last[:, :width], start_ref[0, 1], last[:, width:]], axis=1
    )
    longer = product(first, [ref[:, 1] for ref in right_refs])
    both = product(longer, [ref[:, 2] for ref in right_refs])
    add_result(pl.program_id(0), target, sign, both, out_ref)


def chain(slot, target, sign, nodes, start, rights):
    order = nodes.shape[2]
    whole = (RES_COL, 2, order, order)
    early = start.shape[-1]
    return pl.pallas_call(
        chain_kernel,
        grid_spec=pltpu.PrefetchScalarGridSpec(
            num_scalar_prefetch=3,
            grid=(slot.shape[0],),
            in_specs=[
                pl.BlockSpec((1, 2, order, order), lambda k, slot, t, s: (slot[k], 0, 0, 0)),
                pl.BlockSpec((1, 2, order, early), lambda k, slot, t, s: (k, 0, 0, 0)),
                *[triple_spec(right) for right in rights],
            ],
            out_specs=pl.BlockSpec(whole, lambda k, slot, t, s: (0, 0, 0, 0)),
        ),
        out_shape=jax.ShapeDtypeStruct(whole, jnp.float32),
        compiler_params=CHAIN,
        name="chain",
    )(slot, target, sign, nodes, start, *rights)


def all_columns(x):
    if lax.axis_size("pair") == 1:
        return x
    return lax.all_gather(x, "pair", axis=3, tiled=True)


def per_device(node_blocks, node_slot, pair_list, second_list, targets, spin_signs):
    devices = lax.axis_size("node")
    column = lax.axis_index("node")
    group = devices // 2
    node_col, _, _, local_width = node_blocks.shape
    second_col = second_list.shape[0] // devices
    width = min(LANES, local_width)
    cuts = [cut_rows(node_blocks, group, c, width) for c in range(local_width // width)]

    slots = node_slot[pair_list]
    slots = slots[second_list].reshape(devices, second_col, 4)
    rights = fetch_items(cuts, slots[:, :, 1:].reshape(devices, second_col * 3))

    own_slots = lax.dynamic_index_in_dim(slots[:, :, 0], column, 0, keepdims=False)
    own_slots = own_slots - column * node_col
    own_signs = lax.dynamic_slice_in_dim(spin_signs, column * second_col, second_col, 0)
    own_targets = lax.dynamic_slice_in_dim(targets, column * second_col, second_col, 0)
    own_targets = own_targets - column * RES_COL

    if lax.axis_size("pair") == 1 and len(rights) > 1:
        start = multiply(own_slots, node_blocks, rights[:-1], 0)
        return chain(own_slots, own_targets, own_signs, node_blocks, start, rights)
    same = jnp.arange(second_col, dtype=jnp.int32)
    products = multiply(own_slots, all_columns(node_blocks), rights, 0)
    longer = multiply(same, all_columns(products), rights, 1)
    return finish(own_targets, own_signs, all_columns(longer), rights)


def solution(mesh):
    placed = (P(("cfg", "node"), None, None, "pair"), P(), P(), P(), P(), P())

    return jax.shard_map(
        per_device,
        mesh=mesh,
        in_specs=placed,
        out_specs=P(("cfg", "node"), None, None, "pair"),
        check_vma=False,
    )
```

```python
import functools

import jax
import jax.numpy as jnp
from jax import lax
from jax.experimental import pallas as pl
from jax.experimental.pallas import tpu as pltpu
from jax.sharding import PartitionSpec as P


RES_COL = 2
LANES = 128
CROSS_SHARE = 17 / 32
NEAR_SHARE = 13 / 32
PIECES = 2
PLANES = 4
SMEM = pl.BlockSpec(memory_space=pltpu.SMEM)
VMEM = pl.BlockSpec(memory_space=pltpu.VMEM)
PARAMS = pltpu.CompilerParams(vmem_limit_bytes=24 * 1024 * 1024)
CHAIN = pltpu.CompilerParams(vmem_limit_bytes=44 * 1024 * 1024)


def cut_kernel(in_ref, out_ref):
    rows = out_ref.shape[3]
    for j in range(out_ref.shape[0]):
        out_ref[j] = in_ref[:, :, j * rows : (j + 1) * rows, :]


def cut_rows(nodes, group, part, width):
    count, _, order, _ = nodes.shape
    rows = order // group
    steps = 4 if group % 4 == 0 else 1
    return pl.pallas_call(
        cut_kernel,
        grid=(steps,),
        in_specs=[pl.BlockSpec((count, 2, order // steps, width), lambda i: (0, 0, i, part))],
        out_specs=pl.BlockSpec((group // steps, count, 2, rows, width), lambda i: (i, 0, 0, 0, 0)),
        out_shape=jax.ShapeDtypeStruct((group, count, 2, rows, width), jnp.float32),
        name="cut_rows",
    )(nodes)


def plan_kernel(plane_ref, ids_ref, cross_ref, near_ref, far_ref, source_ref, mark_ref, place_ref):
    plane = plane_ref[0]
    asked = source_ref.shape[0]
    cross_room, near_room, far_room = cross_ref.shape[0], near_ref.shape[0], far_ref.shape[0]
    total = mark_ref.shape[0]
    count = total // PLANES
    half = plane // 2
    partner = plane ^ 1

    def clear(i, carry):
        mark_ref[i] = -1
        place_ref[i] = -1
        return carry

    lax.fori_loop(0, total, clear, 0, unroll=8)
    for ref in (cross_ref, near_ref, far_ref):

        def empty(i, carry, ref=ref):
            ref[i] = 0
            return carry

        lax.fori_loop(0, ref.shape[0], empty, 0)

    def enter(fresh, marks, item, found, room, ref, value):
        @pl.when(fresh)
        def _():
            marks[item] = found

        @pl.when(fresh & (found < room))
        def _():
            ref[found] = value

        return found + fresh.astype(jnp.int32)

    def to_other_half(q, found):
        item = ids_ref[(1 - half) * 2 * asked + q]
        fresh = (item // count == plane) & (mark_ref[item] < 0)
        return enter(fresh, mark_ref, item, found, cross_room, cross_ref, item - plane * count)

    lax.fori_loop(0, 2 * asked, to_other_half, jnp.int32(0))

    def from_other_half(q, found):
        item = ids_ref[half * 2 * asked + q]
        fresh = (item // count == (plane ^ 2)) & (place_ref[item] < 0)

        @pl.when(fresh)
        def _():
            place_ref[item] = found

        return found + fresh.astype(jnp.int32)

    lax.fori_loop(0, 2 * asked, from_other_half, jnp.int32(0))

    def clear_marks(i, carry):
        mark_ref[i] = -1
        return carry

    lax.fori_loop(0, total, clear_marks, 0, unroll=8)

    def to_partner(q, founds):
        near, far = founds
        item = ids_ref[partner * asked + q]
        owner = item // count
        fresh = mark_ref[item] < 0
        near = enter(
            fresh & (owner == plane), mark_ref, item, near, near_room, near_ref, item - plane * count
        )
        crossed = jnp.clip(place_ref[item], 0, cross_room - 1)
        far = enter(
            fresh & (owner == (plane ^ 2)), mark_ref, item, far, far_room, far_ref, crossed
        )
        return near, far

    lax.fori_loop(0, asked, to_partner, (jnp.int32(0), jnp.int32(0)))
    lax.fori_loop(0, total, clear_marks, 0, unroll=8)

    def own(q, founds):
        near, far = founds
        item = ids_ref[plane * asked + q]
        owner = item // count
        known = mark_ref[item]
        from_near = owner == partner
        from_far = owner == (plane ^ 3)
        found = jnp.where(from_near, near, far)
        fresh = (known < 0) & (from_near | from_far)

        @pl.when(fresh)
        def _():
            mark_ref[item] = found

        place = jnp.where(known < 0, found, known)
        source = jnp.where(
            owner == plane,
            item - plane * count,
            jnp.where(
                owner == (plane ^ 2),
                count + place_ref[item],
                count + cross_room + place + jnp.where(from_near, 0, near_room),
            ),
        )
        source_ref[q] = source
        step = fresh.astype(jnp.int32)
        return near + jnp.where(from_near, step, 0), far + jnp.where(from_far, step, 0)

    lax.fori_loop(0, asked, own, (jnp.int32(0), jnp.int32(0)))


def make_plan(plane, ids, count, rooms):
    asked = ids.shape[0] // PLANES
    return pl.pallas_call(
        plan_kernel,
        in_specs=[SMEM] * 2,
        out_specs=[SMEM] * 4,
        out_shape=[jax.ShapeDtypeStruct((n,), jnp.int32) for n in (*rooms, asked)],
        scratch_shapes=[pltpu.SMEM((PLANES * count,), jnp.int32)] * 2,
        compiler_params=PARAMS,
        name="make_plan",
    )(plane, ids)


def is_crowded(ids, count, rooms):
    items = jnp.arange(PLANES * count, dtype=jnp.int32)
    wants = (ids.reshape(PLANES, -1, 1) == items).any(axis=1)
    halves = wants.reshape(2, 2, PLANES * count).any(axis=1)
    crowded = jnp.bool_(False)
    for plane in range(PLANES):
        cross = halves[1 - plane // 2, plane * count : (plane + 1) * count]
        crowded |= jnp.sum(cross.astype(jnp.int32)) > rooms[0]
        for step, room in ((1, rooms[1]), (3, rooms[2])):
            other = plane ^ step
            wanted = wants[plane, other * count : (other + 1) * count]
            crowded |= jnp.sum(wanted.astype(jnp.int32)) > room
    return crowded


def leave_kernel(cross_ids, near_ids, spread_ref, *refs):
    cross_refs, near_ref = refs[:-1], refs[-1]
    rows = cross_refs[0].shape[2]

    def copy(i, carry):
        item = spread_ref[cross_ids[i]]
        for r, ref in enumerate(cross_refs):
            ref[i] = item[:, r * rows : (r + 1) * rows]
        return carry

    lax.fori_loop(0, cross_refs[0].shape[0], copy, 0, unroll=4)

    def copy_near(i, carry):
        near_ref[i] = spread_ref[near_ids[i]]
        return carry

    lax.fori_loop(0, near_ref.shape[0], copy_near, 0, unroll=4)


def pick_leaving(cross, near, spread):
    _, _, rows, width = spread.shape
    piece = (cross.shape[0], 2, rows // PIECES, width)
    shapes = [piece] * PIECES + [(near.shape[0],) + spread.shape[1:]]
    return pl.pallas_call(
        leave_kernel,
        in_specs=[SMEM, SMEM, VMEM],
        out_specs=[VMEM] * (PIECES + 1),
        out_shape=[jax.ShapeDtypeStruct(shape, jnp.float32) for shape in shapes],
        compiler_params=PARAMS,
        name="pick_leaving",
    )(cross, near, spread)


def pass_kernel(far_ids, crossed_ref, out_ref):
    def copy(i, carry):
        out_ref[i] = crossed_ref[far_ids[i]]
        return carry

    lax.fori_loop(0, out_ref.shape[0], copy, 0, unroll=4)


def pick_passing(far, crossed):
    return pl.pallas_call(
        pass_kernel,
        in_specs=[SMEM, VMEM],
        out_specs=VMEM,
        out_shape=jax.ShapeDtypeStruct((far.shape[0],) + crossed.shape[1:], jnp.float32),
        compiler_params=PARAMS,
        name="pick_passing",
    )(far, crossed)


def collect_kernel(first_row, source_ref, spread_ref, crossed_ref, near_ref, far_ref, out_ref):
    rows = out_ref.shape[2]
    piece = slice(first_row, first_row + rows)
    bases = [0]
    for ref in (spread_ref, crossed_ref, near_ref):
        bases.append(bases[-1] + ref.shape[0])

    def copy(q, carry):
        source = source_ref[q]

        def index(place, ref):
            return jnp.clip(source - bases[place], 0, ref.shape[0] - 1)

        value = spread_ref[index(0, spread_ref), :, piece, :]
        value = jnp.where(source < bases[1], value, crossed_ref[index(1, crossed_ref)])
        value = jnp.where(source < bases[2], value, near_ref[index(2, near_ref), :, piece, :])
        out_ref[q] = jnp.where(source < bases[3], value, far_ref[index(3, far_ref)])
        return carry

    lax.fori_loop(0, out_ref.shape[0], copy, 0, unroll=4)


def collect(source, spread, crossed, near, far, piece):
    rows = crossed.shape[2]
    return pl.pallas_call(
        functools.partial(collect_kernel, piece * rows),
        in_specs=[SMEM] + [VMEM] * 4,
        out_specs=VMEM,
        out_shape=jax.ShapeDtypeStruct((source.shape[0],) + crossed.shape[1:], jnp.float32),
        compiler_params=PARAMS,
        name="collect",
    )(source, spread, crossed, near, far)


def fetch_items(cuts, ids):
    devices = lax.axis_size("node")
    group = devices // PLANES
    plane = (lax.axis_index("node") // group).astype(jnp.int32)
    planes = [[p * group + i for i in range(group)] for p in range(PLANES)]
    swap = [(i, (i // group ^ 2) * group + i % group) for i in range(devices)]
    mate = [(i, (i // group ^ 1) * group + i % group) for i in range(devices)]
    count = group * cuts[0].shape[1]
    rooms = tuple(
        min(count, max(8, int(count * share))) for share in (CROSS_SHARE, NEAR_SHARE, NEAR_SHARE)
    )
    flat = ids.reshape(-1)
    cross, near, far, source = make_plan(plane.reshape(1), flat, count, rooms)
    crowded = is_crowded(flat, count, rooms)
    own_ids = lax.dynamic_index_in_dim(ids.reshape(PLANES, -1), plane, 0, keepdims=False)

    def exchange(x):
        return lax.all_to_all(x, "node", 0, 0, axis_index_groups=planes, tiled=True)

    def gather_all(spread, crossed, near_by, far_by, piece):
        rows = crossed.shape[2]
        here = spread[:, :, piece * rows : (piece + 1) * rows]
        crossing = lax.ppermute(here, "node", swap)
        both = jnp.concatenate([here, crossing])
        every = jnp.concatenate([both, lax.ppermute(both, "node", mate)])
        order = own_ids // count ^ plane
        index = jnp.array([0, 2, 1, 3])[order] * count + own_ids % count
        return jnp.take(every, index, axis=0)

    delivered = []
    for cut in cuts:
        spread = exchange(cut)
        spread = spread.reshape((count,) + spread.shape[2:])
        *leaving, staying = pick_leaving(cross, near, spread)
        crossed = []
        for r in range(PIECES):
            crossed.append(lax.ppermute(leaving[r], "node", swap))
        near_by = lax.ppermute(staying, "node", mate)
        pieces = []
        for r in range(PIECES):
            passing = pick_passing(far, crossed[r])
            far_by = lax.ppermute(passing, "node", mate)
            picked = lax.cond(
                crowded,
                functools.partial(gather_all, piece=r),
                functools.partial(collect, source, piece=r),
                spread,
                crossed[r],
                near_by,
                far_by,
            )
            picked = picked.reshape((group, ids.shape[1]) + picked.shape[1:])
            pieces.append(exchange(picked))
        delivered.append(pieces)
    return delivered


def halves_of(x):
    high = x.astype(jnp.bfloat16)
    return high, (x - high.astype(jnp.float32)).astype(jnp.bfloat16)


def joined(pieces):
    rows = jnp.concatenate([p[:, None] for p in pieces], axis=1)
    return rows.reshape(-1, rows.shape[-1])


def stacked(blocks):
    real, imag = (
        jnp.concatenate([joined([piece[:, c] for piece in block]) for block in blocks], axis=1)
        for c in range(2)
    )
    pairs = zip(halves_of(real), halves_of(imag))
    return [
        jnp.concatenate([jnp.concatenate([r, i], axis=1), jnp.concatenate([-i, r], axis=1)], axis=0)
        for r, i in pairs
    ]


def product(left, blocks):
    left_high, left_low = halves_of(left)
    right_high, right_low = stacked(blocks)
    dot = functools.partial(jnp.dot, preferred_element_type=jnp.float32)
    small = dot(left_high, right_low) + dot(left_low, right_high)
    return dot(left_high, right_high) + small


def columns_of(rights):
    return sum(right.shape[-1] for right in rights) // PIECES


def wide(ref):
    return jnp.concatenate([ref[0, 0], ref[0, 1]], axis=1)


def triple_spec(array):
    group, _, _, rows, width = array.shape
    return pl.BlockSpec((group, 3, 2, rows, width), lambda k, *scalars: (0, k, 0, 0, 0))


def items(refs, which):
    pieces = [ref[:, which] for ref in refs]
    return [pieces[i : i + PIECES] for i in range(0, len(pieces), PIECES)]


def multiply_kernel(which, index_ref, left_ref, *refs):
    right_refs, out_ref = refs[:-1], refs[-1]
    both = product(wide(left_ref), items(right_refs, which))
    width = out_ref.shape[-1]
    out_ref[0, 0] = both[:, :width]
    out_ref[0, 1] = both[:, width:]


def multiply(left_index, lefts, rights, which):
    order = lefts.shape[2]
    number = left_index.shape[0]
    cols = columns_of(rights)
    return pl.pallas_call(
        functools.partial(multiply_kernel, which),
        grid_spec=pltpu.PrefetchScalarGridSpec(
            num_scalar_prefetch=1,
            grid=(number,),
            in_specs=[
                pl.BlockSpec((1, 2, order, order), lambda k, index: (index[k], 0, 0, 0)),
                *[triple_spec(right) for right in rights],
            ],
            out_specs=pl.BlockSpec((1, 2, order, cols), lambda k, index: (k, 0, 0, 0)),
        ),
        out_shape=jax.ShapeDtypeStruct((number, 2, order, cols), jnp.float32),
        compiler_params=CHAIN,
        name="multiply",
    )(left_index, lefts, *rights)


def add_result(step, target, sign, both, out_ref):
    width = out_ref.shape[-1]

    @pl.when(step == 0)
    def _():
        out_ref[...] = jnp.zeros_like(out_ref)

    both = both * sign[step].astype(jnp.float32)
    row = target[step]
    out_ref[row, 0] += both[:, :width]
    out_ref[row, 1] += both[:, width:]


def finish_kernel(target, sign, left_ref, *refs):
    right_refs, out_ref = refs[:-1], refs[-1]
    both = product(wide(left_ref), items(right_refs, 2))
    add_result(pl.program_id(0), target, sign, both, out_ref)


def finish(target, sign, lefts, rights):
    order = lefts.shape[2]
    whole = (RES_COL, 2, order, columns_of(rights))
    return pl.pallas_call(
        finish_kernel,
        grid_spec=pltpu.PrefetchScalarGridSpec(
            num_scalar_prefetch=2,
            grid=(lefts.shape[0],),
            in_specs=[
                pl.BlockSpec((1, 2, order, order), lambda k, t, s: (k, 0, 0, 0)),
                *[triple_spec(right) for right in rights],
            ],
            out_specs=pl.BlockSpec(whole, lambda k, t, s: (0, 0, 0, 0)),
        ),
        out_shape=jax.ShapeDtypeStruct(whole, jnp.float32),
        compiler_params=CHAIN,
        name="finish",
    )(target, sign, lefts, *rights)


def chain_kernel(slot, target, sign, node_ref, start_ref, *refs):
    right_refs, out_ref = refs[:-1], refs[-1]
    last = product(wide(node_ref), items(right_refs[-PIECES:], 0))
    width = last.shape[1] // 2
    first = jnp.concatenate(
        [start_ref[0, 0], last[:, :width], start_ref[0, 1], last[:, width:]], axis=1
    )
    longer = product(first, items(right_refs, 1))
    both = product(longer, items(right_refs, 2))
    add_result(pl.program_id(0), target, sign, both, out_ref)


def chain(slot, target, sign, nodes, start, rights):
    order = nodes.shape[2]
    whole = (RES_COL, 2, order, order)
    early = start.shape[-1]
    return pl.pallas_call(
        chain_kernel,
        grid_spec=pltpu.PrefetchScalarGridSpec(
            num_scalar_prefetch=3,
            grid=(slot.shape[0],),
            in_specs=[
                pl.BlockSpec((1, 2, order, order), lambda k, slot, t, s: (slot[k], 0, 0, 0)),
                pl.BlockSpec((1, 2, order, early), lambda k, slot, t, s: (k, 0, 0, 0)),
                *[triple_spec(right) for right in rights],
            ],
            out_specs=pl.BlockSpec(whole, lambda k, slot, t, s: (0, 0, 0, 0)),
        ),
        out_shape=jax.ShapeDtypeStruct(whole, jnp.float32),
        compiler_params=CHAIN,
        name="chain",
    )(slot, target, sign, nodes, start, *rights)


def all_columns(x):
    if lax.axis_size("pair") == 1:
        return x
    return lax.all_gather(x, "pair", axis=3, tiled=True)


def per_device(node_blocks, node_slot, pair_list, second_list, targets, spin_signs):
    devices = lax.axis_size("node")
    column = lax.axis_index("node")
    group = devices // PLANES
    node_col, _, _, local_width = node_blocks.shape
    second_col = second_list.shape[0] // devices
    width = min(LANES, local_width)
    cuts = [cut_rows(node_blocks, group, c, width) for c in range(local_width // width)]

    slots = node_slot[pair_list]
    slots = slots[second_list].reshape(devices, second_col, 4)
    rights = fetch_items(cuts, slots[:, :, 1:].reshape(devices, second_col * 3))

    own_slots = lax.dynamic_index_in_dim(slots[:, :, 0], column, 0, keepdims=False)
    own_slots = own_slots - column * node_col
    own_signs = lax.dynamic_slice_in_dim(spin_signs, column * second_col, second_col, 0)
    own_targets = lax.dynamic_slice_in_dim(targets, column * second_col, second_col, 0)
    own_targets = own_targets - column * RES_COL

    parts = len(rights)
    rights = [piece for pieces in rights for piece in pieces]
    if lax.axis_size("pair") == 1 and parts > 1:
        start = multiply(own_slots, node_blocks, rights[:-PIECES], 0)
        return chain(own_slots, own_targets, own_signs, node_blocks, start, rights)
    same = jnp.arange(second_col, dtype=jnp.int32)
    products = multiply(own_slots, all_columns(node_blocks), rights, 0)
    longer = multiply(same, all_columns(products), rights, 1)
    return finish(own_targets, own_signs, all_columns(longer), rights)


def solution(mesh):
    placed = (P(("cfg", "node"), None, None, "pair"), P(), P(), P(), P(), P())

    return jax.shard_map(
        per_device,
        mesh=mesh,
        in_specs=placed,
        out_specs=P(("cfg", "node"), None, None, "pair"),
        check_vma=False,
    )
```

```python
import functools

import jax
import jax.numpy as jnp
from jax import lax
from jax.experimental import pallas as pl
from jax.experimental.pallas import tpu as pltpu
from jax.sharding import PartitionSpec as P


RES_COL = 2
LANES = 128
CROSS_SHARE = 17 / 32
NEAR_SHARE = 13 / 32
PIECES = 2
PLANES = 4
SMEM = pl.BlockSpec(memory_space=pltpu.SMEM)
VMEM = pl.BlockSpec(memory_space=pltpu.VMEM)
PARAMS = pltpu.CompilerParams(vmem_limit_bytes=24 * 1024 * 1024)
COLLECT = PARAMS
CHAIN = pltpu.CompilerParams(vmem_limit_bytes=44 * 1024 * 1024)


def cut_kernel(in_ref, out_ref):
    rows = out_ref.shape[3]
    for j in range(out_ref.shape[0]):
        out_ref[j] = in_ref[:, :, j * rows : (j + 1) * rows, :]


def cut_rows(nodes, group, part, width):
    count, _, order, _ = nodes.shape
    rows = order // group
    steps = 4 if group % 4 == 0 else 1
    return pl.pallas_call(
        cut_kernel,
        grid=(steps,),
        in_specs=[pl.BlockSpec((count, 2, order // steps, width), lambda i: (0, 0, i, part))],
        out_specs=pl.BlockSpec((group // steps, count, 2, rows, width), lambda i: (i, 0, 0, 0, 0)),
        out_shape=jax.ShapeDtypeStruct((group, count, 2, rows, width), jnp.float32),
        name="cut_rows",
    )(nodes)


def plan_kernel(plane_ref, ids_ref, cross_ref, near_ref, far_ref, source_ref, mark_ref, place_ref):
    plane = plane_ref[0]
    asked = source_ref.shape[0]
    cross_room, near_room, far_room = cross_ref.shape[0], near_ref.shape[0], far_ref.shape[0]
    total = mark_ref.shape[0]
    count = total // PLANES
    half = plane // 2
    partner = plane ^ 1

    def clear(i, carry):
        mark_ref[i] = -1
        place_ref[i] = -1
        return carry

    lax.fori_loop(0, total, clear, 0, unroll=8)
    for ref in (cross_ref, near_ref, far_ref):

        def empty(i, carry, ref=ref):
            ref[i] = 0
            return carry

        lax.fori_loop(0, ref.shape[0], empty, 0)

    def enter(fresh, marks, item, found, room, ref, value):
        @pl.when(fresh)
        def _():
            marks[item] = found

        @pl.when(fresh & (found < room))
        def _():
            ref[found] = value

        return found + fresh.astype(jnp.int32)

    def to_other_half(q, found):
        item = ids_ref[(1 - half) * 2 * asked + q]
        fresh = (item // count == plane) & (mark_ref[item] < 0)
        return enter(fresh, mark_ref, item, found, cross_room, cross_ref, item - plane * count)

    lax.fori_loop(0, 2 * asked, to_other_half, jnp.int32(0))

    def from_other_half(q, found):
        item = ids_ref[half * 2 * asked + q]
        fresh = (item // count == (plane ^ 2)) & (place_ref[item] < 0)

        @pl.when(fresh)
        def _():
            place_ref[item] = found

        return found + fresh.astype(jnp.int32)

    lax.fori_loop(0, 2 * asked, from_other_half, jnp.int32(0))

    def clear_marks(i, carry):
        mark_ref[i] = -1
        return carry

    lax.fori_loop(0, total, clear_marks, 0, unroll=8)

    def to_partner(q, founds):
        near, far = founds
        item = ids_ref[partner * asked + q]
        owner = item // count
        fresh = mark_ref[item] < 0
        near = enter(
            fresh & (owner == plane), mark_ref, item, near, near_room, near_ref, item - plane * count
        )
        crossed = jnp.clip(place_ref[item], 0, cross_room - 1)
        far = enter(
            fresh & (owner == (plane ^ 2)), mark_ref, item, far, far_room, far_ref, crossed
        )
        return near, far

    lax.fori_loop(0, asked, to_partner, (jnp.int32(0), jnp.int32(0)))
    lax.fori_loop(0, total, clear_marks, 0, unroll=8)

    def own(q, founds):
        near, far = founds
        item = ids_ref[plane * asked + q]
        owner = item // count
        known = mark_ref[item]
        from_near = owner == partner
        from_far = owner == (plane ^ 3)
        found = jnp.where(from_near, near, far)
        fresh = (known < 0) & (from_near | from_far)

        @pl.when(fresh)
        def _():
            mark_ref[item] = found

        place = jnp.where(known < 0, found, known)
        source = jnp.where(
            owner == plane,
            item - plane * count,
            jnp.where(
                owner == (plane ^ 2),
                count + place_ref[item],
                count + cross_room + place + jnp.where(from_near, 0, near_room),
            ),
        )
        source_ref[q] = source
        step = fresh.astype(jnp.int32)
        return near + jnp.where(from_near, step, 0), far + jnp.where(from_far, step, 0)

    lax.fori_loop(0, asked, own, (jnp.int32(0), jnp.int32(0)))


def make_plan(plane, ids, count, rooms):
    asked = ids.shape[0] // PLANES
    return pl.pallas_call(
        plan_kernel,
        in_specs=[SMEM] * 2,
        out_specs=[SMEM] * 4,
        out_shape=[jax.ShapeDtypeStruct((n,), jnp.int32) for n in (*rooms, asked)],
        scratch_shapes=[pltpu.SMEM((PLANES * count,), jnp.int32)] * 2,
        compiler_params=PARAMS,
        name="make_plan",
    )(plane, ids)


def is_crowded(ids, count, rooms):
    items = jnp.arange(PLANES * count, dtype=jnp.int32)
    wants = (ids.reshape(PLANES, -1, 1) == items).any(axis=1)
    halves = wants.reshape(2, 2, PLANES * count).any(axis=1)
    crowded = jnp.bool_(False)
    for plane in range(PLANES):
        cross = halves[1 - plane // 2, plane * count : (plane + 1) * count]
        crowded |= jnp.sum(cross.astype(jnp.int32)) > rooms[0]
        for step, room in ((1, rooms[1]), (3, rooms[2])):
            other = plane ^ step
            wanted = wants[plane, other * count : (other + 1) * count]
            crowded |= jnp.sum(wanted.astype(jnp.int32)) > room
    return crowded


def leave_kernel(cross_ids, near_ids, spread_ref, *refs):
    cross_refs, near_ref = refs[:-1], refs[-1]
    rows = cross_refs[0].shape[2]

    def copy(i, carry):
        item = spread_ref[cross_ids[i]]
        for r, ref in enumerate(cross_refs):
            ref[i] = item[:, r * rows : (r + 1) * rows]
        return carry

    lax.fori_loop(0, cross_refs[0].shape[0], copy, 0, unroll=4)

    def copy_near(i, carry):
        near_ref[i] = spread_ref[near_ids[i]]
        return carry

    lax.fori_loop(0, near_ref.shape[0], copy_near, 0, unroll=4)


def pick_leaving(cross, near, spread):
    _, _, rows, width = spread.shape
    piece = (cross.shape[0], 2, rows // PIECES, width)
    shapes = [piece] * PIECES + [(near.shape[0],) + spread.shape[1:]]
    return pl.pallas_call(
        leave_kernel,
        in_specs=[SMEM, SMEM, VMEM],
        out_specs=[VMEM] * (PIECES + 1),
        out_shape=[jax.ShapeDtypeStruct(shape, jnp.float32) for shape in shapes],
        compiler_params=PARAMS,
        name="pick_leaving",
    )(cross, near, spread)


def pass_kernel(far_ids, crossed_ref, out_ref):
    def copy(i, carry):
        out_ref[i] = crossed_ref[far_ids[i]]
        return carry

    lax.fori_loop(0, out_ref.shape[0], copy, 0, unroll=4)


def pick_passing(far, crossed):
    return pl.pallas_call(
        pass_kernel,
        in_specs=[SMEM, VMEM],
        out_specs=VMEM,
        out_shape=jax.ShapeDtypeStruct((far.shape[0],) + crossed.shape[1:], jnp.float32),
        compiler_params=PARAMS,
        name="pick_passing",
    )(far, crossed)


def collect_kernel(source_ref, spread_ref, crossed_ref, near_ref, far_ref, out_ref):
    def copy(q, carry):
        source = source_ref[q]
        value, base = None, 0
        for ref in (spread_ref, crossed_ref, near_ref, far_ref):
            here = ref[jnp.clip(source - base, 0, ref.shape[0] - 1)]
            value = here if value is None else jnp.where(source < base, value, here)
            base += ref.shape[0]
        out_ref[q] = value
        return carry

    lax.fori_loop(0, out_ref.shape[0], copy, 0, unroll=8)


def collect(source, spread, crossed, near, far, piece):
    _, _, rows, width = crossed.shape

    def rows_of(array):
        return pl.BlockSpec((array.shape[0], 2, rows, width), lambda i: (0, 0, piece, 0))

    return pl.pallas_call(
        collect_kernel,
        grid=(1,),
        in_specs=[SMEM, rows_of(spread), VMEM, rows_of(near), VMEM],
        out_specs=VMEM,
        out_shape=jax.ShapeDtypeStruct((source.shape[0],) + crossed.shape[1:], jnp.float32),
        compiler_params=COLLECT,
        name="collect",
    )(source, spread, crossed, near, far)


def fetch_items(cuts, ids):
    devices = lax.axis_size("node")
    group = devices // PLANES
    plane = (lax.axis_index("node") // group).astype(jnp.int32)
    planes = [[p * group + i for i in range(group)] for p in range(PLANES)]
    swap = [(i, (i // group ^ 2) * group + i % group) for i in range(devices)]
    mate = [(i, (i // group ^ 1) * group + i % group) for i in range(devices)]
    count = group * cuts[0].shape[1]
    rooms = tuple(
        min(count, max(8, int(count * share))) for share in (CROSS_SHARE, NEAR_SHARE, NEAR_SHARE)
    )
    flat = ids.reshape(-1)
    cross, near, far, source = make_plan(plane.reshape(1), flat, count, rooms)
    crowded = is_crowded(flat, count, rooms)
    own_ids = lax.dynamic_index_in_dim(ids.reshape(PLANES, -1), plane, 0, keepdims=False)

    def exchange(x):
        return lax.all_to_all(x, "node", 0, 0, axis_index_groups=planes, tiled=True)

    def gather_all(spread, crossed, near_by, far_by, piece):
        rows = crossed.shape[2]
        here = spread[:, :, piece * rows : (piece + 1) * rows]
        crossing = lax.ppermute(here, "node", swap)
        both = jnp.concatenate([here, crossing])
        every = jnp.concatenate([both, lax.ppermute(both, "node", mate)])
        order = own_ids // count ^ plane
        index = jnp.array([0, 2, 1, 3])[order] * count + own_ids % count
        return jnp.take(every, index, axis=0)

    delivered = []
    for cut in cuts:
        spread = exchange(cut)
        spread = spread.reshape((count,) + spread.shape[2:])
        *leaving, staying = pick_leaving(cross, near, spread)
        crossed = []
        for r in range(PIECES):
            crossed.append(lax.ppermute(leaving[r], "node", swap))
        near_by = lax.ppermute(staying, "node", mate)
        pieces = []
        for r in range(PIECES):
            passing = pick_passing(far, crossed[r])
            far_by = lax.ppermute(passing, "node", mate)
            picked = lax.cond(
                crowded,
                functools.partial(gather_all, piece=r),
                functools.partial(collect, source, piece=r),
                spread,
                crossed[r],
                near_by,
                far_by,
            )
            picked = picked.reshape((group, ids.shape[1]) + picked.shape[1:])
            pieces.append(exchange(picked))
        delivered.append(pieces)
    return delivered


def halves_of(x):
    high = x.astype(jnp.bfloat16)
    return high, (x - high.astype(jnp.float32)).astype(jnp.bfloat16)


def joined(pieces):
    rows = jnp.concatenate([p[:, None] for p in pieces], axis=1)
    return rows.reshape(-1, rows.shape[-1])


def stacked(blocks):
    real, imag = (
        jnp.concatenate([joined([piece[:, c] for piece in block]) for block in blocks], axis=1)
        for c in range(2)
    )
    pairs = zip(halves_of(real), halves_of(imag))
    return [
        jnp.concatenate([jnp.concatenate([r, i], axis=1), jnp.concatenate([-i, r], axis=1)], axis=0)
        for r, i in pairs
    ]


def product(left, blocks):
    left_high, left_low = halves_of(left)
    right_high, right_low = stacked(blocks)
    dot = functools.partial(jnp.dot, preferred_element_type=jnp.float32)
    small = dot(left_high, right_low) + dot(left_low, right_high)
    return dot(left_high, right_high) + small


def columns_of(rights):
    return sum(right.shape[-1] for right in rights) // PIECES


def wide(ref):
    return jnp.concatenate([ref[0, 0], ref[0, 1]], axis=1)


def triple_spec(array):
    group, _, _, rows, width = array.shape
    return pl.BlockSpec((group, 3, 2, rows, width), lambda k, *scalars: (0, k, 0, 0, 0))


def items(refs, which):
    pieces = [ref[:, which] for ref in refs]
    return [pieces[i : i + PIECES] for i in range(0, len(pieces), PIECES)]


def multiply_kernel(which, index_ref, left_ref, *refs):
    right_refs, out_ref = refs[:-1], refs[-1]
    both = product(wide(left_ref), items(right_refs, which))
    width = out_ref.shape[-1]
    out_ref[0, 0] = both[:, :width]
    out_ref[0, 1] = both[:, width:]


def multiply(left_index, lefts, rights, which):
    order = lefts.shape[2]
    number = left_index.shape[0]
    cols = columns_of(rights)
    return pl.pallas_call(
        functools.partial(multiply_kernel, which),
        grid_spec=pltpu.PrefetchScalarGridSpec(
            num_scalar_prefetch=1,
            grid=(number,),
            in_specs=[
                pl.BlockSpec((1, 2, order, order), lambda k, index: (index[k], 0, 0, 0)),
                *[triple_spec(right) for right in rights],
            ],
            out_specs=pl.BlockSpec((1, 2, order, cols), lambda k, index: (k, 0, 0, 0)),
        ),
        out_shape=jax.ShapeDtypeStruct((number, 2, order, cols), jnp.float32),
        compiler_params=CHAIN,
        name="multiply",
    )(left_index, lefts, *rights)


def add_result(step, target, sign, both, out_ref):
    width = out_ref.shape[-1]

    @pl.when(step == 0)
    def _():
        out_ref[...] = jnp.zeros_like(out_ref)

    both = both * sign[step].astype(jnp.float32)
    row = target[step]
    out_ref[row, 0] += both[:, :width]
    out_ref[row, 1] += both[:, width:]


def finish_kernel(target, sign, left_ref, *refs):
    right_refs, out_ref = refs[:-1], refs[-1]
    both = product(wide(left_ref), items(right_refs, 2))
    add_result(pl.program_id(0), target, sign, both, out_ref)


def finish(target, sign, lefts, rights):
    order = lefts.shape[2]
    whole = (RES_COL, 2, order, columns_of(rights))
    return pl.pallas_call(
        finish_kernel,
        grid_spec=pltpu.PrefetchScalarGridSpec(
            num_scalar_prefetch=2,
            grid=(lefts.shape[0],),
            in_specs=[
                pl.BlockSpec((1, 2, order, order), lambda k, t, s: (k, 0, 0, 0)),
                *[triple_spec(right) for right in rights],
            ],
            out_specs=pl.BlockSpec(whole, lambda k, t, s: (0, 0, 0, 0)),
        ),
        out_shape=jax.ShapeDtypeStruct(whole, jnp.float32),
        compiler_params=CHAIN,
        name="finish",
    )(target, sign, lefts, *rights)


def chain_kernel(slot, target, sign, node_ref, start_ref, *refs):
    right_refs, out_ref = refs[:-1], refs[-1]
    last = product(wide(node_ref), items(right_refs[-PIECES:], 0))
    width = last.shape[1] // 2
    first = jnp.concatenate(
        [start_ref[0, 0], last[:, :width], start_ref[0, 1], last[:, width:]], axis=1
    )
    longer = product(first, items(right_refs, 1))
    both = product(longer, items(right_refs, 2))
    add_result(pl.program_id(0), target, sign, both, out_ref)


def chain(slot, target, sign, nodes, start, rights):
    order = nodes.shape[2]
    whole = (RES_COL, 2, order, order)
    early = start.shape[-1]
    return pl.pallas_call(
        chain_kernel,
        grid_spec=pltpu.PrefetchScalarGridSpec(
            num_scalar_prefetch=3,
            grid=(slot.shape[0],),
            in_specs=[
                pl.BlockSpec((1, 2, order, order), lambda k, slot, t, s: (slot[k], 0, 0, 0)),
                pl.BlockSpec((1, 2, order, early), lambda k, slot, t, s: (k, 0, 0, 0)),
                *[triple_spec(right) for right in rights],
            ],
            out_specs=pl.BlockSpec(whole, lambda k, slot, t, s: (0, 0, 0, 0)),
        ),
        out_shape=jax.ShapeDtypeStruct(whole, jnp.float32),
        compiler_params=CHAIN,
        name="chain",
    )(slot, target, sign, nodes, start, *rights)


def all_columns(x):
    if lax.axis_size("pair") == 1:
        return x
    return lax.all_gather(x, "pair", axis=3, tiled=True)


def per_device(node_blocks, node_slot, pair_list, second_list, targets, spin_signs):
    devices = lax.axis_size("node")
    column = lax.axis_index("node")
    group = devices // PLANES
    node_col, _, _, local_width = node_blocks.shape
    second_col = second_list.shape[0] // devices
    width = min(LANES, local_width)
    cuts = [cut_rows(node_blocks, group, c, width) for c in range(local_width // width)]

    slots = node_slot[pair_list]
    slots = slots[second_list].reshape(devices, second_col, 4)
    rights = fetch_items(cuts, slots[:, :, 1:].reshape(devices, second_col * 3))

    own_slots = lax.dynamic_index_in_dim(slots[:, :, 0], column, 0, keepdims=False)
    own_slots = own_slots - column * node_col
    own_signs = lax.dynamic_slice_in_dim(spin_signs, column * second_col, second_col, 0)
    own_targets = lax.dynamic_slice_in_dim(targets, column * second_col, second_col, 0)
    own_targets = own_targets - column * RES_COL

    parts = len(rights)
    rights = [piece for pieces in rights for piece in pieces]
    if lax.axis_size("pair") == 1 and parts > 1:
        start = multiply(own_slots, node_blocks, rights[:-PIECES], 0)
        return chain(own_slots, own_targets, own_signs, node_blocks, start, rights)
    same = jnp.arange(second_col, dtype=jnp.int32)
    products = multiply(own_slots, all_columns(node_blocks), rights, 0)
    longer = multiply(same, all_columns(products), rights, 1)
    return finish(own_targets, own_signs, all_columns(longer), rights)


def solution(mesh):
    placed = (P(("cfg", "node"), None, None, "pair"), P(), P(), P(), P(), P())

    return jax.shard_map(
        per_device,
        mesh=mesh,
        in_specs=placed,
        out_specs=P(("cfg", "node"), None, None, "pair"),
        check_vma=False,
    )
```

```python
import functools

import jax
import jax.numpy as jnp
from jax import lax
from jax.experimental import pallas as pl
from jax.experimental.pallas import tpu as pltpu
from jax.sharding import PartitionSpec as P


RES_COL = 2
LANES = 128
CROSS_SHARE = 29 / 64
ANY = pl.BlockSpec(memory_space=pl.ANY)
HBM = pl.BlockSpec(memory_space=pltpu.HBM)
SMEM = pl.BlockSpec(memory_space=pltpu.SMEM)
VMEM = pl.BlockSpec(memory_space=pltpu.VMEM)
PARAMS = pltpu.CompilerParams(vmem_limit_bytes=24 * 1024 * 1024)
LARGE = pltpu.CompilerParams(vmem_limit_bytes=56 * 1024 * 1024)
CHAIN = pltpu.CompilerParams(vmem_limit_bytes=44 * 1024 * 1024)


def cut_kernel(in_ref, out_ref):
    rows = out_ref.shape[3]
    for j in range(out_ref.shape[0]):
        out_ref[j] = in_ref[:, :, j * rows : (j + 1) * rows, :]


def cut_rows(nodes, group, part, width):
    count, _, order, _ = nodes.shape
    rows = order // group
    steps = 2 if group % 2 == 0 else 1
    return pl.pallas_call(
        cut_kernel,
        grid=(steps,),
        in_specs=[pl.BlockSpec((count, 2, order // steps, width), lambda i: (0, 0, i, part))],
        out_specs=pl.BlockSpec((group // steps, count, 2, rows, width), lambda i: (i, 0, 0, 0, 0)),
        out_shape=jax.ShapeDtypeStruct((group, count, 2, rows, width), jnp.float32),
        name="cut_rows",
    )(nodes)


def plan_kernel(room, half_ref, ids_ref, send_ref, source_ref, crowded_ref, place_ref):
    half = half_ref[0]
    count = send_ref.shape[0]
    asked = source_ref.shape[0]

    def clear(i, carry):
        place_ref[i] = -1
        return carry

    def empty(i, carry):
        send_ref[i] = 0
        return carry

    lax.fori_loop(0, 2 * count, clear, 0, unroll=8)
    lax.fori_loop(0, count, empty, 0, unroll=8)

    def visit_other(q, found):
        item = ids_ref[(1 - half) * asked + q]
        here = item - half * count
        fresh = (here >= 0) & (here < count) & (place_ref[item] < 0)

        @pl.when(fresh)
        def _():
            place_ref[item] = 0
            send_ref[found] = here

        return found + fresh.astype(jnp.int32)

    def visit_own(q, found):
        item = ids_ref[half * asked + q]
        here = item - half * count
        inside = (here >= 0) & (here < count)
        known = place_ref[item]
        fresh = jnp.logical_not(inside) & (known < 0)
        there = count + room + item - (1 - half) * count
        place = jnp.where(known < 0, jnp.where(found < room, count + found, there), known)

        @pl.when(fresh)
        def _():
            place_ref[item] = place

        source_ref[q] = jnp.where(inside, here, place)
        return found + fresh.astype(jnp.int32)

    sent = lax.fori_loop(0, asked, visit_other, jnp.int32(0))
    received = lax.fori_loop(0, asked, visit_own, jnp.int32(0))
    crowded_ref[0] = (jnp.maximum(sent, received) > room).astype(jnp.int32)


def make_plan(half, ids, count, room):
    asked = ids.shape[0] // 2
    return pl.pallas_call(
        functools.partial(plan_kernel, room),
        in_specs=[SMEM] * 2,
        out_specs=[SMEM] * 3,
        out_shape=[
            jax.ShapeDtypeStruct((count,), jnp.int32),
            jax.ShapeDtypeStruct((asked,), jnp.int32),
            jax.ShapeDtypeStruct((1,), jnp.int32),
        ],
        scratch_shapes=[pltpu.SMEM((2 * count,), jnp.int32)],
        compiler_params=PARAMS,
        name="make_plan",
    )(half, ids)


def leave_kernel(send_ref, spread_ref, out_ref):
    def copy(i, carry):
        out_ref[i] = spread_ref[send_ref[i]]
        return carry

    lax.fori_loop(0, out_ref.shape[0], copy, 0, unroll=8)


def pick_leaving(send, spread, room):
    return pl.pallas_call(
        leave_kernel,
        in_specs=[SMEM, VMEM],
        out_specs=VMEM,
        out_shape=jax.ShapeDtypeStruct((room,) + spread.shape[1:], jnp.float32),
        compiler_params=PARAMS,
        name="pick_leaving",
    )(send, spread)


def collect_kernel(source_ref, crowded_ref, spread_ref, arrived_ref, extra_ref, out_ref, sem):
    count, room = spread_ref.shape[0], arrived_ref.shape[0]

    def copy(q, carry):
        source = source_ref[q]
        near = jnp.minimum(source, count - 1)
        far = jnp.clip(source - count, 0, room - 1)
        out_ref[q] = jnp.where(source < count, spread_ref[near], arrived_ref[far])
        return carry

    lax.fori_loop(0, out_ref.shape[0], copy, 0, unroll=8)

    @pl.when(crowded_ref[0] > 0)
    def _():
        def fetch(q, carry):
            source = source_ref[q] - (count + room)

            @pl.when(source >= 0)
            def _():
                slow = pltpu.make_async_copy(extra_ref.at[source], out_ref.at[q], sem)
                slow.start()
                slow.wait()

            return carry

        lax.fori_loop(0, out_ref.shape[0], fetch, 0)


def collect(source, crowded, spread, arrived, extra):
    return pl.pallas_call(
        collect_kernel,
        in_specs=[SMEM, SMEM, VMEM, VMEM, ANY],
        out_specs=VMEM,
        out_shape=jax.ShapeDtypeStruct((source.shape[0],) + spread.shape[1:], jnp.float32),
        scratch_shapes=[pltpu.SemaphoreType.DMA],
        compiler_params=PARAMS,
        name="collect",
    )(source, crowded, spread, arrived, extra)


def fetch_items(cuts, ids):
    devices = lax.axis_size("node")
    group = devices // 2
    half = (lax.axis_index("node") // group).astype(jnp.int32).reshape(1)
    halves = [[h * group + i for i in range(group)] for h in range(2)]
    swap = [(i, (i + group) % devices) for i in range(devices)]
    count = group * cuts[0].shape[1]
    room = min(count, max(8, int(count * CROSS_SHARE)))
    send, source, crowded = make_plan(half, ids.reshape(-1), count, room)

    def exchange(x):
        return lax.all_to_all(x, "node", 0, 0, axis_index_groups=halves, tiled=True)

    delivered = []
    for cut in cuts:
        spread = exchange(cut)
        spread = spread.reshape((count,) + spread.shape[2:])
        leaving = pick_leaving(send, spread, room)
        arrived = lax.ppermute(leaving, "node", swap)
        extra = lax.cond(
            crowded[0] > 0,
            lambda x: lax.ppermute(x, "node", swap),
            jnp.zeros_like,
            spread,
        )
        picked = collect(source, crowded, spread, arrived, extra)
        picked = picked.reshape((group, ids.shape[1]) + picked.shape[1:])
        delivered.append(exchange(picked))
    return delivered


def halves_of(x):
    high = x.astype(jnp.bfloat16)
    return high, (x - high.astype(jnp.float32)).astype(jnp.bfloat16)


def stacked(blocks):
    order = blocks[0].shape[0] * blocks[0].shape[2]
    real, imag = (
        jnp.concatenate([b[:, c].reshape(order, b.shape[-1]) for b in blocks], axis=1)
        for c in range(2)
    )
    pairs = zip(halves_of(real), halves_of(imag))
    return [
        jnp.concatenate([jnp.concatenate([r, i], axis=1), jnp.concatenate([-i, r], axis=1)], axis=0)
        for r, i in pairs
    ]


def product(left, blocks):
    left_high, left_low = halves_of(left)
    right_high, right_low = stacked(blocks)
    return jnp.dot(
        jnp.concatenate([left_high, left_high, left_low], axis=1),
        jnp.concatenate([right_high, right_low, right_high], axis=0),
        preferred_element_type=jnp.float32,
    )


def wide(ref):
    return jnp.concatenate([ref[0, 0], ref[0, 1]], axis=1)


def triple_spec(array):
    group, _, _, rows, width = array.shape
    return pl.BlockSpec((group, 3, 2, rows, width), lambda k, *scalars: (0, k, 0, 0, 0))


def multiply_kernel(which, index_ref, left_ref, *refs):
    right_refs, out_ref = refs[:-1], refs[-1]
    both = product(wide(left_ref), [ref[:, which] for ref in right_refs])
    width = out_ref.shape[-1]
    out_ref[0, 0] = both[:, :width]
    out_ref[0, 1] = both[:, width:]


def multiply(left_index, lefts, rights, which):
    order = lefts.shape[2]
    number = left_index.shape[0]
    cols = sum(right.shape[-1] for right in rights)
    return pl.pallas_call(
        functools.partial(multiply_kernel, which),
        grid_spec=pltpu.PrefetchScalarGridSpec(
            num_scalar_prefetch=1,
            grid=(number,),
            in_specs=[
                pl.BlockSpec((1, 2, order, order), lambda k, index: (index[k], 0, 0, 0)),
                *[triple_spec(right) for right in rights],
            ],
            out_specs=pl.BlockSpec((1, 2, order, cols), lambda k, index: (k, 0, 0, 0)),
        ),
        out_shape=jax.ShapeDtypeStruct((number, 2, order, cols), jnp.float32),
        compiler_params=LARGE,
        name="multiply",
    )(left_index, lefts, *rights)


def add_result(step, target, sign, both, out_ref):
    width = out_ref.shape[-1]

    @pl.when(step == 0)
    def _():
        out_ref[...] = jnp.zeros_like(out_ref)

    both = both * sign[step].astype(jnp.float32)
    row = target[step]
    out_ref[row, 0] += both[:, :width]
    out_ref[row, 1] += both[:, width:]


def finish_kernel(target, sign, left_ref, *refs):
    right_refs, out_ref = refs[:-1], refs[-1]
    both = product(wide(left_ref), [ref[:, 2] for ref in right_refs])
    add_result(pl.program_id(0), target, sign, both, out_ref)


def finish(target, sign, lefts, rights):
    order = lefts.shape[2]
    whole = (RES_COL, 2, order, sum(right.shape[-1] for right in rights))
    return pl.pallas_call(
        finish_kernel,
        grid_spec=pltpu.PrefetchScalarGridSpec(
            num_scalar_prefetch=2,
            grid=(lefts.shape[0],),
            in_specs=[
                pl.BlockSpec((1, 2, order, order), lambda k, t, s: (k, 0, 0, 0)),
                *[triple_spec(right) for right in rights],
            ],
            out_specs=pl.BlockSpec(whole, lambda k, t, s: (0, 0, 0, 0)),
        ),
        out_shape=jax.ShapeDtypeStruct(whole, jnp.float32),
        compiler_params=LARGE,
        name="finish",
    )(target, sign, lefts, *rights)


def chain_kernel(slot, target, sign, node_ref, *refs):
    right_refs, out_ref = refs[:-1], refs[-1]
    left = wide(node_ref)
    for which in range(3):
        left = product(left, [ref[:, which] for ref in right_refs])
    add_result(pl.program_id(0), target, sign, left, out_ref)


def chain(slot, target, sign, nodes, rights):
    order = nodes.shape[2]
    whole = (RES_COL, 2, order, order)
    return pl.pallas_call(
        chain_kernel,
        grid_spec=pltpu.PrefetchScalarGridSpec(
            num_scalar_prefetch=3,
            grid=(slot.shape[0],),
            in_specs=[
                pl.BlockSpec((1, 2, order, order), lambda k, slot, t, s: (slot[k], 0, 0, 0)),
                *[triple_spec(right) for right in rights],
            ],
            out_specs=pl.BlockSpec(whole, lambda k, slot, t, s: (0, 0, 0, 0)),
        ),
        out_shape=jax.ShapeDtypeStruct(whole, jnp.float32),
        compiler_params=CHAIN,
        name="chain",
    )(slot, target, sign, nodes, *rights)


def all_columns(x):
    if lax.axis_size("pair") == 1:
        return x
    return lax.all_gather(x, "pair", axis=3, tiled=True)


def per_device(node_blocks, node_slot, pair_list, second_list, targets, spin_signs):
    devices = lax.axis_size("node")
    column = lax.axis_index("node")
    group = devices // 2
    node_col, _, _, local_width = node_blocks.shape
    second_col = second_list.shape[0] // devices
    width = min(LANES, local_width)
    cuts = [cut_rows(node_blocks, group, c, width) for c in range(local_width // width)]

    slots = node_slot[pair_list]
    slots = slots[second_list].reshape(devices, second_col, 4)
    rights = fetch_items(cuts, slots[:, :, 1:].reshape(devices, second_col * 3))

    own_slots = lax.dynamic_index_in_dim(slots[:, :, 0], column, 0, keepdims=False)
    own_slots = own_slots - column * node_col
    own_signs = lax.dynamic_slice_in_dim(spin_signs, column * second_col, second_col, 0)
    own_targets = lax.dynamic_slice_in_dim(targets, column * second_col, second_col, 0)
    own_targets = own_targets - column * RES_COL

    if lax.axis_size("pair") == 1:
        return chain(own_slots, own_targets, own_signs, node_blocks, rights)
    same = jnp.arange(second_col, dtype=jnp.int32)
    products = multiply(own_slots, all_columns(node_blocks), rights, 0)
    longer = multiply(same, all_columns(products), rights, 1)
    return finish(own_targets, own_signs, all_columns(longer), rights)


def solution(mesh):
    placed = (P(("cfg", "node"), None, None, "pair"), P(), P(), P(), P(), P())

    return jax.shard_map(
        per_device,
        mesh=mesh,
        in_specs=placed,
        out_specs=P(("cfg", "node"), None, None, "pair"),
        check_vma=False,
    )
```

```python
import functools

import jax
import jax.numpy as jnp
from jax import lax
from jax.experimental import pallas as pl
from jax.experimental.pallas import tpu as pltpu
from jax.sharding import PartitionSpec as P


RES_COL = 2
LANES = 128
CROSS_SHARE = 29 / 64
ANY = pl.BlockSpec(memory_space=pl.ANY)
HBM = pl.BlockSpec(memory_space=pltpu.HBM)
SMEM = pl.BlockSpec(memory_space=pltpu.SMEM)
VMEM = pl.BlockSpec(memory_space=pltpu.VMEM)
PARAMS = pltpu.CompilerParams(vmem_limit_bytes=24 * 1024 * 1024)
LARGE = pltpu.CompilerParams(vmem_limit_bytes=56 * 1024 * 1024)
CHAIN = pltpu.CompilerParams(vmem_limit_bytes=44 * 1024 * 1024)


def cut_kernel(in_ref, out_ref):
    rows = out_ref.shape[3]
    for j in range(out_ref.shape[0]):
        out_ref[j] = in_ref[:, :, j * rows : (j + 1) * rows, :]


def cut_rows(nodes, group, part, width):
    count, _, order, _ = nodes.shape
    rows = order // group
    steps = 2 if group % 2 == 0 else 1
    return pl.pallas_call(
        cut_kernel,
        grid=(steps,),
        in_specs=[pl.BlockSpec((count, 2, order // steps, width), lambda i: (0, 0, i, part))],
        out_specs=pl.BlockSpec((group // steps, count, 2, rows, width), lambda i: (i, 0, 0, 0, 0)),
        out_shape=jax.ShapeDtypeStruct((group, count, 2, rows, width), jnp.float32),
        name="cut_rows",
    )(nodes)


def plan_kernel(room, half_ref, ids_ref, send_ref, source_ref, crowded_ref, place_ref):
    half = half_ref[0]
    count = send_ref.shape[0]
    asked = source_ref.shape[0]

    def clear(i, carry):
        place_ref[i] = -1
        return carry

    def empty(i, carry):
        send_ref[i] = 0
        return carry

    lax.fori_loop(0, 2 * count, clear, 0, unroll=8)
    lax.fori_loop(0, count, empty, 0, unroll=8)

    def visit_other(q, found):
        item = ids_ref[(1 - half) * asked + q]
        here = item - half * count
        fresh = (here >= 0) & (here < count) & (place_ref[item] < 0)

        @pl.when(fresh)
        def _():
            place_ref[item] = 0
            send_ref[found] = here

        return found + fresh.astype(jnp.int32)

    def visit_own(q, found):
        item = ids_ref[half * asked + q]
        here = item - half * count
        inside = (here >= 0) & (here < count)
        known = place_ref[item]
        fresh = jnp.logical_not(inside) & (known < 0)
        there = count + room + item - (1 - half) * count
        place = jnp.where(known < 0, jnp.where(found < room, count + found, there), known)

        @pl.when(fresh)
        def _():
            place_ref[item] = place

        source_ref[q] = jnp.where(inside, here, place)
        return found + fresh.astype(jnp.int32)

    sent = lax.fori_loop(0, asked, visit_other, jnp.int32(0))
    received = lax.fori_loop(0, asked, visit_own, jnp.int32(0))
    crowded_ref[0] = (jnp.maximum(sent, received) > room).astype(jnp.int32)


def make_plan(half, ids, count, room):
    asked = ids.shape[0] // 2
    return pl.pallas_call(
        functools.partial(plan_kernel, room),
        in_specs=[SMEM] * 2,
        out_specs=[SMEM] * 3,
        out_shape=[
            jax.ShapeDtypeStruct((count,), jnp.int32),
            jax.ShapeDtypeStruct((asked,), jnp.int32),
            jax.ShapeDtypeStruct((1,), jnp.int32),
        ],
        scratch_shapes=[pltpu.SMEM((2 * count,), jnp.int32)],
        compiler_params=PARAMS,
        name="make_plan",
    )(half, ids)


def leave_kernel(send_ref, spread_ref, out_ref):
    def copy(i, carry):
        out_ref[i] = spread_ref[send_ref[i]]
        return carry

    lax.fori_loop(0, out_ref.shape[0], copy, 0, unroll=8)


def pick_leaving(send, spread, room):
    return pl.pallas_call(
        leave_kernel,
        in_specs=[SMEM, VMEM],
        out_specs=VMEM,
        out_shape=jax.ShapeDtypeStruct((room,) + spread.shape[1:], jnp.float32),
        compiler_params=PARAMS,
        name="pick_leaving",
    )(send, spread)


def collect_kernel(
    source_ref, flags_ref, spread_ref, first_ref, second_ref, extra_ref, out_ref, sem
):
    count, room = spread_ref.shape[0], first_ref.shape[0]
    outer = flags_ref[1] > 0

    def copy(q, carry):
        source = source_ref[q]
        near = jnp.minimum(source, count - 1)
        far = jnp.clip(source - count, 0, room - 1)
        arrived = jnp.where(outer, second_ref[far], first_ref[far])
        out_ref[q] = jnp.where(source < count, spread_ref[near], arrived)
        return carry

    lax.fori_loop(0, out_ref.shape[0], copy, 0, unroll=8)

    @pl.when(flags_ref[0] > 0)
    def _():
        def fetch(q, carry):
            source = source_ref[q] - (count + room)

            @pl.when(source >= 0)
            def _():
                slow = pltpu.make_async_copy(extra_ref.at[source], out_ref.at[q], sem)
                slow.start()
                slow.wait()

            return carry

        lax.fori_loop(0, out_ref.shape[0], fetch, 0)


def collect(source, flags, spread, first, second, extra):
    return pl.pallas_call(
        collect_kernel,
        in_specs=[SMEM, SMEM, VMEM, VMEM, VMEM, ANY],
        out_specs=VMEM,
        out_shape=jax.ShapeDtypeStruct((source.shape[0],) + spread.shape[1:], jnp.float32),
        scratch_shapes=[pltpu.SemaphoreType.DMA],
        compiler_params=PARAMS,
        name="collect",
    )(source, flags, spread, first, second, extra)


def fetch_items(cuts, ids):
    devices = lax.axis_size("node")
    group = devices // 2
    half = (lax.axis_index("node") // group).astype(jnp.int32).reshape(1)
    halves = [[h * group + i for i in range(group)] for h in range(2)]
    swap = [(i, (i + group) % devices) for i in range(devices)]
    outer = [i < group // 2 or i >= devices - group // 2 for i in range(devices)]
    outer_swap = [pair for pair in swap if outer[pair[0]]]
    inner_swap = [pair for pair in swap if not outer[pair[0]]]
    index = lax.axis_index("node")
    is_outer = (index < group // 2) | (index >= devices - group // 2)
    count = group * cuts[0].shape[1]
    room = min(count, max(8, int(count * CROSS_SHARE)))
    send, source, crowded = make_plan(half, ids.reshape(-1), count, room)
    flags = jnp.concatenate([crowded, is_outer.astype(jnp.int32).reshape(1)])

    def exchange(x):
        return lax.all_to_all(x, "node", 0, 0, axis_index_groups=halves, tiled=True)

    delivered = []
    for cut in cuts:
        spread = exchange(cut)
        spread = spread.reshape((count,) + spread.shape[2:])
        leaving = pick_leaving(send, spread, room)
        first = lax.ppermute(leaving, "node", outer_swap)
        second = lax.ppermute(leaving, "node", inner_swap)
        extra = lax.cond(
            crowded[0] > 0,
            lambda x: lax.ppermute(x, "node", swap),
            jnp.zeros_like,
            spread,
        )
        picked = collect(source, flags, spread, first, second, extra)
        picked = picked.reshape((group, ids.shape[1]) + picked.shape[1:])
        delivered.append(exchange(picked))
    return delivered


def halves_of(x):
    high = x.astype(jnp.bfloat16)
    return high, (x - high.astype(jnp.float32)).astype(jnp.bfloat16)


def stacked(blocks):
    order = blocks[0].shape[0] * blocks[0].shape[2]
    real, imag = (
        jnp.concatenate([b[:, c].reshape(order, b.shape[-1]) for b in blocks], axis=1)
        for c in range(2)
    )
    pairs = zip(halves_of(real), halves_of(imag))
    return [
        jnp.concatenate([jnp.concatenate([r, i], axis=1), jnp.concatenate([-i, r], axis=1)], axis=0)
        for r, i in pairs
    ]


def product(left, blocks):
    left_high, left_low = halves_of(left)
    right_high, right_low = stacked(blocks)
    return jnp.dot(
        jnp.concatenate([left_high, left_high, left_low], axis=1),
        jnp.concatenate([right_high, right_low, right_high], axis=0),
        preferred_element_type=jnp.float32,
    )


def wide(ref):
    return jnp.concatenate([ref[0, 0], ref[0, 1]], axis=1)


def triple_spec(array):
    group, _, _, rows, width = array.shape
    return pl.BlockSpec((group, 3, 2, rows, width), lambda k, *scalars: (0, k, 0, 0, 0))


def multiply_kernel(which, index_ref, left_ref, *refs):
    right_refs, out_ref = refs[:-1], refs[-1]
    both = product(wide(left_ref), [ref[:, which] for ref in right_refs])
    width = out_ref.shape[-1]
    out_ref[0, 0] = both[:, :width]
    out_ref[0, 1] = both[:, width:]


def multiply(left_index, lefts, rights, which):
    order = lefts.shape[2]
    number = left_index.shape[0]
    cols = sum(right.shape[-1] for right in rights)
    return pl.pallas_call(
        functools.partial(multiply_kernel, which),
        grid_spec=pltpu.PrefetchScalarGridSpec(
            num_scalar_prefetch=1,
            grid=(number,),
            in_specs=[
                pl.BlockSpec((1, 2, order, order), lambda k, index: (index[k], 0, 0, 0)),
                *[triple_spec(right) for right in rights],
            ],
            out_specs=pl.BlockSpec((1, 2, order, cols), lambda k, index: (k, 0, 0, 0)),
        ),
        out_shape=jax.ShapeDtypeStruct((number, 2, order, cols), jnp.float32),
        compiler_params=LARGE,
        name="multiply",
    )(left_index, lefts, *rights)


def add_result(step, target, sign, both, out_ref):
    width = out_ref.shape[-1]

    @pl.when(step == 0)
    def _():
        out_ref[...] = jnp.zeros_like(out_ref)

    both = both * sign[step].astype(jnp.float32)
    row = target[step]
    out_ref[row, 0] += both[:, :width]
    out_ref[row, 1] += both[:, width:]


def finish_kernel(target, sign, left_ref, *refs):
    right_refs, out_ref = refs[:-1], refs[-1]
    both = product(wide(left_ref), [ref[:, 2] for ref in right_refs])
    add_result(pl.program_id(0), target, sign, both, out_ref)


def finish(target, sign, lefts, rights):
    order = lefts.shape[2]
    whole = (RES_COL, 2, order, sum(right.shape[-1] for right in rights))
    return pl.pallas_call(
        finish_kernel,
        grid_spec=pltpu.PrefetchScalarGridSpec(
            num_scalar_prefetch=2,
            grid=(lefts.shape[0],),
            in_specs=[
                pl.BlockSpec((1, 2, order, order), lambda k, t, s: (k, 0, 0, 0)),
                *[triple_spec(right) for right in rights],
            ],
            out_specs=pl.BlockSpec(whole, lambda k, t, s: (0, 0, 0, 0)),
        ),
        out_shape=jax.ShapeDtypeStruct(whole, jnp.float32),
        compiler_params=LARGE,
        name="finish",
    )(target, sign, lefts, *rights)


def chain_kernel(slot, target, sign, node_ref, *refs):
    right_refs, out_ref = refs[:-1], refs[-1]
    left = wide(node_ref)
    for which in range(3):
        left = product(left, [ref[:, which] for ref in right_refs])
    add_result(pl.program_id(0), target, sign, left, out_ref)


def chain(slot, target, sign, nodes, rights):
    order = nodes.shape[2]
    whole = (RES_COL, 2, order, order)
    return pl.pallas_call(
        chain_kernel,
        grid_spec=pltpu.PrefetchScalarGridSpec(
            num_scalar_prefetch=3,
            grid=(slot.shape[0],),
            in_specs=[
                pl.BlockSpec((1, 2, order, order), lambda k, slot, t, s: (slot[k], 0, 0, 0)),
                *[triple_spec(right) for right in rights],
            ],
            out_specs=pl.BlockSpec(whole, lambda k, slot, t, s: (0, 0, 0, 0)),
        ),
        out_shape=jax.ShapeDtypeStruct(whole, jnp.float32),
        compiler_params=CHAIN,
        name="chain",
    )(slot, target, sign, nodes, *rights)


def all_columns(x):
    if lax.axis_size("pair") == 1:
        return x
    return lax.all_gather(x, "pair", axis=3, tiled=True)


def per_device(node_blocks, node_slot, pair_list, second_list, targets, spin_signs):
    devices = lax.axis_size("node")
    column = lax.axis_index("node")
    group = devices // 2
    node_col, _, _, local_width = node_blocks.shape
    second_col = second_list.shape[0] // devices
    width = min(LANES, local_width)
    cuts = [cut_rows(node_blocks, group, c, width) for c in range(local_width // width)]

    slots = node_slot[pair_list]
    slots = slots[second_list].reshape(devices, second_col, 4)
    rights = fetch_items(cuts, slots[:, :, 1:].reshape(devices, second_col * 3))

    own_slots = lax.dynamic_index_in_dim(slots[:, :, 0], column, 0, keepdims=False)
    own_slots = own_slots - column * node_col
    own_signs = lax.dynamic_slice_in_dim(spin_signs, column * second_col, second_col, 0)
    own_targets = lax.dynamic_slice_in_dim(targets, column * second_col, second_col, 0)
    own_targets = own_targets - column * RES_COL

    if lax.axis_size("pair") == 1:
        return chain(own_slots, own_targets, own_signs, node_blocks, rights)
    same = jnp.arange(second_col, dtype=jnp.int32)
    products = multiply(own_slots, all_columns(node_blocks), rights, 0)
    longer = multiply(same, all_columns(products), rights, 1)
    return finish(own_targets, own_signs, all_columns(longer), rights)


def solution(mesh):
    placed = (P(("cfg", "node"), None, None, "pair"), P(), P(), P(), P(), P())

    return jax.shard_map(
        per_device,
        mesh=mesh,
        in_specs=placed,
        out_specs=P(("cfg", "node"), None, None, "pair"),
        check_vma=False,
    )
```

```python
import functools

import jax
import jax.numpy as jnp
from jax import lax
from jax.experimental import pallas as pl
from jax.experimental.pallas import tpu as pltpu
from jax.sharding import PartitionSpec as P


RES_COL = 2
LANES = 128
CROSS_SHARE = 29 / 64
ANY = pl.BlockSpec(memory_space=pl.ANY)
HBM = pl.BlockSpec(memory_space=pltpu.HBM)
SMEM = pl.BlockSpec(memory_space=pltpu.SMEM)
VMEM = pl.BlockSpec(memory_space=pltpu.VMEM)
PARAMS = pltpu.CompilerParams(vmem_limit_bytes=24 * 1024 * 1024)
LARGE = pltpu.CompilerParams(vmem_limit_bytes=56 * 1024 * 1024)
CHAIN = pltpu.CompilerParams(vmem_limit_bytes=44 * 1024 * 1024)


def cut_kernel(in_ref, out_ref):
    rows = out_ref.shape[3]
    for j in range(out_ref.shape[0]):
        out_ref[j] = in_ref[:, :, j * rows : (j + 1) * rows, :]


def cut_rows(nodes, group, part, width):
    count, _, order, _ = nodes.shape
    rows = order // group
    steps = 2 if group % 2 == 0 else 1
    return pl.pallas_call(
        cut_kernel,
        grid=(steps,),
        in_specs=[pl.BlockSpec((count, 2, order // steps, width), lambda i: (0, 0, i, part))],
        out_specs=pl.BlockSpec((group // steps, count, 2, rows, width), lambda i: (i, 0, 0, 0, 0)),
        out_shape=jax.ShapeDtypeStruct((group, count, 2, rows, width), jnp.float32),
        name="cut_rows",
    )(nodes)


def plan_kernel(room, half_ref, ids_ref, send_ref, source_ref, crowded_ref, place_ref):
    half = half_ref[0]
    count = send_ref.shape[0]
    asked = source_ref.shape[0]

    def clear(i, carry):
        place_ref[i] = -1
        return carry

    def empty(i, carry):
        send_ref[i] = 0
        return carry

    lax.fori_loop(0, 2 * count, clear, 0, unroll=8)
    lax.fori_loop(0, count, empty, 0, unroll=8)

    def visit_other(q, found):
        item = ids_ref[(1 - half) * asked + q]
        here = item - half * count
        fresh = (here >= 0) & (here < count) & (place_ref[item] < 0)

        @pl.when(fresh)
        def _():
            place_ref[item] = 0
            send_ref[found] = here

        return found + fresh.astype(jnp.int32)

    def visit_own(q, found):
        item = ids_ref[half * asked + q]
        here = item - half * count
        inside = (here >= 0) & (here < count)
        known = place_ref[item]
        fresh = jnp.logical_not(inside) & (known < 0)
        there = count + room + item - (1 - half) * count
        place = jnp.where(known < 0, jnp.where(found < room, count + found, there), known)

        @pl.when(fresh)
        def _():
            place_ref[item] = place

        source_ref[q] = jnp.where(inside, here, place)
        return found + fresh.astype(jnp.int32)

    sent = lax.fori_loop(0, asked, visit_other, jnp.int32(0))
    received = lax.fori_loop(0, asked, visit_own, jnp.int32(0))
    crowded_ref[0] = (jnp.maximum(sent, received) > room).astype(jnp.int32)


def make_plan(half, ids, count, room):
    asked = ids.shape[0] // 2
    return pl.pallas_call(
        functools.partial(plan_kernel, room),
        in_specs=[SMEM] * 2,
        out_specs=[SMEM] * 3,
        out_shape=[
            jax.ShapeDtypeStruct((count,), jnp.int32),
            jax.ShapeDtypeStruct((asked,), jnp.int32),
            jax.ShapeDtypeStruct((1,), jnp.int32),
        ],
        scratch_shapes=[pltpu.SMEM((2 * count,), jnp.int32)],
        compiler_params=PARAMS,
        name="make_plan",
    )(half, ids)


def leave_kernel(send_ref, spread_ref, out_ref):
    def copy(i, carry):
        out_ref[i] = spread_ref[send_ref[i]]
        return carry

    lax.fori_loop(0, out_ref.shape[0], copy, 0, unroll=8)


def pick_leaving(send, spread, room):
    return pl.pallas_call(
        leave_kernel,
        in_specs=[SMEM, VMEM],
        out_specs=VMEM,
        out_shape=jax.ShapeDtypeStruct((room,) + spread.shape[1:], jnp.float32),
        compiler_params=PARAMS,
        name="pick_leaving",
    )(send, spread)


def collect_kernel(source_ref, crowded_ref, spread_ref, arrived_ref, extra_ref, out_ref, sem):
    count, room = spread_ref.shape[0], arrived_ref.shape[0]

    def copy(q, carry):
        source = source_ref[q]
        near = jnp.minimum(source, count - 1)
        far = jnp.clip(source - count, 0, room - 1)
        out_ref[q] = jnp.where(source < count, spread_ref[near], arrived_ref[far])
        return carry

    lax.fori_loop(0, out_ref.shape[0], copy, 0, unroll=8)

    @pl.when(crowded_ref[0] > 0)
    def _():
        def fetch(q, carry):
            source = source_ref[q] - (count + room)

            @pl.when(source >= 0)
            def _():
                slow = pltpu.make_async_copy(extra_ref.at[source], out_ref.at[q], sem)
                slow.start()
                slow.wait()

            return carry

        lax.fori_loop(0, out_ref.shape[0], fetch, 0)


def collect(source, crowded, spread, arrived, extra):
    return pl.pallas_call(
        collect_kernel,
        in_specs=[SMEM, SMEM, VMEM, VMEM, ANY],
        out_specs=VMEM,
        out_shape=jax.ShapeDtypeStruct((source.shape[0],) + spread.shape[1:], jnp.float32),
        scratch_shapes=[pltpu.SemaphoreType.DMA],
        compiler_params=PARAMS,
        name="collect",
    )(source, crowded, spread, arrived, extra)


def partner(index, k, group):
    return index ^ k if group & (group - 1) == 0 else (k - index + group) % group


def scatter_kernel(source_ref, flags_ref, spread_ref, arrived_ref, extra_ref, *refs):
    out_refs, sem = refs[:-1], refs[-1]
    count, room = spread_ref.shape[0], arrived_ref.shape[0]
    wanted = out_refs[0].shape[0]
    for k, out_ref in enumerate(out_refs):
        base = partner(flags_ref[1], k, len(out_refs)) * wanted

        def copy(q, carry, base=base, out_ref=out_ref):
            source = source_ref[base + q]
            near = jnp.minimum(source, count - 1)
            far = jnp.clip(source - count, 0, room - 1)
            out_ref[q] = jnp.where(source < count, spread_ref[near], arrived_ref[far])
            return carry

        lax.fori_loop(0, wanted, copy, 0, unroll=4)

        @pl.when(flags_ref[0] > 0)
        def _(base=base, out_ref=out_ref):
            def fetch(q, carry):
                source = source_ref[base + q] - (count + room)

                @pl.when(source >= 0)
                def _():
                    slow = pltpu.make_async_copy(extra_ref.at[source], out_ref.at[q], sem)
                    slow.start()
                    slow.wait()

                return carry

            lax.fori_loop(0, wanted, fetch, 0)


def scatter(source, flags, spread, arrived, extra, group):
    shape = (source.shape[0] // group,) + spread.shape[1:]
    return pl.pallas_call(
        scatter_kernel,
        in_specs=[SMEM, SMEM, VMEM, VMEM, ANY],
        out_specs=[VMEM] * group,
        out_shape=[jax.ShapeDtypeStruct(shape, jnp.float32)] * group,
        scratch_shapes=[pltpu.SemaphoreType.DMA],
        compiler_params=PARAMS,
        name="scatter",
    )(source, flags, spread, arrived, extra)


def fetch_items(cuts, ids, pairwise):
    devices = lax.axis_size("node")
    group = devices // 2
    half = (lax.axis_index("node") // group).astype(jnp.int32).reshape(1)
    halves = [[h * group + i for i in range(group)] for h in range(2)]
    swap = [(i, (i + group) % devices) for i in range(devices)]
    count = group * cuts[0].shape[1]
    room = min(count, max(8, int(count * CROSS_SHARE)))
    send, source, crowded = make_plan(half, ids.reshape(-1), count, room)

    def exchange(x):
        return lax.all_to_all(x, "node", 0, 0, axis_index_groups=halves, tiled=True)

    delivered = []
    for c, cut in enumerate(cuts):
        spread = exchange(cut)
        spread = spread.reshape((count,) + spread.shape[2:])
        leaving = pick_leaving(send, spread, room)
        arrived = lax.ppermute(leaving, "node", swap)
        extra = lax.cond(
            crowded[0] > 0,
            lambda x: lax.ppermute(x, "node", swap),
            jnp.zeros_like,
            spread,
        )
        if pairwise and c == len(cuts) - 1:
            member = (lax.axis_index("node") % group).astype(jnp.int32).reshape(1)
            flags = jnp.concatenate([crowded, member])
            sent = scatter(source, flags, spread, arrived, extra, group)
            got = []
            for k in range(group):
                pairs = [
                    (i, i // group * group + partner(i % group, k, group))
                    for i in range(devices)
                ]
                still = all(i == j for i, j in pairs)
                got.append(sent[k] if still else lax.ppermute(sent[k], "node", pairs))
            delivered.append(got)
            continue
        picked = collect(source, crowded, spread, arrived, extra)
        picked = picked.reshape((group, ids.shape[1]) + picked.shape[1:])
        delivered.append(exchange(picked))
    return delivered


def halves_of(x):
    high = x.astype(jnp.bfloat16)
    return high, (x - high.astype(jnp.float32)).astype(jnp.bfloat16)


def stacked(blocks):
    order = blocks[0].shape[0] * blocks[0].shape[2]
    real, imag = (
        jnp.concatenate([b[:, c].reshape(order, b.shape[-1]) for b in blocks], axis=1)
        for c in range(2)
    )
    pairs = zip(halves_of(real), halves_of(imag))
    return [
        jnp.concatenate([jnp.concatenate([r, i], axis=1), jnp.concatenate([-i, r], axis=1)], axis=0)
        for r, i in pairs
    ]


def product(left, blocks):
    left_high, left_low = halves_of(left)
    right_high, right_low = stacked(blocks)
    return jnp.dot(
        jnp.concatenate([left_high, left_high, left_low], axis=1),
        jnp.concatenate([right_high, right_low, right_high], axis=0),
        preferred_element_type=jnp.float32,
    )


def wide(ref):
    return jnp.concatenate([ref[0, 0], ref[0, 1]], axis=1)


def triple_spec(array):
    group, _, _, rows, width = array.shape
    return pl.BlockSpec((group, 3, 2, rows, width), lambda k, *scalars: (0, k, 0, 0, 0))


def multiply_kernel(which, index_ref, left_ref, *refs):
    right_refs, out_ref = refs[:-1], refs[-1]
    both = product(wide(left_ref), [ref[:, which] for ref in right_refs])
    width = out_ref.shape[-1]
    out_ref[0, 0] = both[:, :width]
    out_ref[0, 1] = both[:, width:]


def multiply(left_index, lefts, rights, which):
    order = lefts.shape[2]
    number = left_index.shape[0]
    cols = sum(right.shape[-1] for right in rights)
    return pl.pallas_call(
        functools.partial(multiply_kernel, which),
        grid_spec=pltpu.PrefetchScalarGridSpec(
            num_scalar_prefetch=1,
            grid=(number,),
            in_specs=[
                pl.BlockSpec((1, 2, order, order), lambda k, index: (index[k], 0, 0, 0)),
                *[triple_spec(right) for right in rights],
            ],
            out_specs=pl.BlockSpec((1, 2, order, cols), lambda k, index: (k, 0, 0, 0)),
        ),
        out_shape=jax.ShapeDtypeStruct((number, 2, order, cols), jnp.float32),
        compiler_params=LARGE,
        name="multiply",
    )(left_index, lefts, *rights)


def add_result(step, target, sign, both, out_ref):
    width = out_ref.shape[-1]

    @pl.when(step == 0)
    def _():
        out_ref[...] = jnp.zeros_like(out_ref)

    both = both * sign[step].astype(jnp.float32)
    row = target[step]
    out_ref[row, 0] += both[:, :width]
    out_ref[row, 1] += both[:, width:]


def finish_kernel(target, sign, left_ref, *refs):
    right_refs, out_ref = refs[:-1], refs[-1]
    both = product(wide(left_ref), [ref[:, 2] for ref in right_refs])
    add_result(pl.program_id(0), target, sign, both, out_ref)


def finish(target, sign, lefts, rights):
    order = lefts.shape[2]
    whole = (RES_COL, 2, order, sum(right.shape[-1] for right in rights))
    return pl.pallas_call(
        finish_kernel,
        grid_spec=pltpu.PrefetchScalarGridSpec(
            num_scalar_prefetch=2,
            grid=(lefts.shape[0],),
            in_specs=[
                pl.BlockSpec((1, 2, order, order), lambda k, t, s: (k, 0, 0, 0)),
                *[triple_spec(right) for right in rights],
            ],
            out_specs=pl.BlockSpec(whole, lambda k, t, s: (0, 0, 0, 0)),
        ),
        out_shape=jax.ShapeDtypeStruct(whole, jnp.float32),
        compiler_params=LARGE,
        name="finish",
    )(target, sign, lefts, *rights)


def chain_kernel(parts, member, slot, target, sign, node_ref, *refs):
    part_refs, got_refs, (out_ref, last_ref) = refs[:parts], refs[parts:-2], refs[-2:]
    for k, ref in enumerate(got_refs):
        rows = ref.shape[2]
        row = pl.multiple_of(partner(member[0], k, len(got_refs)) * rows, rows)
        for which in range(3):
            last_ref[which, 0, :, pl.ds(row, rows)] = ref[which]
    left = wide(node_ref)
    for which in range(3):
        blocks = [ref[:, which] for ref in part_refs] + [last_ref[which]]
        left = product(left, blocks)
    add_result(pl.program_id(0), target, sign, left, out_ref)


def chain(member, slot, target, sign, nodes, rights):
    order = nodes.shape[2]
    whole = (RES_COL, 2, order, order)
    *parts, got = rights
    _, _, rows, width = got[0].shape

    return pl.pallas_call(
        functools.partial(chain_kernel, len(parts)),
        grid_spec=pltpu.PrefetchScalarGridSpec(
            num_scalar_prefetch=4,
            grid=(slot.shape[0],),
            in_specs=[
                pl.BlockSpec((1, 2, order, order), lambda k, m, slot, t, s: (slot[k], 0, 0, 0)),
                *[triple_spec(part) for part in parts],
                *[pl.BlockSpec((3, 2, rows, width), lambda k, *scalars: (k, 0, 0, 0))] * len(got),
            ],
            out_specs=pl.BlockSpec(whole, lambda k, *scalars: (0, 0, 0, 0)),
            scratch_shapes=[pltpu.VMEM((3, 1, 2, order, width), jnp.float32)],
        ),
        out_shape=jax.ShapeDtypeStruct(whole, jnp.float32),
        compiler_params=CHAIN,
        name="chain",
    )(member, slot, target, sign, nodes, *parts, *got)


def all_columns(x):
    if lax.axis_size("pair") == 1:
        return x
    return lax.all_gather(x, "pair", axis=3, tiled=True)


def per_device(node_blocks, node_slot, pair_list, second_list, targets, spin_signs):
    devices = lax.axis_size("node")
    column = lax.axis_index("node")
    group = devices // 2
    node_col, _, _, local_width = node_blocks.shape
    second_col = second_list.shape[0] // devices
    width = min(LANES, local_width)
    cuts = [cut_rows(node_blocks, group, c, width) for c in range(local_width // width)]

    slots = node_slot[pair_list]
    slots = slots[second_list].reshape(devices, second_col, 4)
    pairwise = lax.axis_size("pair") == 1
    rights = fetch_items(cuts, slots[:, :, 1:].reshape(devices, second_col * 3), pairwise)

    own_slots = lax.dynamic_index_in_dim(slots[:, :, 0], column, 0, keepdims=False)
    own_slots = own_slots - column * node_col
    own_signs = lax.dynamic_slice_in_dim(spin_signs, column * second_col, second_col, 0)
    own_targets = lax.dynamic_slice_in_dim(targets, column * second_col, second_col, 0)
    own_targets = own_targets - column * RES_COL

    if pairwise:
        member = (column % group).astype(jnp.int32).reshape(1)
        return chain(member, own_slots, own_targets, own_signs, node_blocks, rights)
    same = jnp.arange(second_col, dtype=jnp.int32)
    products = multiply(own_slots, all_columns(node_blocks), rights, 0)
    longer = multiply(same, all_columns(products), rights, 1)
    return finish(own_targets, own_signs, all_columns(longer), rights)


def solution(mesh):
    placed = (P(("cfg", "node"), None, None, "pair"), P(), P(), P(), P(), P())

    return jax.shard_map(
        per_device,
        mesh=mesh,
        in_specs=placed,
        out_specs=P(("cfg", "node"), None, None, "pair"),
        check_vma=False,
    )
```

```python
import functools

import jax
import jax.numpy as jnp
from jax import lax
from jax.experimental import pallas as pl
from jax.experimental.pallas import tpu as pltpu
from jax.sharding import PartitionSpec as P


RES_COL = 2
LANES = 128
CROSS_SHARE = 29 / 64
ANY = pl.BlockSpec(memory_space=pl.ANY)
HBM = pl.BlockSpec(memory_space=pltpu.HBM)
SMEM = pl.BlockSpec(memory_space=pltpu.SMEM)
VMEM = pl.BlockSpec(memory_space=pltpu.VMEM)
PARAMS = pltpu.CompilerParams(vmem_limit_bytes=24 * 1024 * 1024)
LARGE = pltpu.CompilerParams(vmem_limit_bytes=56 * 1024 * 1024)
CHAIN = pltpu.CompilerParams(vmem_limit_bytes=44 * 1024 * 1024)


def cut_kernel(in_ref, out_ref):
    rows = out_ref.shape[3]
    for j in range(out_ref.shape[0]):
        out_ref[j] = in_ref[:, :, j * rows : (j + 1) * rows, :]


def cut_rows(nodes, group, part, width):
    count, _, order, _ = nodes.shape
    rows = order // group
    steps = 2 if group % 2 == 0 else 1
    return pl.pallas_call(
        cut_kernel,
        grid=(steps,),
        in_specs=[pl.BlockSpec((count, 2, order // steps, width), lambda i: (0, 0, i, part))],
        out_specs=pl.BlockSpec((group // steps, count, 2, rows, width), lambda i: (i, 0, 0, 0, 0)),
        out_shape=jax.ShapeDtypeStruct((group, count, 2, rows, width), jnp.float32),
        name="cut_rows",
    )(nodes)


def partner(index, k, group):
    return index ^ k if group & (group - 1) == 0 else (k - index + group) % group


def split_kernel(member, in_ref, *out_refs):
    rows = out_refs[0].shape[2]
    for k, out_ref in enumerate(out_refs):
        row = pl.multiple_of(partner(member[0], k, len(out_refs)) * rows, rows)
        out_ref[...] = in_ref[:, :, pl.ds(row, rows), :]


def split_rows(member, nodes, group, part, width):
    count, _, order, _ = nodes.shape
    shape = (count, 2, order // group, width)
    return pl.pallas_call(
        split_kernel,
        grid_spec=pltpu.PrefetchScalarGridSpec(
            num_scalar_prefetch=1,
            grid=(1,),
            in_specs=[pl.BlockSpec((count, 2, order, width), lambda i, member: (0, 0, 0, part))],
            out_specs=[pl.BlockSpec(shape, lambda i, member: (0, 0, 0, 0))] * group,
        ),
        out_shape=[jax.ShapeDtypeStruct(shape, jnp.float32)] * group,
        name="split_rows",
    )(member, nodes)


def load_spread(member, refs, spread_ref, sems):
    copies = []
    for k, ref in enumerate(refs):
        number = ref.shape[0]
        first = partner(member, k, len(refs)) * number if len(refs) > 1 else 0
        copies.append(
            pltpu.make_async_copy(ref, spread_ref.at[pl.ds(first, number)], sems.at[k])
        )
    for copy in copies:
        copy.start()
    for copy in copies:
        copy.wait()


def spread_scratch(spread):
    count = sum(array.shape[0] for array in spread)
    return [
        pltpu.VMEM((count,) + spread[0].shape[1:], jnp.float32),
        pltpu.SemaphoreType.DMA((len(spread),)),
    ]


def plan_kernel(room, half_ref, ids_ref, send_ref, source_ref, crowded_ref, place_ref):
    half = half_ref[0]
    count = send_ref.shape[0]
    asked = source_ref.shape[0]

    def clear(i, carry):
        place_ref[i] = -1
        return carry

    def empty(i, carry):
        send_ref[i] = 0
        return carry

    lax.fori_loop(0, 2 * count, clear, 0, unroll=8)
    lax.fori_loop(0, count, empty, 0, unroll=8)

    def visit_other(q, found):
        item = ids_ref[(1 - half) * asked + q]
        here = item - half * count
        fresh = (here >= 0) & (here < count) & (place_ref[item] < 0)

        @pl.when(fresh)
        def _():
            place_ref[item] = 0
            send_ref[found] = here

        return found + fresh.astype(jnp.int32)

    def visit_own(q, found):
        item = ids_ref[half * asked + q]
        here = item - half * count
        inside = (here >= 0) & (here < count)
        known = place_ref[item]
        fresh = jnp.logical_not(inside) & (known < 0)
        there = count + room + item - (1 - half) * count
        place = jnp.where(known < 0, jnp.where(found < room, count + found, there), known)

        @pl.when(fresh)
        def _():
            place_ref[item] = place

        source_ref[q] = jnp.where(inside, here, place)
        return found + fresh.astype(jnp.int32)

    sent = lax.fori_loop(0, asked, visit_other, jnp.int32(0))
    received = lax.fori_loop(0, asked, visit_own, jnp.int32(0))
    crowded_ref[0] = (jnp.maximum(sent, received) > room).astype(jnp.int32)


def make_plan(half, ids, count, room):
    asked = ids.shape[0] // 2
    return pl.pallas_call(
        functools.partial(plan_kernel, room),
        in_specs=[SMEM] * 2,
        out_specs=[SMEM] * 3,
        out_shape=[
            jax.ShapeDtypeStruct((count,), jnp.int32),
            jax.ShapeDtypeStruct((asked,), jnp.int32),
            jax.ShapeDtypeStruct((1,), jnp.int32),
        ],
        scratch_shapes=[pltpu.SMEM((2 * count,), jnp.int32)],
        compiler_params=PARAMS,
        name="make_plan",
    )(half, ids)


def leave_kernel(send_ref, member_ref, *refs):
    *parts, out_ref, spread_ref, sems = refs
    load_spread(member_ref[0], parts, spread_ref, sems)

    def copy(i, carry):
        out_ref[i] = spread_ref[send_ref[i]]
        return carry

    lax.fori_loop(0, out_ref.shape[0], copy, 0, unroll=8)


def pick_leaving(send, member, spread, room):
    return pl.pallas_call(
        leave_kernel,
        in_specs=[SMEM, SMEM] + [ANY] * len(spread),
        out_specs=VMEM,
        out_shape=jax.ShapeDtypeStruct((room,) + spread[0].shape[1:], jnp.float32),
        scratch_shapes=spread_scratch(spread),
        compiler_params=PARAMS,
        name="pick_leaving",
    )(send, member, *spread)


def collect_kernel(source_ref, crowded_ref, spread_ref, arrived_ref, extra_ref, out_ref, sem):
    count, room = spread_ref.shape[0], arrived_ref.shape[0]

    def copy(q, carry):
        source = source_ref[q]
        near = jnp.minimum(source, count - 1)
        far = jnp.clip(source - count, 0, room - 1)
        out_ref[q] = jnp.where(source < count, spread_ref[near], arrived_ref[far])
        return carry

    lax.fori_loop(0, out_ref.shape[0], copy, 0, unroll=8)

    @pl.when(crowded_ref[0] > 0)
    def _():
        def fetch(q, carry):
            source = source_ref[q] - (count + room)

            @pl.when(source >= 0)
            def _():
                slow = pltpu.make_async_copy(extra_ref.at[source], out_ref.at[q], sem)
                slow.start()
                slow.wait()

            return carry

        lax.fori_loop(0, out_ref.shape[0], fetch, 0)


def collect(source, crowded, spread, arrived, extra):
    return pl.pallas_call(
        collect_kernel,
        in_specs=[SMEM, SMEM, VMEM, VMEM, ANY],
        out_specs=VMEM,
        out_shape=jax.ShapeDtypeStruct((source.shape[0],) + spread.shape[1:], jnp.float32),
        scratch_shapes=[pltpu.SemaphoreType.DMA],
        compiler_params=PARAMS,
        name="collect",
    )(source, crowded, spread, arrived, extra)


def scatter_kernel(parts, source_ref, flags_ref, arrived_ref, extra_ref, *refs):
    out_refs, (spread_ref, sems, sem) = refs[parts:-3], refs[-3:]
    load_spread(flags_ref[1], refs[:parts], spread_ref, sems)
    count, room = spread_ref.shape[0], arrived_ref.shape[0]
    wanted = out_refs[0].shape[0]
    for k, out_ref in enumerate(out_refs):
        base = partner(flags_ref[1], k, len(out_refs)) * wanted

        def copy(q, carry, base=base, out_ref=out_ref):
            source = source_ref[base + q]
            near = jnp.minimum(source, count - 1)
            far = jnp.clip(source - count, 0, room - 1)
            out_ref[q] = jnp.where(source < count, spread_ref[near], arrived_ref[far])
            return carry

        lax.fori_loop(0, wanted, copy, 0, unroll=4)

        @pl.when(flags_ref[0] > 0)
        def _(base=base, out_ref=out_ref):
            def fetch(q, carry):
                source = source_ref[base + q] - (count + room)

                @pl.when(source >= 0)
                def _():
                    slow = pltpu.make_async_copy(extra_ref.at[source], out_ref.at[q], sem)
                    slow.start()
                    slow.wait()

                return carry

            lax.fori_loop(0, wanted, fetch, 0)


def scatter(source, flags, spread, arrived, extra, group):
    shape = (source.shape[0] // group,) + spread[0].shape[1:]
    return pl.pallas_call(
        functools.partial(scatter_kernel, len(spread)),
        in_specs=[SMEM, SMEM, VMEM, ANY] + [ANY] * len(spread),
        out_specs=[VMEM] * group,
        out_shape=[jax.ShapeDtypeStruct(shape, jnp.float32)] * group,
        scratch_shapes=[*spread_scratch(spread), pltpu.SemaphoreType.DMA],
        compiler_params=PARAMS,
        name="scatter",
    )(source, flags, arrived, extra, *spread)


def fetch_items(nodes, ids, pairwise):
    devices = lax.axis_size("node")
    group = devices // 2
    index = lax.axis_index("node")
    half = (index // group).astype(jnp.int32).reshape(1)
    member = (index % group).astype(jnp.int32).reshape(1)
    halves = [[h * group + i for i in range(group)] for h in range(2)]
    swap = [(i, (i + group) % devices) for i in range(devices)]
    count = group * nodes.shape[0]
    width = min(LANES, nodes.shape[3])
    parts = nodes.shape[3] // width
    room = min(count, max(8, int(count * CROSS_SHARE)))
    send, source, crowded = make_plan(half, ids.reshape(-1), count, room)

    def exchange(x):
        return lax.all_to_all(x, "node", 0, 0, axis_index_groups=halves, tiled=True)

    def trade(arrays):
        got = []
        for k, array in enumerate(arrays):
            pairs = [
                (i, i // group * group + partner(i % group, k, group)) for i in range(devices)
            ]
            still = all(i == j for i, j in pairs)
            got.append(array if still else lax.ppermute(array, "node", pairs))
        return got

    def cross_all(spread):
        if len(spread) == 1:
            return lax.ppermute(spread[0], "node", swap)
        members = jnp.arange(group, dtype=jnp.int32)
        order = jnp.argsort(jnp.stack([partner(member[0], k, group) for k in range(group)]))
        every = jnp.take(jnp.stack(spread), order[members], axis=0)
        return lax.ppermute(every.reshape((count,) + every.shape[2:]), "node", swap)

    delivered = []
    for c in range(parts):
        if pairwise and c > 0:
            spread = trade(split_rows(member, nodes, group, c, width))
        else:
            cut = cut_rows(nodes, group, c, width)
            spread = exchange(cut)
            spread = [spread.reshape((count,) + spread.shape[2:])]
        leaving = pick_leaving(send, member, spread, room)
        arrived = lax.ppermute(leaving, "node", swap)
        piece = (count,) + leaving.shape[1:]
        extra = lax.cond(crowded[0] > 0, cross_all, lambda _: jnp.zeros(piece, jnp.float32), spread)
        if pairwise and c == parts - 1:
            flags = jnp.concatenate([crowded, member])
            sent = scatter(source, flags, spread, arrived, extra, group)
            delivered.append(trade(sent))
            continue
        if len(spread) > 1:
            order = [partner(member[0], k, group) for k in range(group)]
            spread = [jnp.take(jnp.stack(spread), jnp.argsort(jnp.stack(order)), axis=0)]
            spread = [spread[0].reshape((count,) + spread[0].shape[2:])]
        picked = collect(source, crowded, spread[0], arrived, extra)
        picked = picked.reshape((group, ids.shape[1]) + picked.shape[1:])
        delivered.append(exchange(picked))
    return delivered


def halves_of(x):
    high = x.astype(jnp.bfloat16)
    return high, (x - high.astype(jnp.float32)).astype(jnp.bfloat16)


def stacked(blocks):
    order = blocks[0].shape[0] * blocks[0].shape[2]
    real, imag = (
        jnp.concatenate([b[:, c].reshape(order, b.shape[-1]) for b in blocks], axis=1)
        for c in range(2)
    )
    pairs = zip(halves_of(real), halves_of(imag))
    return [
        jnp.concatenate([jnp.concatenate([r, i], axis=1), jnp.concatenate([-i, r], axis=1)], axis=0)
        for r, i in pairs
    ]


def product(left, blocks):
    left_high, left_low = halves_of(left)
    right_high, right_low = stacked(blocks)
    return jnp.dot(
        jnp.concatenate([left_high, left_high, left_low], axis=1),
        jnp.concatenate([right_high, right_low, right_high], axis=0),
        preferred_element_type=jnp.float32,
    )


def wide(ref):
    return jnp.concatenate([ref[0, 0], ref[0, 1]], axis=1)


def triple_spec(array):
    group, _, _, rows, width = array.shape
    return pl.BlockSpec((group, 3, 2, rows, width), lambda k, *scalars: (0, k, 0, 0, 0))


def multiply_kernel(which, index_ref, left_ref, *refs):
    right_refs, out_ref = refs[:-1], refs[-1]
    both = product(wide(left_ref), [ref[:, which] for ref in right_refs])
    width = out_ref.shape[-1]
    out_ref[0, 0] = both[:, :width]
    out_ref[0, 1] = both[:, width:]


def multiply(left_index, lefts, rights, which):
    order = lefts.shape[2]
    number = left_index.shape[0]
    cols = sum(right.shape[-1] for right in rights)
    return pl.pallas_call(
        functools.partial(multiply_kernel, which),
        grid_spec=pltpu.PrefetchScalarGridSpec(
            num_scalar_prefetch=1,
            grid=(number,),
            in_specs=[
                pl.BlockSpec((1, 2, order, order), lambda k, index: (index[k], 0, 0, 0)),
                *[triple_spec(right) for right in rights],
            ],
            out_specs=pl.BlockSpec((1, 2, order, cols), lambda k, index: (k, 0, 0, 0)),
        ),
        out_shape=jax.ShapeDtypeStruct((number, 2, order, cols), jnp.float32),
        compiler_params=LARGE,
        name="multiply",
    )(left_index, lefts, *rights)


def add_result(step, target, sign, both, out_ref):
    width = out_ref.shape[-1]

    @pl.when(step == 0)
    def _():
        out_ref[...] = jnp.zeros_like(out_ref)

    both = both * sign[step].astype(jnp.float32)
    row = target[step]
    out_ref[row, 0] += both[:, :width]
    out_ref[row, 1] += both[:, width:]


def finish_kernel(target, sign, left_ref, *refs):
    right_refs, out_ref = refs[:-1], refs[-1]
    both = product(wide(left_ref), [ref[:, 2] for ref in right_refs])
    add_result(pl.program_id(0), target, sign, both, out_ref)


def finish(target, sign, lefts, rights):
    order = lefts.shape[2]
    whole = (RES_COL, 2, order, sum(right.shape[-1] for right in rights))
    return pl.pallas_call(
        finish_kernel,
        grid_spec=pltpu.PrefetchScalarGridSpec(
            num_scalar_prefetch=2,
            grid=(lefts.shape[0],),
            in_specs=[
                pl.BlockSpec((1, 2, order, order), lambda k, t, s: (k, 0, 0, 0)),
                *[triple_spec(right) for right in rights],
            ],
            out_specs=pl.BlockSpec(whole, lambda k, t, s: (0, 0, 0, 0)),
        ),
        out_shape=jax.ShapeDtypeStruct(whole, jnp.float32),
        compiler_params=LARGE,
        name="finish",
    )(target, sign, lefts, *rights)


def chain_kernel(parts, member, slot, target, sign, node_ref, *refs):
    part_refs, got_refs, (out_ref, last_ref) = refs[:parts], refs[parts:-2], refs[-2:]
    for k, ref in enumerate(got_refs):
        rows = ref.shape[2]
        row = pl.multiple_of(partner(member[0], k, len(got_refs)) * rows, rows)
        for which in range(3):
            last_ref[which, 0, :, pl.ds(row, rows)] = ref[which]
    left = wide(node_ref)
    for which in range(3):
        blocks = [ref[:, which] for ref in part_refs] + [last_ref[which]]
        left = product(left, blocks)
    add_result(pl.program_id(0), target, sign, left, out_ref)


def chain(member, slot, target, sign, nodes, rights):
    order = nodes.shape[2]
    whole = (RES_COL, 2, order, order)
    *parts, got = rights
    _, _, rows, width = got[0].shape

    return pl.pallas_call(
        functools.partial(chain_kernel, len(parts)),
        grid_spec=pltpu.PrefetchScalarGridSpec(
            num_scalar_prefetch=4,
            grid=(slot.shape[0],),
            in_specs=[
                pl.BlockSpec((1, 2, order, order), lambda k, m, slot, t, s: (slot[k], 0, 0, 0)),
                *[triple_spec(part) for part in parts],
                *[pl.BlockSpec((3, 2, rows, width), lambda k, *scalars: (k, 0, 0, 0))] * len(got),
            ],
            out_specs=pl.BlockSpec(whole, lambda k, *scalars: (0, 0, 0, 0)),
            scratch_shapes=[pltpu.VMEM((3, 1, 2, order, width), jnp.float32)],
        ),
        out_shape=jax.ShapeDtypeStruct(whole, jnp.float32),
        compiler_params=CHAIN,
        name="chain",
    )(member, slot, target, sign, nodes, *parts, *got)


def all_columns(x):
    if lax.axis_size("pair") == 1:
        return x
    return lax.all_gather(x, "pair", axis=3, tiled=True)


def per_device(node_blocks, node_slot, pair_list, second_list, targets, spin_signs):
    devices = lax.axis_size("node")
    column = lax.axis_index("node")
    group = devices // 2
    node_col = node_blocks.shape[0]
    second_col = second_list.shape[0] // devices

    slots = node_slot[pair_list]
    slots = slots[second_list].reshape(devices, second_col, 4)
    pairwise = lax.axis_size("pair") == 1
    rights = fetch_items(node_blocks, slots[:, :, 1:].reshape(devices, second_col * 3), pairwise)

    own_slots = lax.dynamic_index_in_dim(slots[:, :, 0], column, 0, keepdims=False)
    own_slots = own_slots - column * node_col
    own_signs = lax.dynamic_slice_in_dim(spin_signs, column * second_col, second_col, 0)
    own_targets = lax.dynamic_slice_in_dim(targets, column * second_col, second_col, 0)
    own_targets = own_targets - column * RES_COL

    if pairwise:
        member = (column % group).astype(jnp.int32).reshape(1)
        return chain(member, own_slots, own_targets, own_signs, node_blocks, rights)
    same = jnp.arange(second_col, dtype=jnp.int32)
    products = multiply(own_slots, all_columns(node_blocks), rights, 0)
    longer = multiply(same, all_columns(products), rights, 1)
    return finish(own_targets, own_signs, all_columns(longer), rights)


def solution(mesh):
    placed = (P(("cfg", "node"), None, None, "pair"), P(), P(), P(), P(), P())

    return jax.shard_map(
        per_device,
        mesh=mesh,
        in_specs=placed,
        out_specs=P(("cfg", "node"), None, None, "pair"),
        check_vma=False,
    )
```

```python
import functools

import jax
import jax.numpy as jnp
from jax import lax
from jax.experimental import pallas as pl
from jax.experimental.pallas import tpu as pltpu
from jax.sharding import PartitionSpec as P


RES_COL = 2
LANES = 128
CROSS_SHARE = 29 / 64
ANY = pl.BlockSpec(memory_space=pl.ANY)
HBM = pl.BlockSpec(memory_space=pltpu.HBM)
SMEM = pl.BlockSpec(memory_space=pltpu.SMEM)
VMEM = pl.BlockSpec(memory_space=pltpu.VMEM)
PARAMS = pltpu.CompilerParams(vmem_limit_bytes=24 * 1024 * 1024)
LARGE = pltpu.CompilerParams(vmem_limit_bytes=56 * 1024 * 1024)
CHAIN = pltpu.CompilerParams(vmem_limit_bytes=44 * 1024 * 1024)


def cut_kernel(in_ref, out_ref):
    rows = out_ref.shape[3]
    for j in range(out_ref.shape[0]):
        out_ref[j] = in_ref[:, :, j * rows : (j + 1) * rows, :]


def cut_rows(nodes, group, part, width):
    count, _, order, _ = nodes.shape
    rows = order // group
    steps = 2 if group % 2 == 0 else 1
    return pl.pallas_call(
        cut_kernel,
        grid=(steps,),
        in_specs=[pl.BlockSpec((count, 2, order // steps, width), lambda i: (0, 0, i, part))],
        out_specs=pl.BlockSpec((group // steps, count, 2, rows, width), lambda i: (i, 0, 0, 0, 0)),
        out_shape=jax.ShapeDtypeStruct((group, count, 2, rows, width), jnp.float32),
        name="cut_rows",
    )(nodes)


def partner(index, k, group):
    return index ^ k if group & (group - 1) == 0 else (k - index + group) % group


def split_kernel(member, in_ref, *out_refs):
    rows = out_refs[0].shape[2]
    for k, out_ref in enumerate(out_refs):
        row = pl.multiple_of(partner(member[0], k, len(out_refs)) * rows, rows)
        out_ref[...] = in_ref[:, :, pl.ds(row, rows), :]


def split_rows(member, nodes, group, part, width):
    count, _, order, _ = nodes.shape
    shape = (count, 2, order // group, width)
    return pl.pallas_call(
        split_kernel,
        grid_spec=pltpu.PrefetchScalarGridSpec(
            num_scalar_prefetch=1,
            grid=(1,),
            in_specs=[pl.BlockSpec((count, 2, order, width), lambda i, member: (0, 0, 0, part))],
            out_specs=[pl.BlockSpec(shape, lambda i, member: (0, 0, 0, 0))] * group,
        ),
        out_shape=[jax.ShapeDtypeStruct(shape, jnp.float32)] * group,
        name="split_rows",
    )(member, nodes)


def load_spread(member, refs, spread_ref):
    for k, ref in enumerate(refs):
        number = ref.shape[0]
        spread_ref[pl.ds(partner(member, k, len(refs)) * number, number)] = ref[...]


def spread_scratch(spread):
    count = sum(array.shape[0] for array in spread)
    return [pltpu.VMEM((count,) + spread[0].shape[1:], jnp.float32)] if len(spread) > 1 else []


def plan_kernel(room, half_ref, ids_ref, send_ref, source_ref, crowded_ref, place_ref):
    half = half_ref[0]
    count = send_ref.shape[0]
    asked = source_ref.shape[0]

    def clear(i, carry):
        place_ref[i] = -1
        return carry

    def empty(i, carry):
        send_ref[i] = 0
        return carry

    lax.fori_loop(0, 2 * count, clear, 0, unroll=8)
    lax.fori_loop(0, count, empty, 0, unroll=8)

    def visit_other(q, found):
        item = ids_ref[(1 - half) * asked + q]
        here = item - half * count
        fresh = (here >= 0) & (here < count) & (place_ref[item] < 0)

        @pl.when(fresh)
        def _():
            place_ref[item] = 0
            send_ref[found] = here

        return found + fresh.astype(jnp.int32)

    def visit_own(q, found):
        item = ids_ref[half * asked + q]
        here = item - half * count
        inside = (here >= 0) & (here < count)
        known = place_ref[item]
        fresh = jnp.logical_not(inside) & (known < 0)
        there = count + room + item - (1 - half) * count
        place = jnp.where(known < 0, jnp.where(found < room, count + found, there), known)

        @pl.when(fresh)
        def _():
            place_ref[item] = place

        source_ref[q] = jnp.where(inside, here, place)
        return found + fresh.astype(jnp.int32)

    sent = lax.fori_loop(0, asked, visit_other, jnp.int32(0))
    received = lax.fori_loop(0, asked, visit_own, jnp.int32(0))
    crowded_ref[0] = (jnp.maximum(sent, received) > room).astype(jnp.int32)


def make_plan(half, ids, count, room):
    asked = ids.shape[0] // 2
    return pl.pallas_call(
        functools.partial(plan_kernel, room),
        in_specs=[SMEM] * 2,
        out_specs=[SMEM] * 3,
        out_shape=[
            jax.ShapeDtypeStruct((count,), jnp.int32),
            jax.ShapeDtypeStruct((asked,), jnp.int32),
            jax.ShapeDtypeStruct((1,), jnp.int32),
        ],
        scratch_shapes=[pltpu.SMEM((2 * count,), jnp.int32)],
        compiler_params=PARAMS,
        name="make_plan",
    )(half, ids)


def leave_kernel(send_ref, member_ref, *refs):
    if len(refs) == 2:
        spread_ref, out_ref = refs
    else:
        *parts, out_ref, spread_ref = refs
        load_spread(member_ref[0], parts, spread_ref)

    def copy(i, carry):
        out_ref[i] = spread_ref[send_ref[i]]
        return carry

    lax.fori_loop(0, out_ref.shape[0], copy, 0, unroll=8)


def pick_leaving(send, member, spread, room):
    return pl.pallas_call(
        leave_kernel,
        in_specs=[SMEM, SMEM] + [VMEM] * len(spread),
        out_specs=VMEM,
        out_shape=jax.ShapeDtypeStruct((room,) + spread[0].shape[1:], jnp.float32),
        scratch_shapes=spread_scratch(spread),
        compiler_params=PARAMS,
        name="pick_leaving",
    )(send, member, *spread)


def collect_kernel(source_ref, crowded_ref, spread_ref, arrived_ref, extra_ref, out_ref, sem):
    count, room = spread_ref.shape[0], arrived_ref.shape[0]

    def copy(q, carry):
        source = source_ref[q]
        near = jnp.minimum(source, count - 1)
        far = jnp.clip(source - count, 0, room - 1)
        out_ref[q] = jnp.where(source < count, spread_ref[near], arrived_ref[far])
        return carry

    lax.fori_loop(0, out_ref.shape[0], copy, 0, unroll=8)

    @pl.when(crowded_ref[0] > 0)
    def _():
        def fetch(q, carry):
            source = source_ref[q] - (count + room)

            @pl.when(source >= 0)
            def _():
                slow = pltpu.make_async_copy(extra_ref.at[source], out_ref.at[q], sem)
                slow.start()
                slow.wait()

            return carry

        lax.fori_loop(0, out_ref.shape[0], fetch, 0)


def collect(source, crowded, spread, arrived, extra):
    return pl.pallas_call(
        collect_kernel,
        in_specs=[SMEM, SMEM, VMEM, VMEM, ANY],
        out_specs=VMEM,
        out_shape=jax.ShapeDtypeStruct((source.shape[0],) + spread.shape[1:], jnp.float32),
        scratch_shapes=[pltpu.SemaphoreType.DMA],
        compiler_params=PARAMS,
        name="collect",
    )(source, crowded, spread, arrived, extra)


def scatter_kernel(parts, source_ref, flags_ref, arrived_ref, extra_ref, *refs):
    if parts == 1:
        spread_ref, *out_refs, sem = refs
    else:
        out_refs, (spread_ref, sem) = refs[parts:-2], refs[-2:]
        load_spread(flags_ref[1], refs[:parts], spread_ref)
    count, room = spread_ref.shape[0], arrived_ref.shape[0]
    wanted = out_refs[0].shape[0]
    for k, out_ref in enumerate(out_refs):
        base = partner(flags_ref[1], k, len(out_refs)) * wanted

        def copy(q, carry, base=base, out_ref=out_ref):
            source = source_ref[base + q]
            near = jnp.minimum(source, count - 1)
            far = jnp.clip(source - count, 0, room - 1)
            out_ref[q] = jnp.where(source < count, spread_ref[near], arrived_ref[far])
            return carry

        lax.fori_loop(0, wanted, copy, 0, unroll=4)

        @pl.when(flags_ref[0] > 0)
        def _(base=base, out_ref=out_ref):
            def fetch(q, carry):
                source = source_ref[base + q] - (count + room)

                @pl.when(source >= 0)
                def _():
                    slow = pltpu.make_async_copy(extra_ref.at[source], out_ref.at[q], sem)
                    slow.start()
                    slow.wait()

                return carry

            lax.fori_loop(0, wanted, fetch, 0)


def scatter(source, flags, spread, arrived, extra, group):
    shape = (source.shape[0] // group,) + spread[0].shape[1:]
    return pl.pallas_call(
        functools.partial(scatter_kernel, len(spread)),
        in_specs=[SMEM, SMEM, VMEM, ANY] + [VMEM] * len(spread),
        out_specs=[VMEM] * group,
        out_shape=[jax.ShapeDtypeStruct(shape, jnp.float32)] * group,
        scratch_shapes=[*spread_scratch(spread), pltpu.SemaphoreType.DMA],
        compiler_params=PARAMS,
        name="scatter",
    )(source, flags, arrived, extra, *spread)


def fetch_items(nodes, ids, pairwise):
    devices = lax.axis_size("node")
    group = devices // 2
    index = lax.axis_index("node")
    half = (index // group).astype(jnp.int32).reshape(1)
    member = (index % group).astype(jnp.int32).reshape(1)
    halves = [[h * group + i for i in range(group)] for h in range(2)]
    swap = [(i, (i + group) % devices) for i in range(devices)]
    count = group * nodes.shape[0]
    width = min(LANES, nodes.shape[3])
    parts = nodes.shape[3] // width
    room = min(count, max(8, int(count * CROSS_SHARE)))
    send, source, crowded = make_plan(half, ids.reshape(-1), count, room)

    def exchange(x):
        return lax.all_to_all(x, "node", 0, 0, axis_index_groups=halves, tiled=True)

    def trade(arrays):
        got = []
        for k, array in enumerate(arrays):
            pairs = [
                (i, i // group * group + partner(i % group, k, group)) for i in range(devices)
            ]
            still = all(i == j for i, j in pairs)
            got.append(array if still else lax.ppermute(array, "node", pairs))
        return got

    def cross_all(spread):
        if len(spread) == 1:
            return lax.ppermute(spread[0], "node", swap)
        members = jnp.arange(group, dtype=jnp.int32)
        order = jnp.argsort(jnp.stack([partner(member[0], k, group) for k in range(group)]))
        every = jnp.take(jnp.stack(spread), order[members], axis=0)
        return lax.ppermute(every.reshape((count,) + every.shape[2:]), "node", swap)

    delivered = []
    for c in range(parts):
        if pairwise and c > 0:
            spread = trade(split_rows(member, nodes, group, c, width))
        else:
            cut = cut_rows(nodes, group, c, width)
            spread = exchange(cut)
            spread = [spread.reshape((count,) + spread.shape[2:])]
        leaving = pick_leaving(send, member, spread, room)
        arrived = lax.ppermute(leaving, "node", swap)
        piece = (count,) + leaving.shape[1:]
        extra = lax.cond(crowded[0] > 0, cross_all, lambda _: jnp.zeros(piece, jnp.float32), spread)
        if pairwise and c == parts - 1:
            flags = jnp.concatenate([crowded, member])
            sent = scatter(source, flags, spread, arrived, extra, group)
            delivered.append(trade(sent))
            continue
        if len(spread) > 1:
            order = [partner(member[0], k, group) for k in range(group)]
            spread = [jnp.take(jnp.stack(spread), jnp.argsort(jnp.stack(order)), axis=0)]
            spread = [spread[0].reshape((count,) + spread[0].shape[2:])]
        picked = collect(source, crowded, spread[0], arrived, extra)
        picked = picked.reshape((group, ids.shape[1]) + picked.shape[1:])
        delivered.append(exchange(picked))
    return delivered


def halves_of(x):
    high = x.astype(jnp.bfloat16)
    return high, (x - high.astype(jnp.float32)).astype(jnp.bfloat16)


def stacked(blocks):
    order = blocks[0].shape[0] * blocks[0].shape[2]
    real, imag = (
        jnp.concatenate([b[:, c].reshape(order, b.shape[-1]) for b in blocks], axis=1)
        for c in range(2)
    )
    pairs = zip(halves_of(real), halves_of(imag))
    return [
        jnp.concatenate([jnp.concatenate([r, i], axis=1), jnp.concatenate([-i, r], axis=1)], axis=0)
        for r, i in pairs
    ]


def product(left, blocks):
    left_high, left_low = halves_of(left)
    right_high, right_low = stacked(blocks)
    return jnp.dot(
        jnp.concatenate([left_high, left_high, left_low], axis=1),
        jnp.concatenate([right_high, right_low, right_high], axis=0),
        preferred_element_type=jnp.float32,
    )


def wide(ref):
    return jnp.concatenate([ref[0, 0], ref[0, 1]], axis=1)


def triple_spec(array):
    group, _, _, rows, width = array.shape
    return pl.BlockSpec((group, 3, 2, rows, width), lambda k, *scalars: (0, k, 0, 0, 0))


def multiply_kernel(which, index_ref, left_ref, *refs):
    right_refs, out_ref = refs[:-1], refs[-1]
    both = product(wide(left_ref), [ref[:, which] for ref in right_refs])
    width = out_ref.shape[-1]
    out_ref[0, 0] = both[:, :width]
    out_ref[0, 1] = both[:, width:]


def multiply(left_index, lefts, rights, which):
    order = lefts.shape[2]
    number = left_index.shape[0]
    cols = sum(right.shape[-1] for right in rights)
    return pl.pallas_call(
        functools.partial(multiply_kernel, which),
        grid_spec=pltpu.PrefetchScalarGridSpec(
            num_scalar_prefetch=1,
            grid=(number,),
            in_specs=[
                pl.BlockSpec((1, 2, order, order), lambda k, index: (index[k], 0, 0, 0)),
                *[triple_spec(right) for right in rights],
            ],
            out_specs=pl.BlockSpec((1, 2, order, cols), lambda k, index: (k, 0, 0, 0)),
        ),
        out_shape=jax.ShapeDtypeStruct((number, 2, order, cols), jnp.float32),
        compiler_params=LARGE,
        name="multiply",
    )(left_index, lefts, *rights)


def add_result(step, target, sign, both, out_ref):
    width = out_ref.shape[-1]

    @pl.when(step == 0)
    def _():
        out_ref[...] = jnp.zeros_like(out_ref)

    both = both * sign[step].astype(jnp.float32)
    row = target[step]
    out_ref[row, 0] += both[:, :width]
    out_ref[row, 1] += both[:, width:]


def finish_kernel(target, sign, left_ref, *refs):
    right_refs, out_ref = refs[:-1], refs[-1]
    both = product(wide(left_ref), [ref[:, 2] for ref in right_refs])
    add_result(pl.program_id(0), target, sign, both, out_ref)


def finish(target, sign, lefts, rights):
    order = lefts.shape[2]
    whole = (RES_COL, 2, order, sum(right.shape[-1] for right in rights))
    return pl.pallas_call(
        finish_kernel,
        grid_spec=pltpu.PrefetchScalarGridSpec(
            num_scalar_prefetch=2,
            grid=(lefts.shape[0],),
            in_specs=[
                pl.BlockSpec((1, 2, order, order), lambda k, t, s: (k, 0, 0, 0)),
                *[triple_spec(right) for right in rights],
            ],
            out_specs=pl.BlockSpec(whole, lambda k, t, s: (0, 0, 0, 0)),
        ),
        out_shape=jax.ShapeDtypeStruct(whole, jnp.float32),
        compiler_params=LARGE,
        name="finish",
    )(target, sign, lefts, *rights)


def chain_kernel(parts, member, slot, target, sign, node_ref, *refs):
    part_refs, got_refs, (out_ref, last_ref) = refs[:parts], refs[parts:-2], refs[-2:]
    for k, ref in enumerate(got_refs):
        rows = ref.shape[2]
        row = pl.multiple_of(partner(member[0], k, len(got_refs)) * rows, rows)
        for which in range(3):
            last_ref[which, 0, :, pl.ds(row, rows)] = ref[which]
    left = wide(node_ref)
    for which in range(3):
        blocks = [ref[:, which] for ref in part_refs] + [last_ref[which]]
        left = product(left, blocks)
    add_result(pl.program_id(0), target, sign, left, out_ref)


def chain(member, slot, target, sign, nodes, rights):
    order = nodes.shape[2]
    whole = (RES_COL, 2, order, order)
    *parts, got = rights
    _, _, rows, width = got[0].shape

    return pl.pallas_call(
        functools.partial(chain_kernel, len(parts)),
        grid_spec=pltpu.PrefetchScalarGridSpec(
            num_scalar_prefetch=4,
            grid=(slot.shape[0],),
            in_specs=[
                pl.BlockSpec((1, 2, order, order), lambda k, m, slot, t, s: (slot[k], 0, 0, 0)),
                *[triple_spec(part) for part in parts],
                *[pl.BlockSpec((3, 2, rows, width), lambda k, *scalars: (k, 0, 0, 0))] * len(got),
            ],
            out_specs=pl.BlockSpec(whole, lambda k, *scalars: (0, 0, 0, 0)),
            scratch_shapes=[pltpu.VMEM((3, 1, 2, order, width), jnp.float32)],
        ),
        out_shape=jax.ShapeDtypeStruct(whole, jnp.float32),
        compiler_params=CHAIN,
        name="chain",
    )(member, slot, target, sign, nodes, *parts, *got)


def all_columns(x):
    if lax.axis_size("pair") == 1:
        return x
    return lax.all_gather(x, "pair", axis=3, tiled=True)


def per_device(node_blocks, node_slot, pair_list, second_list, targets, spin_signs):
    devices = lax.axis_size("node")
    column = lax.axis_index("node")
    group = devices // 2
    node_col = node_blocks.shape[0]
    second_col = second_list.shape[0] // devices

    slots = node_slot[pair_list]
    slots = slots[second_list].reshape(devices, second_col, 4)
    pairwise = lax.axis_size("pair") == 1
    rights = fetch_items(node_blocks, slots[:, :, 1:].reshape(devices, second_col * 3), pairwise)

    own_slots = lax.dynamic_index_in_dim(slots[:, :, 0], column, 0, keepdims=False)
    own_slots = own_slots - column * node_col
    own_signs = lax.dynamic_slice_in_dim(spin_signs, column * second_col, second_col, 0)
    own_targets = lax.dynamic_slice_in_dim(targets, column * second_col, second_col, 0)
    own_targets = own_targets - column * RES_COL

    if pairwise:
        member = (column % group).astype(jnp.int32).reshape(1)
        return chain(member, own_slots, own_targets, own_signs, node_blocks, rights)
    same = jnp.arange(second_col, dtype=jnp.int32)
    products = multiply(own_slots, all_columns(node_blocks), rights, 0)
    longer = multiply(same, all_columns(products), rights, 1)
    return finish(own_targets, own_signs, all_columns(longer), rights)


def solution(mesh):
    placed = (P(("cfg", "node"), None, None, "pair"), P(), P(), P(), P(), P())

    return jax.shard_map(
        per_device,
        mesh=mesh,
        in_specs=placed,
        out_specs=P(("cfg", "node"), None, None, "pair"),
        check_vma=False,
    )
```

```python
import functools

import jax
import jax.numpy as jnp
from jax import lax
from jax.experimental import pallas as pl
from jax.experimental.pallas import tpu as pltpu
from jax.sharding import PartitionSpec as P


RES_COL = 2
LANES = 128
CROSS_SHARE = 29 / 64
ANY = pl.BlockSpec(memory_space=pl.ANY)
HBM = pl.BlockSpec(memory_space=pltpu.HBM)
SMEM = pl.BlockSpec(memory_space=pltpu.SMEM)
VMEM = pl.BlockSpec(memory_space=pltpu.VMEM)
PARAMS = pltpu.CompilerParams(vmem_limit_bytes=24 * 1024 * 1024)
LARGE = pltpu.CompilerParams(vmem_limit_bytes=56 * 1024 * 1024)
CHAIN = pltpu.CompilerParams(vmem_limit_bytes=44 * 1024 * 1024)


def cut_kernel(in_ref, out_ref):
    rows = out_ref.shape[3]
    for j in range(out_ref.shape[0]):
        out_ref[j] = in_ref[:, :, j * rows : (j + 1) * rows, :]


def cut_rows(nodes, group, part, width):
    count, _, order, _ = nodes.shape
    rows = order // group
    steps = 2 if group % 2 == 0 else 1
    return pl.pallas_call(
        cut_kernel,
        grid=(steps,),
        in_specs=[pl.BlockSpec((count, 2, order // steps, width), lambda i: (0, 0, i, part))],
        out_specs=pl.BlockSpec((group // steps, count, 2, rows, width), lambda i: (i, 0, 0, 0, 0)),
        out_shape=jax.ShapeDtypeStruct((group, count, 2, rows, width), jnp.float32),
        name="cut_rows",
    )(nodes)


def partner(index, k, group):
    return index ^ k if group & (group - 1) == 0 else (k - index + group) % group


def split_kernel(member, in_ref, *out_refs):
    rows = out_refs[0].shape[2]
    for k, out_ref in enumerate(out_refs):
        row = pl.multiple_of(partner(member[0], k, len(out_refs)) * rows, rows)
        out_ref[...] = in_ref[:, :, pl.ds(row, rows), :]


def split_rows(member, nodes, group, part, width):
    count, _, order, _ = nodes.shape
    shape = (count, 2, order // group, width)
    return pl.pallas_call(
        split_kernel,
        grid_spec=pltpu.PrefetchScalarGridSpec(
            num_scalar_prefetch=1,
            grid=(1,),
            in_specs=[pl.BlockSpec((count, 2, order, width), lambda i, member: (0, 0, 0, part))],
            out_specs=[pl.BlockSpec(shape, lambda i, member: (0, 0, 0, 0))] * group,
        ),
        out_shape=[jax.ShapeDtypeStruct(shape, jnp.float32)] * group,
        name="split_rows",
    )(member, nodes)


def load_spread(member, refs, spread_ref):
    for k, ref in enumerate(refs):
        number = ref.shape[0]
        spread_ref[pl.ds(partner(member, k, len(refs)) * number, number)] = ref[...]


def spread_scratch(spread):
    count = sum(array.shape[0] for array in spread)
    return [pltpu.VMEM((count,) + spread[0].shape[1:], jnp.float32)] if len(spread) > 1 else []


def plan_kernel(room, half_ref, ids_ref, send_ref, source_ref, crowded_ref, place_ref):
    half = half_ref[0]
    count = send_ref.shape[0]
    asked = source_ref.shape[0]

    def clear(i, carry):
        place_ref[i] = -1
        return carry

    def empty(i, carry):
        send_ref[i] = 0
        return carry

    lax.fori_loop(0, 2 * count, clear, 0, unroll=8)
    lax.fori_loop(0, count, empty, 0, unroll=8)

    def visit_other(q, found):
        item = ids_ref[(1 - half) * asked + q]
        here = item - half * count
        fresh = (here >= 0) & (here < count) & (place_ref[item] < 0)

        @pl.when(fresh)
        def _():
            place_ref[item] = 0
            send_ref[found] = here

        return found + fresh.astype(jnp.int32)

    def visit_own(q, found):
        item = ids_ref[half * asked + q]
        here = item - half * count
        inside = (here >= 0) & (here < count)
        known = place_ref[item]
        fresh = jnp.logical_not(inside) & (known < 0)
        there = count + room + item - (1 - half) * count
        place = jnp.where(known < 0, jnp.where(found < room, count + found, there), known)

        @pl.when(fresh)
        def _():
            place_ref[item] = place

        source_ref[q] = jnp.where(inside, here, place)
        return found + fresh.astype(jnp.int32)

    sent = lax.fori_loop(0, asked, visit_other, jnp.int32(0))
    received = lax.fori_loop(0, asked, visit_own, jnp.int32(0))
    crowded_ref[0] = (jnp.maximum(sent, received) > room).astype(jnp.int32)


def make_plan(half, ids, count, room):
    asked = ids.shape[0] // 2
    return pl.pallas_call(
        functools.partial(plan_kernel, room),
        in_specs=[SMEM] * 2,
        out_specs=[SMEM] * 3,
        out_shape=[
            jax.ShapeDtypeStruct((count,), jnp.int32),
            jax.ShapeDtypeStruct((asked,), jnp.int32),
            jax.ShapeDtypeStruct((1,), jnp.int32),
        ],
        scratch_shapes=[pltpu.SMEM((2 * count,), jnp.int32)],
        compiler_params=PARAMS,
        name="make_plan",
    )(half, ids)


def leave_kernel(send_ref, member_ref, *refs):
    if len(refs) == 2:
        spread_ref, out_ref = refs
    else:
        *parts, out_ref, spread_ref = refs
        load_spread(member_ref[0], parts, spread_ref)

    def copy(i, carry):
        out_ref[i] = spread_ref[send_ref[i]]
        return carry

    lax.fori_loop(0, out_ref.shape[0], copy, 0, unroll=8)


def pick_leaving(send, member, spread, room):
    return pl.pallas_call(
        leave_kernel,
        in_specs=[SMEM, SMEM] + [VMEM] * len(spread),
        out_specs=VMEM,
        out_shape=jax.ShapeDtypeStruct((room,) + spread[0].shape[1:], jnp.float32),
        scratch_shapes=spread_scratch(spread),
        compiler_params=PARAMS,
        name="pick_leaving",
    )(send, member, *spread)


def collect_kernel(source_ref, crowded_ref, spread_ref, arrived_ref, extra_ref, out_ref, sem):
    count, room = spread_ref.shape[0], arrived_ref.shape[0]

    def copy(q, carry):
        source = source_ref[q]
        near = jnp.minimum(source, count - 1)
        far = jnp.clip(source - count, 0, room - 1)
        out_ref[q] = jnp.where(source < count, spread_ref[near], arrived_ref[far])
        return carry

    lax.fori_loop(0, out_ref.shape[0], copy, 0, unroll=8)

    @pl.when(crowded_ref[0] > 0)
    def _():
        def fetch(q, carry):
            source = source_ref[q] - (count + room)

            @pl.when(source >= 0)
            def _():
                slow = pltpu.make_async_copy(extra_ref.at[source], out_ref.at[q], sem)
                slow.start()
                slow.wait()

            return carry

        lax.fori_loop(0, out_ref.shape[0], fetch, 0)


def collect(source, crowded, spread, arrived, extra):
    return pl.pallas_call(
        collect_kernel,
        in_specs=[SMEM, SMEM, VMEM, VMEM, ANY],
        out_specs=VMEM,
        out_shape=jax.ShapeDtypeStruct((source.shape[0],) + spread.shape[1:], jnp.float32),
        scratch_shapes=[pltpu.SemaphoreType.DMA],
        compiler_params=PARAMS,
        name="collect",
    )(source, crowded, spread, arrived, extra)


def scatter_kernel(parts, source_ref, flags_ref, arrived_ref, extra_ref, *refs):
    if parts == 1:
        spread_ref, *out_refs, sem = refs
    else:
        out_refs, (spread_ref, sem) = refs[parts:-2], refs[-2:]
        load_spread(flags_ref[1], refs[:parts], spread_ref)
    count, room = spread_ref.shape[0], arrived_ref.shape[0]
    wanted = out_refs[0].shape[0]
    for k, out_ref in enumerate(out_refs):
        base = partner(flags_ref[1], k, len(out_refs)) * wanted

        def copy(q, carry, base=base, out_ref=out_ref):
            source = source_ref[base + q]
            near = jnp.minimum(source, count - 1)
            far = jnp.clip(source - count, 0, room - 1)
            out_ref[q] = jnp.where(source < count, spread_ref[near], arrived_ref[far])
            return carry

        lax.fori_loop(0, wanted, copy, 0, unroll=4)

        @pl.when(flags_ref[0] > 0)
        def _(base=base, out_ref=out_ref):
            def fetch(q, carry):
                source = source_ref[base + q] - (count + room)

                @pl.when(source >= 0)
                def _():
                    slow = pltpu.make_async_copy(extra_ref.at[source], out_ref.at[q], sem)
                    slow.start()
                    slow.wait()

                return carry

            lax.fori_loop(0, wanted, fetch, 0)


def scatter(source, flags, spread, arrived, extra, group):
    shape = (source.shape[0] // group,) + spread[0].shape[1:]
    return pl.pallas_call(
        functools.partial(scatter_kernel, len(spread)),
        in_specs=[SMEM, SMEM, VMEM, ANY] + [VMEM] * len(spread),
        out_specs=[VMEM] * group,
        out_shape=[jax.ShapeDtypeStruct(shape, jnp.float32)] * group,
        scratch_shapes=[*spread_scratch(spread), pltpu.SemaphoreType.DMA],
        compiler_params=PARAMS,
        name="scatter",
    )(source, flags, arrived, extra, *spread)


def fetch_items(nodes, ids, pairwise):
    devices = lax.axis_size("node")
    group = devices // 2
    index = lax.axis_index("node")
    half = (index // group).astype(jnp.int32).reshape(1)
    member = (index % group).astype(jnp.int32).reshape(1)
    halves = [[h * group + i for i in range(group)] for h in range(2)]
    swap = [(i, (i + group) % devices) for i in range(devices)]
    count = group * nodes.shape[0]
    width = min(LANES, nodes.shape[3])
    parts = nodes.shape[3] // width
    room = min(count, max(8, int(count * CROSS_SHARE)))
    send, source, crowded = make_plan(half, ids.reshape(-1), count, room)

    def exchange(x):
        return lax.all_to_all(x, "node", 0, 0, axis_index_groups=halves, tiled=True)

    def trade(arrays):
        got = []
        for k, array in enumerate(arrays):
            pairs = [
                (i, i // group * group + partner(i % group, k, group)) for i in range(devices)
            ]
            still = all(i == j for i, j in pairs)
            got.append(array if still else lax.ppermute(array, "node", pairs))
        return got

    def cross_all(spread):
        if len(spread) == 1:
            return lax.ppermute(spread[0], "node", swap)
        members = jnp.arange(group, dtype=jnp.int32)
        order = jnp.argsort(jnp.stack([partner(member[0], k, group) for k in range(group)]))
        every = jnp.take(jnp.stack(spread), order[members], axis=0)
        return lax.ppermute(every.reshape((count,) + every.shape[2:]), "node", swap)

    delivered = []
    for c in range(parts):
        if pairwise and c > 0:
            spread = trade(split_rows(member, nodes, group, c, width))
        else:
            cut = cut_rows(nodes, group, c, width)
            spread = exchange(cut)
            spread = [spread.reshape((count,) + spread.shape[2:])]
        leaving = pick_leaving(send, member, spread, room)
        arrived = lax.ppermute(leaving, "node", swap)
        piece = (count,) + leaving.shape[1:]
        extra = lax.cond(crowded[0] > 0, cross_all, lambda _: jnp.zeros(piece, jnp.float32), spread)
        if pairwise:
            flags = jnp.concatenate([crowded, member])
            sent = scatter(source, flags, spread, arrived, extra, group)
            delivered.append(trade(sent))
            continue
        picked = collect(source, crowded, spread[0], arrived, extra)
        picked = picked.reshape((group, ids.shape[1]) + picked.shape[1:])
        delivered.append(exchange(picked))
    return delivered


def halves_of(x):
    high = x.astype(jnp.bfloat16)
    return high, (x - high.astype(jnp.float32)).astype(jnp.bfloat16)


def stacked(blocks):
    order = blocks[0].shape[0] * blocks[0].shape[2]
    real, imag = (
        jnp.concatenate([b[:, c].reshape(order, b.shape[-1]) for b in blocks], axis=1)
        for c in range(2)
    )
    pairs = zip(halves_of(real), halves_of(imag))
    return [
        jnp.concatenate([jnp.concatenate([r, i], axis=1), jnp.concatenate([-i, r], axis=1)], axis=0)
        for r, i in pairs
    ]


def product(left, blocks):
    left_high, left_low = halves_of(left)
    right_high, right_low = stacked(blocks)
    return jnp.dot(
        jnp.concatenate([left_high, left_high, left_low], axis=1),
        jnp.concatenate([right_high, right_low, right_high], axis=0),
        preferred_element_type=jnp.float32,
    )


def wide(ref):
    return jnp.concatenate([ref[0, 0], ref[0, 1]], axis=1)


def triple_spec(array):
    group, _, _, rows, width = array.shape
    return pl.BlockSpec((group, 3, 2, rows, width), lambda k, *scalars: (0, k, 0, 0, 0))


def multiply_kernel(which, index_ref, left_ref, *refs):
    right_refs, out_ref = refs[:-1], refs[-1]
    both = product(wide(left_ref), [ref[:, which] for ref in right_refs])
    width = out_ref.shape[-1]
    out_ref[0, 0] = both[:, :width]
    out_ref[0, 1] = both[:, width:]


def multiply(left_index, lefts, rights, which):
    order = lefts.shape[2]
    number = left_index.shape[0]
    cols = sum(right.shape[-1] for right in rights)
    return pl.pallas_call(
        functools.partial(multiply_kernel, which),
        grid_spec=pltpu.PrefetchScalarGridSpec(
            num_scalar_prefetch=1,
            grid=(number,),
            in_specs=[
                pl.BlockSpec((1, 2, order, order), lambda k, index: (index[k], 0, 0, 0)),
                *[triple_spec(right) for right in rights],
            ],
            out_specs=pl.BlockSpec((1, 2, order, cols), lambda k, index: (k, 0, 0, 0)),
        ),
        out_shape=jax.ShapeDtypeStruct((number, 2, order, cols), jnp.float32),
        compiler_params=LARGE,
        name="multiply",
    )(left_index, lefts, *rights)


def add_result(step, target, sign, both, out_ref):
    width = out_ref.shape[-1]

    @pl.when(step == 0)
    def _():
        out_ref[...] = jnp.zeros_like(out_ref)

    both = both * sign[step].astype(jnp.float32)
    row = target[step]
    out_ref[row, 0] += both[:, :width]
    out_ref[row, 1] += both[:, width:]


def finish_kernel(target, sign, left_ref, *refs):
    right_refs, out_ref = refs[:-1], refs[-1]
    both = product(wide(left_ref), [ref[:, 2] for ref in right_refs])
    add_result(pl.program_id(0), target, sign, both, out_ref)


def finish(target, sign, lefts, rights):
    order = lefts.shape[2]
    whole = (RES_COL, 2, order, sum(right.shape[-1] for right in rights))
    return pl.pallas_call(
        finish_kernel,
        grid_spec=pltpu.PrefetchScalarGridSpec(
            num_scalar_prefetch=2,
            grid=(lefts.shape[0],),
            in_specs=[
                pl.BlockSpec((1, 2, order, order), lambda k, t, s: (k, 0, 0, 0)),
                *[triple_spec(right) for right in rights],
            ],
            out_specs=pl.BlockSpec(whole, lambda k, t, s: (0, 0, 0, 0)),
        ),
        out_shape=jax.ShapeDtypeStruct(whole, jnp.float32),
        compiler_params=LARGE,
        name="finish",
    )(target, sign, lefts, *rights)


def chain_kernel(parts, member, slot, target, sign, node_ref, *refs):
    got_refs, (out_ref, right_ref) = refs[:-2], refs[-2:]
    group = len(got_refs) // parts
    for i, ref in enumerate(got_refs):
        rows = ref.shape[2]
        row = pl.multiple_of(partner(member[0], i % group, group) * rows, rows)
        for which in range(3):
            right_ref[i // group, which, 0, :, pl.ds(row, rows)] = ref[which]
    left = wide(node_ref)
    for which in range(3):
        left = product(left, [right_ref[part, which] for part in range(parts)])
    add_result(pl.program_id(0), target, sign, left, out_ref)


def chain(member, slot, target, sign, nodes, rights):
    order = nodes.shape[2]
    whole = (RES_COL, 2, order, order)
    parts = len(rights)
    got = [array for right in rights for array in right]
    _, _, rows, width = got[0].shape

    return pl.pallas_call(
        functools.partial(chain_kernel, parts),
        grid_spec=pltpu.PrefetchScalarGridSpec(
            num_scalar_prefetch=4,
            grid=(slot.shape[0],),
            in_specs=[
                pl.BlockSpec((1, 2, order, order), lambda k, m, slot, t, s: (slot[k], 0, 0, 0)),
                *[pl.BlockSpec((3, 2, rows, width), lambda k, *scalars: (k, 0, 0, 0))] * len(got),
            ],
            out_specs=pl.BlockSpec(whole, lambda k, *scalars: (0, 0, 0, 0)),
            scratch_shapes=[pltpu.VMEM((parts, 3, 1, 2, order, width), jnp.float32)],
        ),
        out_shape=jax.ShapeDtypeStruct(whole, jnp.float32),
        compiler_params=CHAIN,
        name="chain",
    )(member, slot, target, sign, nodes, *got)


def all_columns(x):
    if lax.axis_size("pair") == 1:
        return x
    return lax.all_gather(x, "pair", axis=3, tiled=True)


def per_device(node_blocks, node_slot, pair_list, second_list, targets, spin_signs):
    devices = lax.axis_size("node")
    column = lax.axis_index("node")
    group = devices // 2
    node_col = node_blocks.shape[0]
    second_col = second_list.shape[0] // devices

    slots = node_slot[pair_list]
    slots = slots[second_list].reshape(devices, second_col, 4)
    pairwise = lax.axis_size("pair") == 1
    rights = fetch_items(node_blocks, slots[:, :, 1:].reshape(devices, second_col * 3), pairwise)

    own_slots = lax.dynamic_index_in_dim(slots[:, :, 0], column, 0, keepdims=False)
    own_slots = own_slots - column * node_col
    own_signs = lax.dynamic_slice_in_dim(spin_signs, column * second_col, second_col, 0)
    own_targets = lax.dynamic_slice_in_dim(targets, column * second_col, second_col, 0)
    own_targets = own_targets - column * RES_COL

    if pairwise:
        member = (column % group).astype(jnp.int32).reshape(1)
        return chain(member, own_slots, own_targets, own_signs, node_blocks, rights)
    same = jnp.arange(second_col, dtype=jnp.int32)
    products = multiply(own_slots, all_columns(node_blocks), rights, 0)
    longer = multiply(same, all_columns(products), rights, 1)
    return finish(own_targets, own_signs, all_columns(longer), rights)


def solution(mesh):
    placed = (P(("cfg", "node"), None, None, "pair"), P(), P(), P(), P(), P())

    return jax.shard_map(
        per_device,
        mesh=mesh,
        in_specs=placed,
        out_specs=P(("cfg", "node"), None, None, "pair"),
        check_vma=False,
    )
```

```python
import functools

import jax
import jax.numpy as jnp
from jax import lax
from jax.experimental import pallas as pl
from jax.experimental.pallas import tpu as pltpu
from jax.sharding import PartitionSpec as P


RES_COL = 2
LANES = 128
CROSS_SHARE = 29 / 64
ANY = pl.BlockSpec(memory_space=pl.ANY)
HBM = pl.BlockSpec(memory_space=pltpu.HBM)
SMEM = pl.BlockSpec(memory_space=pltpu.SMEM)
VMEM = pl.BlockSpec(memory_space=pltpu.VMEM)
PARAMS = pltpu.CompilerParams(vmem_limit_bytes=24 * 1024 * 1024)
LARGE = pltpu.CompilerParams(vmem_limit_bytes=56 * 1024 * 1024)
CHAIN = pltpu.CompilerParams(vmem_limit_bytes=44 * 1024 * 1024)


def cut_kernel(in_ref, out_ref):
    rows = out_ref.shape[3]
    for j in range(out_ref.shape[0]):
        out_ref[j] = in_ref[:, :, j * rows : (j + 1) * rows, :]


def cut_rows(nodes, group, part, width):
    count, _, order, _ = nodes.shape
    rows = order // group
    steps = 2 if group % 2 == 0 else 1
    return pl.pallas_call(
        cut_kernel,
        grid=(steps,),
        in_specs=[pl.BlockSpec((count, 2, order // steps, width), lambda i: (0, 0, i, part))],
        out_specs=pl.BlockSpec((group // steps, count, 2, rows, width), lambda i: (i, 0, 0, 0, 0)),
        out_shape=jax.ShapeDtypeStruct((group, count, 2, rows, width), jnp.float32),
        name="cut_rows",
    )(nodes)


def partner(index, k, group):
    return index ^ k if group & (group - 1) == 0 else (k - index + group) % group


def split_kernel(member, in_ref, *out_refs):
    rows = out_refs[0].shape[2]
    for k, out_ref in enumerate(out_refs):
        row = pl.multiple_of(partner(member[0], k, len(out_refs)) * rows, rows)
        out_ref[...] = in_ref[:, :, pl.ds(row, rows), :]


def split_rows(member, nodes, group, part, width):
    count, _, order, _ = nodes.shape
    shape = (count, 2, order // group, width)
    return pl.pallas_call(
        split_kernel,
        grid_spec=pltpu.PrefetchScalarGridSpec(
            num_scalar_prefetch=1,
            grid=(1,),
            in_specs=[pl.BlockSpec((count, 2, order, width), lambda i, member: (0, 0, 0, part))],
            out_specs=[pl.BlockSpec(shape, lambda i, member: (0, 0, 0, 0))] * group,
        ),
        out_shape=[jax.ShapeDtypeStruct(shape, jnp.float32)] * group,
        name="split_rows",
    )(member, nodes)


def load_spread(member, refs, spread_ref):
    for k, ref in enumerate(refs):
        number = ref.shape[0]
        spread_ref[pl.ds(partner(member, k, len(refs)) * number, number)] = ref[...]


def spread_scratch(spread):
    count = sum(array.shape[0] for array in spread)
    return [pltpu.VMEM((count,) + spread[0].shape[1:], jnp.float32)] if len(spread) > 1 else []


def plan_kernel(room, half_ref, ids_ref, send_ref, source_ref, crowded_ref, place_ref):
    half = half_ref[0]
    count = send_ref.shape[0]
    asked = source_ref.shape[0]

    def clear(i, carry):
        place_ref[i] = -1
        return carry

    def empty(i, carry):
        send_ref[i] = 0
        return carry

    lax.fori_loop(0, 2 * count, clear, 0, unroll=8)
    lax.fori_loop(0, count, empty, 0, unroll=8)

    def visit_other(q, found):
        item = ids_ref[(1 - half) * asked + q]
        here = item - half * count
        fresh = (here >= 0) & (here < count) & (place_ref[item] < 0)

        @pl.when(fresh)
        def _():
            place_ref[item] = 0
            send_ref[found] = here

        return found + fresh.astype(jnp.int32)

    def visit_own(q, found):
        item = ids_ref[half * asked + q]
        here = item - half * count
        inside = (here >= 0) & (here < count)
        known = place_ref[item]
        fresh = jnp.logical_not(inside) & (known < 0)
        there = count + room + item - (1 - half) * count
        place = jnp.where(known < 0, jnp.where(found < room, count + found, there), known)

        @pl.when(fresh)
        def _():
            place_ref[item] = place

        source_ref[q] = jnp.where(inside, here, place)
        return found + fresh.astype(jnp.int32)

    sent = lax.fori_loop(0, asked, visit_other, jnp.int32(0))
    received = lax.fori_loop(0, asked, visit_own, jnp.int32(0))
    crowded_ref[0] = (jnp.maximum(sent, received) > room).astype(jnp.int32)


def make_plan(half, ids, count, room):
    asked = ids.shape[0] // 2
    return pl.pallas_call(
        functools.partial(plan_kernel, room),
        in_specs=[SMEM] * 2,
        out_specs=[SMEM] * 3,
        out_shape=[
            jax.ShapeDtypeStruct((count,), jnp.int32),
            jax.ShapeDtypeStruct((asked,), jnp.int32),
            jax.ShapeDtypeStruct((1,), jnp.int32),
        ],
        scratch_shapes=[pltpu.SMEM((2 * count,), jnp.int32)],
        compiler_params=PARAMS,
        name="make_plan",
    )(half, ids)


def leave_kernel(send_ref, member_ref, *refs):
    if len(refs) == 2:
        spread_ref, out_ref = refs
    else:
        *parts, out_ref, spread_ref = refs
        load_spread(member_ref[0], parts, spread_ref)

    def copy(i, carry):
        out_ref[i] = spread_ref[send_ref[i]]
        return carry

    lax.fori_loop(0, out_ref.shape[0], copy, 0, unroll=8)


def pick_leaving(send, member, spread, room):
    return pl.pallas_call(
        leave_kernel,
        in_specs=[SMEM, SMEM] + [VMEM] * len(spread),
        out_specs=VMEM,
        out_shape=jax.ShapeDtypeStruct((room,) + spread[0].shape[1:], jnp.float32),
        scratch_shapes=spread_scratch(spread),
        compiler_params=PARAMS,
        name="pick_leaving",
    )(send, member, *spread)


def collect_kernel(source_ref, crowded_ref, spread_ref, arrived_ref, extra_ref, out_ref, sem):
    count, room = spread_ref.shape[0], arrived_ref.shape[0]

    def copy(q, carry):
        source = source_ref[q]
        near = jnp.minimum(source, count - 1)
        far = jnp.clip(source - count, 0, room - 1)
        out_ref[q] = jnp.where(source < count, spread_ref[near], arrived_ref[far])
        return carry

    lax.fori_loop(0, out_ref.shape[0], copy, 0, unroll=8)

    @pl.when(crowded_ref[0] > 0)
    def _():
        def fetch(q, carry):
            source = source_ref[q] - (count + room)

            @pl.when(source >= 0)
            def _():
                slow = pltpu.make_async_copy(extra_ref.at[source], out_ref.at[q], sem)
                slow.start()
                slow.wait()

            return carry

        lax.fori_loop(0, out_ref.shape[0], fetch, 0)


def collect(source, crowded, spread, arrived, extra):
    return pl.pallas_call(
        collect_kernel,
        in_specs=[SMEM, SMEM, VMEM, VMEM, ANY],
        out_specs=VMEM,
        out_shape=jax.ShapeDtypeStruct((source.shape[0],) + spread.shape[1:], jnp.float32),
        scratch_shapes=[pltpu.SemaphoreType.DMA],
        compiler_params=PARAMS,
        name="collect",
    )(source, crowded, spread, arrived, extra)


def scatter_kernel(parts, source_ref, flags_ref, arrived_ref, extra_ref, *refs):
    if parts == 1:
        spread_ref, *out_refs, sem = refs
    else:
        out_refs, (spread_ref, sem) = refs[parts:-2], refs[-2:]
        load_spread(flags_ref[1], refs[:parts], spread_ref)
    count, room = spread_ref.shape[0], arrived_ref.shape[0]
    wanted = out_refs[0].shape[0]
    for k, out_ref in enumerate(out_refs):
        base = partner(flags_ref[1], k, len(out_refs)) * wanted

        def copy(q, carry, base=base, out_ref=out_ref):
            source = source_ref[base + q]
            near = jnp.minimum(source, count - 1)
            far = jnp.clip(source - count, 0, room - 1)
            out_ref[q] = jnp.where(source < count, spread_ref[near], arrived_ref[far])
            return carry

        lax.fori_loop(0, wanted, copy, 0, unroll=4)

        @pl.when(flags_ref[0] > 0)
        def _(base=base, out_ref=out_ref):
            def fetch(q, carry):
                source = source_ref[base + q] - (count + room)

                @pl.when(source >= 0)
                def _():
                    slow = pltpu.make_async_copy(extra_ref.at[source], out_ref.at[q], sem)
                    slow.start()
                    slow.wait()

                return carry

            lax.fori_loop(0, wanted, fetch, 0)


def scatter(source, flags, spread, arrived, extra, group):
    shape = (source.shape[0] // group,) + spread[0].shape[1:]
    return pl.pallas_call(
        functools.partial(scatter_kernel, len(spread)),
        in_specs=[SMEM, SMEM, VMEM, ANY] + [VMEM] * len(spread),
        out_specs=[VMEM] * group,
        out_shape=[jax.ShapeDtypeStruct(shape, jnp.float32)] * group,
        scratch_shapes=[*spread_scratch(spread), pltpu.SemaphoreType.DMA],
        compiler_params=PARAMS,
        name="scatter",
    )(source, flags, arrived, extra, *spread)


def fetch_items(nodes, ids, pairwise):
    devices = lax.axis_size("node")
    group = devices // 2
    index = lax.axis_index("node")
    half = (index // group).astype(jnp.int32).reshape(1)
    member = (index % group).astype(jnp.int32).reshape(1)
    halves = [[h * group + i for i in range(group)] for h in range(2)]
    swap = [(i, (i + group) % devices) for i in range(devices)]
    count = group * nodes.shape[0]
    width = min(LANES, nodes.shape[3])
    parts = nodes.shape[3] // width
    room = min(count, max(8, int(count * CROSS_SHARE)))
    send, source, crowded = make_plan(half, ids.reshape(-1), count, room)

    def exchange(x):
        return lax.all_to_all(x, "node", 0, 0, axis_index_groups=halves, tiled=True)

    def trade(arrays):
        got = []
        for k, array in enumerate(arrays):
            pairs = [
                (i, i // group * group + partner(i % group, k, group)) for i in range(devices)
            ]
            still = all(i == j for i, j in pairs)
            got.append(array if still else lax.ppermute(array, "node", pairs))
        return got

    def cross_all(spread):
        if len(spread) == 1:
            return lax.ppermute(spread[0], "node", swap)
        members = jnp.arange(group, dtype=jnp.int32)
        order = jnp.argsort(jnp.stack([partner(member[0], k, group) for k in range(group)]))
        every = jnp.take(jnp.stack(spread), order[members], axis=0)
        return lax.ppermute(every.reshape((count,) + every.shape[2:]), "node", swap)

    delivered = []
    for c in range(parts):
        if pairwise and c > 0:
            spread = trade(split_rows(member, nodes, group, c, width))
        else:
            cut = cut_rows(nodes, group, c, width)
            spread = exchange(cut)
            spread = [spread.reshape((count,) + spread.shape[2:])]
        leaving = pick_leaving(send, member, spread, room)
        arrived = lax.ppermute(leaving, "node", swap)
        piece = (count,) + leaving.shape[1:]
        extra = lax.cond(crowded[0] > 0, cross_all, lambda _: jnp.zeros(piece, jnp.float32), spread)
        if pairwise and c == parts - 1:
            flags = jnp.concatenate([crowded, member])
            sent = scatter(source, flags, spread, arrived, extra, group)
            delivered.append(trade(sent))
            continue
        if len(spread) > 1:
            order = [partner(member[0], k, group) for k in range(group)]
            spread = [jnp.take(jnp.stack(spread), jnp.argsort(jnp.stack(order)), axis=0)]
            spread = [spread[0].reshape((count,) + spread[0].shape[2:])]
        picked = collect(source, crowded, spread[0], arrived, extra)
        picked = picked.reshape((group, ids.shape[1]) + picked.shape[1:])
        delivered.append(exchange(picked))
    return delivered


def halves_of(x):
    high = x.astype(jnp.bfloat16)
    return high, (x - high.astype(jnp.float32)).astype(jnp.bfloat16)


def stacked(blocks):
    order = blocks[0].shape[0] * blocks[0].shape[2]
    real, imag = (
        jnp.concatenate([b[:, c].reshape(order, b.shape[-1]) for b in blocks], axis=1)
        for c in range(2)
    )
    pairs = zip(halves_of(real), halves_of(imag))
    return [
        jnp.concatenate([jnp.concatenate([r, i], axis=1), jnp.concatenate([-i, r], axis=1)], axis=0)
        for r, i in pairs
    ]


def product(left, blocks):
    left_high, left_low = halves_of(left)
    right_high, right_low = stacked(blocks)
    return jnp.dot(
        jnp.concatenate([left_high, left_high, left_low], axis=1),
        jnp.concatenate([right_high, right_low, right_high], axis=0),
        preferred_element_type=jnp.float32,
    )


def wide(ref):
    return jnp.concatenate([ref[0, 0], ref[0, 1]], axis=1)


def triple_spec(array, each=1):
    group, _, _, rows, width = array.shape
    return pl.BlockSpec((group, 3 * each, 2, rows, width), lambda k, *scalars: (0, k, 0, 0, 0))


def multiply_kernel(which, index_ref, left_ref, *refs):
    right_refs, out_ref = refs[:-1], refs[-1]
    both = product(wide(left_ref), [ref[:, which] for ref in right_refs])
    width = out_ref.shape[-1]
    out_ref[0, 0] = both[:, :width]
    out_ref[0, 1] = both[:, width:]


def multiply(left_index, lefts, rights, which):
    order = lefts.shape[2]
    number = left_index.shape[0]
    cols = sum(right.shape[-1] for right in rights)
    return pl.pallas_call(
        functools.partial(multiply_kernel, which),
        grid_spec=pltpu.PrefetchScalarGridSpec(
            num_scalar_prefetch=1,
            grid=(number,),
            in_specs=[
                pl.BlockSpec((1, 2, order, order), lambda k, index: (index[k], 0, 0, 0)),
                *[triple_spec(right) for right in rights],
            ],
            out_specs=pl.BlockSpec((1, 2, order, cols), lambda k, index: (k, 0, 0, 0)),
        ),
        out_shape=jax.ShapeDtypeStruct((number, 2, order, cols), jnp.float32),
        compiler_params=LARGE,
        name="multiply",
    )(left_index, lefts, *rights)


def add_result(step, target, sign, both, out_ref):
    width = out_ref.shape[-1]

    @pl.when(step == 0)
    def _():
        out_ref[...] = jnp.zeros_like(out_ref)

    both = both * sign[step].astype(jnp.float32)
    row = target[step]
    out_ref[row, 0] += both[:, :width]
    out_ref[row, 1] += both[:, width:]


def finish_kernel(target, sign, left_ref, *refs):
    right_refs, out_ref = refs[:-1], refs[-1]
    both = product(wide(left_ref), [ref[:, 2] for ref in right_refs])
    add_result(pl.program_id(0), target, sign, both, out_ref)


def finish(target, sign, lefts, rights):
    order = lefts.shape[2]
    whole = (RES_COL, 2, order, sum(right.shape[-1] for right in rights))
    return pl.pallas_call(
        finish_kernel,
        grid_spec=pltpu.PrefetchScalarGridSpec(
            num_scalar_prefetch=2,
            grid=(lefts.shape[0],),
            in_specs=[
                pl.BlockSpec((1, 2, order, order), lambda k, t, s: (k, 0, 0, 0)),
                *[triple_spec(right) for right in rights],
            ],
            out_specs=pl.BlockSpec(whole, lambda k, t, s: (0, 0, 0, 0)),
        ),
        out_shape=jax.ShapeDtypeStruct(whole, jnp.float32),
        compiler_params=LARGE,
        name="finish",
    )(target, sign, lefts, *rights)


def chain_kernel(parts, each, member, slot, target, sign, *refs):
    node_refs, refs = refs[:each], refs[each:]
    part_refs, got_refs, (out_ref, last_ref) = refs[:parts], refs[parts:-2], refs[-2:]
    step = pl.program_id(0)
    width = out_ref.shape[-1]
    for k, ref in enumerate(got_refs):
        rows = ref.shape[2]
        row = pl.multiple_of(partner(member[0], k, len(got_refs)) * rows, rows)
        for which in range(3 * each):
            last_ref[which, 0, :, pl.ds(row, rows)] = ref[which]
    lefts = [wide(ref) for ref in node_refs]
    for which in range(3):
        for n in range(each):
            item = 3 * n + which
            blocks = [ref[:, item] for ref in part_refs] + [last_ref[item]]
            lefts[n] = product(lefts[n], blocks)

    @pl.when(step == 0)
    def _():
        out_ref[...] = jnp.zeros_like(out_ref)

    for n, both in enumerate(lefts):
        both = both * sign[step * each + n].astype(jnp.float32)
        row = target[step * each + n]
        out_ref[row, 0] += both[:, :width]
        out_ref[row, 1] += both[:, width:]


def chain(member, slot, target, sign, nodes, rights):
    order = nodes.shape[2]
    whole = (RES_COL, 2, order, order)
    *parts, got = rights
    _, _, rows, width = got[0].shape
    each = 2 if slot.shape[0] % 2 == 0 else 1

    def node_spec(n):
        return pl.BlockSpec(
            (1, 2, order, order), lambda k, m, slot, t, s: (slot[k * each + n], 0, 0, 0)
        )

    return pl.pallas_call(
        functools.partial(chain_kernel, len(parts), each),
        grid_spec=pltpu.PrefetchScalarGridSpec(
            num_scalar_prefetch=4,
            grid=(slot.shape[0] // each,),
            in_specs=[
                *[node_spec(n) for n in range(each)],
                *[triple_spec(part, each) for part in parts],
                *[pl.BlockSpec((3 * each, 2, rows, width), lambda k, *scalars: (k, 0, 0, 0))] * len(got),
            ],
            out_specs=pl.BlockSpec(whole, lambda k, *scalars: (0, 0, 0, 0)),
            scratch_shapes=[pltpu.VMEM((3 * each, 1, 2, order, width), jnp.float32)],
        ),
        out_shape=jax.ShapeDtypeStruct(whole, jnp.float32),
        compiler_params=CHAIN,
        name="chain",
    )(member, slot, target, sign, *[nodes] * each, *parts, *got)


def all_columns(x):
    if lax.axis_size("pair") == 1:
        return x
    return lax.all_gather(x, "pair", axis=3, tiled=True)


def per_device(node_blocks, node_slot, pair_list, second_list, targets, spin_signs):
    devices = lax.axis_size("node")
    column = lax.axis_index("node")
    group = devices // 2
    node_col = node_blocks.shape[0]
    second_col = second_list.shape[0] // devices

    slots = node_slot[pair_list]
    slots = slots[second_list].reshape(devices, second_col, 4)
    pairwise = lax.axis_size("pair") == 1
    rights = fetch_items(node_blocks, slots[:, :, 1:].reshape(devices, second_col * 3), pairwise)

    own_slots = lax.dynamic_index_in_dim(slots[:, :, 0], column, 0, keepdims=False)
    own_slots = own_slots - column * node_col
    own_signs = lax.dynamic_slice_in_dim(spin_signs, column * second_col, second_col, 0)
    own_targets = lax.dynamic_slice_in_dim(targets, column * second_col, second_col, 0)
    own_targets = own_targets - column * RES_COL

    if pairwise:
        member = (column % group).astype(jnp.int32).reshape(1)
        return chain(member, own_slots, own_targets, own_signs, node_blocks, rights)
    same = jnp.arange(second_col, dtype=jnp.int32)
    products = multiply(own_slots, all_columns(node_blocks), rights, 0)
    longer = multiply(same, all_columns(products), rights, 1)
    return finish(own_targets, own_signs, all_columns(longer), rights)


def solution(mesh):
    placed = (P(("cfg", "node"), None, None, "pair"), P(), P(), P(), P(), P())

    return jax.shard_map(
        per_device,
        mesh=mesh,
        in_specs=placed,
        out_specs=P(("cfg", "node"), None, None, "pair"),
        check_vma=False,
    )
```
